32 devices in a mesh: groups: 2 (over y), cand: 4 (over z), tgt: 2 (over x), mix: 2 (over core).
Axes of the slice: x: 2, y: 2, z: 4, core: 2. Of those that a mesh axis runs over, the one named last changes fastest.
Arguments:
- candidates: bfloat16 [8192, 1024], P(('groups', 'cand')), parts along dimension 0, may hold values from -6 to 6
- targets: bfloat16 [4096, 1024], P(('groups', 'tgt')), parts along dimension 0, may hold values from -6 to 6
- member: int32 [4096], P('groups'), parts along dimension 0, may hold values from 0 to 15
- mix_weight: float32 [64, 32], P('mix', 'groups'), parts along dimension 1, may hold values from 0.1 to 10
Outputs:
- cand_potential: float32 [64, 8192], P('mix', ('groups', 'cand')), parts along dimension 1
- tgt_potential: float32 [64, 4096], P('mix', ('groups', 'tgt')), parts along dimension 1
The draws below stay inside these ranges and needn't reach their ends.
There are 2 independent parts, one for each index of `groups`. The reference program is written for one: setup_inputs(seed, part) draws one part's arguments, and reference() takes and returns one part's arrays. A program takes and returns all parts, laid end to end along the dimension named above; each array names one. Nothing has to cross between parts.
All inputs are finite; a program needn't handle non-finite values.
Results may differ from the reference program's by a relative error of at most 0.0023.
Values sent between devices are 32-bit elements; how exact they have to be, the bound alone decides.
A program may use at most 64 MiB of HBM per device.

```python
import math
import jax
import jax.numpy as jnp
from jax import lax

E = 1024
MIX = 64
TASKS = 16
ITERS = 2
CD = 1024
NC = 4096
NT = 2048
N_CAND = 4


def cluster_axes(key):
    return jax.random.normal(jax.random.fold_in(key, 101), (TASKS, E), jnp.float32)


def member_ids(key):
    base_key = jax.random.fold_in(key, 102)
    first_key, second_key, third_key = jax.random.split(base_key, 3)
    task_ids = jax.random.randint(first_key, (NT,), 0, TASKS, dtype=jnp.int32)
    low_place = jax.random.randint(second_key, (), 0, NT, dtype=jnp.int32)
    high_step = jax.random.randint(third_key, (), 0, NT - 1, dtype=jnp.int32)
    high_place = (low_place + 1 + high_step) % NT
    places = jnp.arange(NT, dtype=jnp.int32)
    task_ids = jnp.where(places == low_place, 0, task_ids)
    task_ids = jnp.where(places == high_place, TASKS - 1, task_ids)
    return task_ids.astype(jnp.int32)


def draw_jitter(key, salt, rows):
    jitter_key = jax.random.fold_in(key, salt)
    return jax.random.normal(jitter_key, (rows, E), jnp.float32)


def draw_member(key, part):
    return member_ids(key)


def draw_targets(key, part):
    task_axes = cluster_axes(key)
    centre = jnp.take(task_axes, member_ids(key), axis=0)
    values = 0.5477226 * centre + 0.83666 * draw_jitter(key, 103, NT)
    return jnp.clip(values, -6.0, 6.0).astype(jnp.bfloat16)


def draw_candidates(key, part):
    task_axes = cluster_axes(key)
    pick_key = jax.random.fold_in(key, 104)
    gain_key = jax.random.fold_in(key, 105)
    task_picks = jax.random.randint(pick_key, (3, NC), 0, TASKS, dtype=jnp.int32)
    gain_rows = 0.35 * jnp.exp(0.5 * jax.random.normal(gain_key, (3, NC, 1), jnp.float32))
    values = 0.7071068 * draw_jitter(key, 106, NC)
    for picked in range(3):
        values = values + gain_rows[picked] * jnp.take(task_axes, task_picks[picked], axis=0)
    return jnp.clip(values, -6.0, 6.0).astype(jnp.bfloat16)


def shard_levels(key, dims, cuts, least, largest):
    loudness, own = 1.0, jax.random.fold_in(key, 6)
    for dim, parts in cuts:
        draws = jnp.exp(jax.random.uniform(jax.random.fold_in(own, dim), (parts,), jnp.float32, least / len(cuts), largest / len(cuts)))
        loudness = loudness * jnp.repeat(draws, dims[dim] // parts).reshape([-1 if axis == dim else 1 for axis in range(len(dims))])
    return loudness


def setup_inputs(seed: int = 0, part: int = 0) -> dict:
    streams_of = jax.random.split(jax.random.key(seed), 5)
    part_splits = jax.random.split(jax.random.fold_in(streams_of[4], part), 5)
    return {
        "candidates": draw_candidates(jax.random.fold_in(jax.random.fold_in(streams_of[4], part), 71), part),
        "targets": draw_targets(jax.random.fold_in(jax.random.fold_in(streams_of[4], part), 71), part),
        "member": draw_member(jax.random.fold_in(jax.random.fold_in(streams_of[4], part), 71), part),
        "mix_weight": jnp.clip(jnp.exp(math.log(10.0) - 4.6051702 * jax.random.uniform(part_splits[3], (MIX, TASKS), jnp.float32) ** shard_levels(part_splits[3], (MIX, TASKS), ((0, 2),), -0.2, 0.2)), 0.1, 10.0),
    }


EPS_FIRST = 0.05
EPS_SECOND = 0.025

def unit_rows(embedding):
    values = embedding.astype(jnp.float32)
    mean_sq = lax.optimization_barrier(jnp.mean(values * values, axis=1, keepdims=True))
    return (values * lax.rsqrt(mean_sq + 1e-06) * (1.0 / math.sqrt(values.shape[1]))).astype(jnp.bfloat16)

def contract_last(left, right):
    return lax.dot_general(left, right, (((1,), (1,)), ((), ())), preferred_element_type=jnp.float32)

def target_mass(own_member, member, mix_weight, cand_total):
    task_ids = jnp.arange(mix_weight.shape[1], dtype=jnp.int32)
    counts = lax.optimization_barrier(jnp.sum((member[None, :] == task_ids[:, None]).astype(jnp.float32), axis=1))
    weight_total = jnp.dot(mix_weight, counts, precision=lax.Precision.HIGHEST)
    onehot = (own_member[None, :] == task_ids[:, None]).astype(jnp.float32)
    per_target = jnp.dot(mix_weight, onehot, precision=lax.Precision.HIGHEST)
    return per_target * (cand_total / weight_total)[:, None]

def reference(candidates, targets, member, mix_weight):
    tgt_unit = unit_rows(targets)
    cand_blocks = unit_rows(candidates).reshape(N_CAND, CD, E)

    def score_block(cand_block):
        return contract_last(cand_block, tgt_unit)
    scores = lax.map(score_block, cand_blocks)
    mass = target_mass(member, member, mix_weight, float(NC))
    scale_tgt = jnp.ones((MIX, NT), jnp.float32)
    scale_blocks = jnp.zeros((N_CAND, MIX, CD), jnp.float32)
    for section_index, epsilon in enumerate((EPS_FIRST, EPS_SECOND)):
        if section_index == 1:
            scale_tgt = scale_tgt * scale_tgt
        for repeat in range(ITERS):

            def cand_pass(score_rows):
                kernel = jnp.exp(score_rows / epsilon) / NT
                return 1.0 / lax.dot_general(scale_tgt, kernel, (((1,), (1,)), ((), ())), precision=lax.Precision.HIGHEST)
            scale_blocks = lax.map(cand_pass, scores)

            def tgt_pass(column_sum, paired):
                kernel = jnp.exp(paired[0] / epsilon) / NT
                return (column_sum + jnp.dot(paired[1], kernel, precision=lax.Precision.HIGHEST), None)
            column_sum, unused = lax.scan(tgt_pass, jnp.zeros((MIX, NT), jnp.float32), (scores, scale_blocks))
            scale_tgt = mass / column_sum
    scale_cand = jnp.transpose(scale_blocks, (1, 0, 2)).reshape(MIX, NC)
    return (jnp.log(scale_cand), jnp.log(scale_tgt))
```

```python
import functools
import math

import jax
import jax.numpy as jnp
from jax import lax
from jax.experimental import pallas as pl
from jax.experimental.pallas import tpu as pltpu
from jax.sharding import PartitionSpec as P

ITERS = 2


EPS_FIRST = 0.05
EPS_SECOND = 0.025

MESH = pl.DeviceIdType.MESH
F32 = jnp.float32
BF16 = jnp.bfloat16
NT_DIMS = (((1,), (1,)), ((), ()))
TN_DIMS = (((0,), (0,)), ((), ()))
NN_DIMS = (((1,), (0,)), ((), ()))


def unit_rows(embedding):
    values = embedding.astype(jnp.float32)
    mean_sq = jnp.mean(values * values, axis=1, keepdims=True)
    return (values * (lax.rsqrt(mean_sq + 1e-06) * (1.0 / math.sqrt(values.shape[1])))).astype(
        jnp.bfloat16
    )


def contract_last(left, right):
    return lax.dot_general(left, right, NT_DIMS, preferred_element_type=jnp.float32)


def split_rows(value):
    head = value.astype(BF16)
    rest = (value - head.astype(F32)).astype(BF16)
    return jnp.concatenate([head, rest], axis=0)


def join_rows(value):
    half = value.shape[0] // 2
    return value[:half] + value[half:]


def fused_kernel(
    n_tgt, n_cand, parts, cand_hbm, tgt_hbm, member_ref, weight_ref, out_cand, out_tgt,
    cand_rows, tgt_rows, tgt_unit, raised, k_one, k_two, mass, cand_sums,
    row_part, row_slots, col_slots, task_slots, cand_slots, rs_send, rs_slots, ag_slots,
    load_sems, x_send, x_recv, z_send, z_recv, row_out, row_in, rs_out, rs_in, ag_out, ag_in,
):
    xi, zi = lax.axis_index("tgt"), lax.axis_index("cand")
    rows, width = cand_hbm.shape
    cols = tgt_hbm.shape[0]
    tasks, mixes = weight_ref.shape
    owners = (n_cand // 2 - 1, n_cand // 2)
    share = cols // len(owners)
    group = mixes // parts
    tgt_total, cand_total = cols * n_tgt, rows * n_cand
    block = 256

    def loads(src, dst, row):
        return [
            pltpu.make_async_copy(
                src.at[pl.ds(at, block)], dst.at[pl.ds(at, block)], load_sems.at[row, at // block]
            )
            for at in range(0, src.shape[0], block)
        ]

    tgt_loads, cand_loads = loads(tgt_hbm, tgt_rows, 0), loads(cand_hbm, cand_rows, 1)
    for copy in tgt_loads + cand_loads:
        copy.start()

    def x_peer(d):
        return {"tgt": lax.rem(xi + d, n_tgt)}

    def z_peer(d):
        return {"cand": lax.rem(zi + d, n_cand)}

    barrier = pltpu.get_barrier_semaphore()
    for d in range(1, n_tgt):
        pl.semaphore_signal(barrier, inc=1, device_id=x_peer(d), device_id_type=MESH)
    for d in range(1, n_cand):
        pl.semaphore_signal(barrier, inc=1, device_id=z_peer(d), device_id_type=MESH)

    pending = []
    xs, zs = (x_send, x_recv), (z_send, z_recv)

    def send(src, dst, sems, phase, d, peer):
        copy = pltpu.make_async_remote_copy(
            src_ref=src, dst_ref=dst,
            send_sem=sems[0].at[phase, d - 1], recv_sem=sems[1].at[phase, d - 1],
            device_id=peer, device_id_type=MESH,
        )
        copy.start()
        pending.append(copy)
        return copy

    def x_sum(slots):
        total = slots[lax.rem(xi + n_tgt, n_tgt)]
        for k in range(1, n_tgt):
            total = total + slots[lax.rem(xi - k + n_tgt, n_tgt)]
        return total

    def z_sum(slots):
        total = slots[lax.rem(zi + n_cand, n_cand)]
        for k in range(1, n_cand):
            total = total + slots[lax.rem(zi - k + n_cand, n_cand)]
        return total

    def x_start(slots, phase):
        return [send(slots.at[0], slots.at[d], xs, phase, d, x_peer(d)) for d in range(1, n_tgt)]

    def z_start(slots, phase):
        return [send(slots.at[0], slots.at[d], zs, phase, d, z_peer(d)) for d in range(1, n_cand)]

    def arrive(copies):
        for copy in copies:
            copy.wait_recv()

    all_ids = lax.broadcasted_iota(jnp.int32, (tasks, tgt_total), 0)
    all_hot = (member_ref[...] == all_ids).astype(F32)
    weights = weight_ref[...]
    per_target = lax.dot_general(
        weights, all_hot, TN_DIMS, precision=lax.Precision.HIGHEST, preferred_element_type=F32
    )
    ratio = float(cand_total) / jnp.sum(per_target, axis=1, keepdims=True)
    own = pl.ds(pl.multiple_of(xi * cols, cols), cols)
    own_hot = (
        member_ref[:, own] == lax.broadcasted_iota(jnp.int32, (tasks, cols), 0)
    ).astype(F32)
    mass[...] = (
        lax.dot_general(
            weights, own_hot, TN_DIMS, precision=lax.Precision.HIGHEST, preferred_element_type=F32
        )
        * ratio
    )

    for index, copy in enumerate(tgt_loads):
        copy.wait()
        at = pl.ds(index * block, block)
        tgt_unit[at, :] = unit_rows(tgt_rows[at, :])
    for copy in cand_loads:
        copy.wait()
    ones = jnp.ones((16, cols), BF16)

    def build(first):
        at = pl.ds(first, block)
        scores = contract_last(unit_rows(cand_rows[at, :]), tgt_unit[...])
        power = jnp.exp(scores * (1.0 / EPS_FIRST))
        raised[at, :] = power
        kernel_rows = (power * (1.0 / tgt_total)).astype(BF16)
        k_one[at, :] = kernel_rows
        return contract_last(ones, kernel_rows)[:1]

    def square(first, last):
        def step(b, carry):
            at = pl.ds(pl.multiple_of(b * 64, 64), 64)
            power = raised[at, :]
            k_two[at, :] = (power * power * (1.0 / tgt_total)).astype(BF16)
            return carry

        lax.fori_loop(first // 64, last // 64, step, 0)

    row_copies = []
    for index in range(rows // block):
        at = pl.ds(index * block, block)
        row_part[:, at] = build(index * block)
        if index == 0:
            pl.semaphore_wait(barrier, n_tgt - 1 + n_cand - 1)
        for d in range(1, n_tgt):
            row_copies.append(pltpu.make_async_remote_copy(
                src_ref=row_part.at[:, at], dst_ref=row_slots.at[d, :, at],
                send_sem=row_out.at[d - 1, index], recv_sem=row_in.at[d - 1, index],
                device_id=x_peer(d), device_id_type=MESH,
            ))
            row_copies[-1].start()
    square(0, rows // 2)
    arrive(row_copies)
    row_sum = row_part[...]
    for d in range(1, n_tgt):
        row_sum = row_sum + row_slots[d]
    scale_row = 1.0 / row_sum
    place = lax.broadcasted_iota(jnp.int32, (16, rows), 0)
    head = scale_row.astype(BF16).astype(F32)
    lhs = jnp.where(place == 0, head, jnp.where(place == 1, scale_row - head, 0.0)).astype(BF16)
    part = lax.dot_general(lhs, k_one[...], NN_DIMS, preferred_element_type=F32)
    col_slots[0] = part[:1] + part[1:2]
    copies = z_start(col_slots, 0)
    square(rows // 2, rows)
    arrive(copies)
    col_sum = z_sum(col_slots)

    task_slots[0] = join_rows(contract_last(split_rows(own_hot / col_sum), k_one[...]))
    arrive(x_start(task_slots, 1))
    cand_sums[...] = ratio * lax.dot_general(
        weights, x_sum(task_slots), TN_DIMS, precision=lax.Precision.HIGHEST,
        preferred_element_type=F32,
    )

    def of(part):
        return pl.ds(part * group, group)

    def half(o):
        return pl.ds(o * share if isinstance(o, int) else pl.multiple_of(o * share, share), share)

    far = 1 - zi // owners[1]
    near = 1 - far

    def to_owner(turn, part, o):
        return pltpu.make_async_remote_copy(
            src_ref=rs_send.at[turn, part, o], dst_ref=rs_slots.at[turn, part, zi],
            send_sem=rs_out.at[turn, part, o], recv_sem=rs_in.at[turn, part, zi],
            device_id={"cand": owners[0] + o}, device_id_type=MESH,
        )

    def from_owner(turn, part, o, peer):
        return pltpu.make_async_remote_copy(
            src_ref=ag_slots.at[turn, part, o], dst_ref=ag_slots.at[turn, part, o],
            send_sem=ag_out.at[turn, part, peer], recv_sem=ag_in.at[turn, part, o],
            device_id={"cand": peer}, device_id_type=MESH,
        )

    def owned_from(turn, part, o, source):
        return pltpu.make_async_remote_copy(
            src_ref=rs_send.at[turn, part, o], dst_ref=rs_slots.at[turn, part, source],
            send_sem=rs_out.at[turn, part, o], recv_sem=rs_in.at[turn, part, source],
            device_id={"cand": source}, device_id_type=MESH,
        )

    def others(o):
        return [z for z in range(n_cand) if z != owners[o]]

    halves = range(len(owners))

    def tgt_send(kernel, turn, part):
        lhs = split_rows(1.0 / cand_sums[of(part), :])
        for o in (far, near):
            rs_send[turn, part, o] = join_rows(
                lax.dot_general(lhs, kernel[:, half(o)], NN_DIMS, preferred_element_type=F32)
            )
            if o is far:
                to_owner(turn, part, o).start()
                continue

            @pl.when(zi != owners[0] + o)
            def _():
                to_owner(turn, part, o).start()

    def tgt_finish(turn, part, change):
        for o in halves:

            @pl.when(zi == owners[o])
            def _():
                for z in others(o):
                    owned_from(turn, part, o, z).wait_recv()
                total = None
                for z in range(n_cand):
                    own = z == owners[o]
                    value = rs_send[turn, part, o] if own else rs_slots[turn, part, z]
                    total = value if total is None else total + value
                ag_slots[turn, part, o] = change(mass[of(part), half(o)] / total)
                for z in others(o):
                    from_owner(turn, part, o, z).start()

    def gathered(turn, part, o):
        @pl.when(zi != owners[0] + o)
        def _():
            from_owner(turn, part, o, owners[0] + o).wait_recv()

    def drain(turn, part):
        for o in halves:

            @pl.when(zi != owners[o])
            def _():
                to_owner(turn, part, o).wait_send()

            @pl.when(zi == owners[o])
            def _():
                for z in others(o):
                    from_owner(turn, part, o, z).wait_send()

    def cand_send(turn, part):
        total = None
        for o in (near, far):
            gathered(turn, part, o)
            value = contract_last(split_rows(ag_slots[turn, part, o]), k_two[:, half(o)])
            total = value if total is None else total + value
        cand_slots[turn, part, 0] = join_rows(total)
        return x_start(cand_slots.at[turn, part], 2 + turn * parts + part)

    def cand_finish(copies, turn, part):
        arrive(copies)
        cand_sums[of(part), :] = x_sum(cand_slots.at[turn, part])

    def keep(scale):
        return scale

    each = range(parts)
    for part in each:
        tgt_send(k_one, 0, part)
    changes = (jnp.square,) + (keep,) * (ITERS - 1)
    for turn in range(ITERS):
        for part in each:
            tgt_finish(turn, part, changes[turn])
        summed = [cand_send(turn, part) for part in each]
        for part in each:
            cand_finish(summed[part], turn, part)
            tgt_send(k_two, 1 + turn, part)
    out_cand[...] = -jnp.log(cand_sums[...])
    for part in each:
        tgt_finish(ITERS, part, jnp.log)
    for part in each:
        for o in halves:
            gathered(ITERS, part, o)
            out_tgt[of(part), half(o)] = ag_slots[ITERS, part, o]
    for turn in range(1 + ITERS):
        for part in each:
            drain(turn, part)
    for copy in pending + row_copies:
        copy.wait_send()


def fused(candidates, targets, member, mix_weight):
    n_tgt, n_cand = lax.axis_size("tgt"), lax.axis_size("cand")
    rows, width = candidates.shape
    cols = targets.shape[0]
    mixes, tasks = mix_weight.shape
    share = cols // 2
    parts = 2 if mixes % 16 == 0 else 1
    group = mixes // parts
    return tuple(pl.pallas_call(
        functools.partial(fused_kernel, n_tgt, n_cand, parts),
        out_shape=(
            jax.ShapeDtypeStruct((mixes, rows), F32),
            jax.ShapeDtypeStruct((mixes, cols), F32),
        ),
        in_specs=[pl.BlockSpec(memory_space=pltpu.HBM)] * 2
        + [pl.BlockSpec(memory_space=pltpu.VMEM)] * 2,
        out_specs=(pl.BlockSpec(memory_space=pltpu.VMEM),) * 2,
        scratch_shapes=[
            pltpu.VMEM((rows, width), BF16),
            pltpu.VMEM((cols, width), BF16),
            pltpu.VMEM((cols, width), BF16),
            pltpu.VMEM((rows, cols), F32),
            pltpu.VMEM((rows, cols), BF16),
            pltpu.VMEM((rows, cols), BF16),
            pltpu.VMEM((mixes, cols), F32),
            pltpu.VMEM((mixes, rows), F32),
            pltpu.VMEM((1, rows), F32),
            pltpu.VMEM((n_tgt, 1, rows), F32),
            pltpu.VMEM((n_cand, 1, cols), F32),
            pltpu.VMEM((n_tgt, tasks, rows), F32),
            pltpu.VMEM((ITERS, parts, n_tgt, group, rows), F32),
            pltpu.VMEM((1 + ITERS, parts, 2, group, share), F32),
            pltpu.VMEM((1 + ITERS, parts, n_cand, group, share), F32),
            pltpu.VMEM((1 + ITERS, parts, 2, group, share), F32),
            pltpu.SemaphoreType.DMA((2, max(rows, cols) // 256)),
            pltpu.SemaphoreType.DMA((2 + ITERS * parts, n_tgt - 1)),
            pltpu.SemaphoreType.DMA((2 + ITERS * parts, n_tgt - 1)),
            pltpu.SemaphoreType.DMA((1, n_cand - 1)),
            pltpu.SemaphoreType.DMA((1, n_cand - 1)),
            pltpu.SemaphoreType.DMA((n_tgt - 1, rows // 256)),
            pltpu.SemaphoreType.DMA((n_tgt - 1, rows // 256)),
            pltpu.SemaphoreType.DMA((1 + ITERS, parts, 2)),
            pltpu.SemaphoreType.DMA((1 + ITERS, parts, n_cand)),
            pltpu.SemaphoreType.DMA((1 + ITERS, parts, n_cand)),
            pltpu.SemaphoreType.DMA((1 + ITERS, parts, 2)),
        ],
        compiler_params=pltpu.CompilerParams(
            collective_id=0, has_side_effects=True, vmem_limit_bytes=56 * 1024 * 1024
        ),
    )(candidates, targets, member.reshape(1, -1), mix_weight.T))


def target_mass(own_member, member, mix_weight, cand_total):
    task_ids = jnp.arange(mix_weight.shape[1], dtype=jnp.int32)
    counts = jnp.sum((member[None, :] == task_ids[:, None]).astype(jnp.float32), axis=1)
    weight_total = jnp.dot(mix_weight, counts, precision=lax.Precision.HIGHEST)
    onehot = (own_member[None, :] == task_ids[:, None]).astype(jnp.float32)
    per_target = jnp.dot(mix_weight, onehot, precision=lax.Precision.HIGHEST)
    return per_target * (cand_total / weight_total)[:, None]


def by_collectives(candidates, targets, member, mix_weight):
    cand_rows = candidates.shape[0]
    tgt_rows = targets.shape[0]
    tgt_total = tgt_rows * lax.axis_size("tgt")
    cand_total = cand_rows * lax.axis_size("cand")
    tgt_unit = unit_rows(targets)
    scores = contract_last(unit_rows(candidates), tgt_unit)
    own_member = lax.dynamic_slice_in_dim(member, lax.axis_index("tgt") * tgt_rows, tgt_rows, 0)
    mass = target_mass(own_member, member, mix_weight, float(cand_total))
    kernel_one = jnp.exp(scores / EPS_FIRST) / tgt_total
    kernel_two = jnp.exp(scores / EPS_SECOND) / tgt_total
    scale_tgt = jnp.ones((mix_weight.shape[0], tgt_rows), jnp.float32)
    scale_cand = jnp.ones((mix_weight.shape[0], cand_rows), jnp.float32)
    for section_index, kernel in enumerate((kernel_one, kernel_two)):
        if section_index == 1:
            scale_tgt = scale_tgt * scale_tgt
        for repeat in range(ITERS):
            partial_value = lax.dot_general(
                scale_tgt, kernel, (((1,), (1,)), ((), ())), precision=lax.Precision.HIGHEST
            )
            scale_cand = 1.0 / lax.psum(partial_value, "tgt")
            column_part = jnp.dot(scale_cand, kernel, precision=lax.Precision.HIGHEST)
            share_cols = tgt_rows // lax.axis_size("cand")
            summed = lax.psum_scatter(column_part, "cand", scatter_dimension=1, tiled=True)
            own_mass = lax.dynamic_slice_in_dim(
                mass, lax.axis_index("cand") * share_cols, share_cols, 1
            )
            scale_tgt = lax.all_gather(own_mass / summed, "cand", axis=1, tiled=True)
    return (jnp.log(scale_cand), jnp.log(scale_tgt))


def solution(mesh):
    in_specs = (
        P(("groups", "cand"), None),
        P(("groups", "tgt"), None),
        P("groups"),
        P("mix", "groups"),
    )
    out_specs = (P("mix", ("groups", "cand")), P("mix", ("groups", "tgt")))
    n_tgt, n_cand = mesh.shape["tgt"], mesh.shape["cand"]

    def local(candidates, targets, member, mix_weight):
        lanes = targets.shape[0] % (128 * n_cand) == 0 and candidates.shape[0] % 512 == 0
        step = fused if lanes and n_cand % 2 == 0 and n_tgt > 1 else by_collectives
        return step(candidates, targets, member, mix_weight)

    return jax.shard_map(local, mesh=mesh, in_specs=in_specs, out_specs=out_specs, check_vma=False)
```

```python
import functools
import math

import jax
import jax.numpy as jnp
from jax import lax
from jax.experimental import pallas as pl
from jax.experimental.pallas import tpu as pltpu
from jax.sharding import PartitionSpec as P

ITERS = 2


EPS_FIRST = 0.05
EPS_SECOND = 0.025

MESH = pl.DeviceIdType.MESH
F32 = jnp.float32
BF16 = jnp.bfloat16
NT_DIMS = (((1,), (1,)), ((), ()))
TN_DIMS = (((0,), (0,)), ((), ()))
NN_DIMS = (((1,), (0,)), ((), ()))


def unit_rows(embedding):
    values = embedding.astype(jnp.float32)
    mean_sq = jnp.mean(values * values, axis=1, keepdims=True)
    return (values * (lax.rsqrt(mean_sq + 1e-06) * (1.0 / math.sqrt(values.shape[1])))).astype(
        jnp.bfloat16
    )


def contract_last(left, right):
    return lax.dot_general(left, right, NT_DIMS, preferred_element_type=jnp.float32)


def fused_kernel(
    n_tgt, n_cand, n_mix, parts, cand_hbm, tgt_hbm, member_ref, weight_ref, out_cand, out_tgt,
    cand_rows, tgt_rows, tgt_unit, raised, k_one, k_two, mass, cand_sums, weights, cand_in,
    row_part, row_slots, col_slots, task_slots, cand_slots, rs_send, rs_slots, ag_slots,
    load_sems, x_send, x_recv, z_send, z_recv, row_out, row_in, rs_out, rs_in, ag_out, ag_in,
    chip_out, chip_in,
):
    xi, zi, ci = lax.axis_index("tgt"), lax.axis_index("cand"), lax.axis_index("mix")
    rows, width = cand_hbm.shape
    cols = tgt_hbm.shape[0]
    tasks, mixes = weight_ref.shape
    lead = n_mix - 1
    owners = (n_cand // 2 - 1, n_cand // 2)
    share = cols // len(owners)
    group = mixes * n_mix // parts
    tgt_total, cand_total = cols * n_tgt, rows * n_cand
    block = 256
    early = rows // n_mix

    def load(src, dst, row, at):
        at = at if isinstance(at, int) else pl.multiple_of(at, block)
        return pltpu.make_async_copy(
            src.at[pl.ds(at, block)], dst.at[pl.ds(at, block)], load_sems.at[row, at // block]
        )

    def cand_loads(core):
        return [load(cand_hbm, cand_rows, 1, core * early + at) for at in range(0, early, block)]

    tgt_loads = [load(tgt_hbm, tgt_rows, 0, at) for at in range(0, cols, block)]
    for copy in tgt_loads + cand_loads(ci):
        copy.start()

    def x_peer(d):
        return {"tgt": lax.rem(xi + d, n_tgt), "mix": lead}

    def z_peer(d):
        return {"cand": lax.rem(zi + d, n_cand), "mix": lead}

    barrier = pltpu.get_barrier_semaphore()

    def hello(**peer):
        pl.semaphore_signal(barrier, inc=1, device_id=peer, device_id_type=MESH)

    for d in range(1, n_cand):
        hello(**z_peer(d))

    @pl.when(ci == lead)
    def _():
        for core in range(lead):
            for copy in cand_loads(core):
                copy.start()
            hello(mix=core)
        for d in range(1, n_tgt):
            for core in range(n_mix):
                hello(tgt=lax.rem(xi + d, n_tgt), mix=core)

    @pl.when(ci != lead)
    def _():
        hello(mix=lead)

    for index, copy in enumerate(tgt_loads):
        copy.wait()
        at = pl.ds(index * block, block)
        tgt_unit[at, :] = unit_rows(tgt_rows[at, :])
    for copy in cand_loads(ci):
        copy.wait()
    ones = jnp.ones((16, cols), BF16)

    def build(first):
        at = pl.ds(first if isinstance(first, int) else pl.multiple_of(first, block), block)
        scores = contract_last(unit_rows(cand_rows[at, :]), tgt_unit[...])
        power = jnp.exp(scores * (1.0 / EPS_FIRST))
        raised[at, :] = power
        kernel_rows = (power * (1.0 / tgt_total)).astype(BF16)
        k_one[at, :] = kernel_rows
        return contract_last(ones, kernel_rows)[:1]

    for first in range(0, early, block):
        row_part[ci, :, pl.ds(first, block)] = build(ci * early + first)

    def row_copy(d, core):
        return pltpu.make_async_remote_copy(
            src_ref=row_part.at[core], dst_ref=row_slots.at[d, core],
            send_sem=row_out.at[d - 1], recv_sem=row_in.at[d - 1, core],
            device_id=x_peer(d), device_id_type=MESH,
        )

    def weight_copy(core):
        return pltpu.make_async_remote_copy(
            src_ref=weights.at[core], dst_ref=weights.at[core],
            send_sem=chip_out.at[0, core], recv_sem=chip_in.at[0, core],
            device_id={"mix": lead}, device_id_type=MESH,
        )

    def cand_copy(core):
        return pltpu.make_async_remote_copy(
            src_ref=cand_sums.at[pl.ds(core * mixes, mixes)], dst_ref=cand_in,
            send_sem=chip_out.at[1, core], recv_sem=chip_in.at[1, core],
            device_id={"mix": core}, device_id_type=MESH,
        )

    def of(part):
        return pl.ds(part * group, group)

    def half(o):
        return pl.ds(o * share if isinstance(o, int) else pl.multiple_of(o * share, share), share)

    def to_owner(turn, part, o):
        return pltpu.make_async_remote_copy(
            src_ref=rs_send.at[turn, part, o], dst_ref=rs_slots.at[turn, part, zi],
            send_sem=rs_out.at[turn, part, o], recv_sem=rs_in.at[turn, part, zi],
            device_id={"cand": owners[0] + o, "mix": lead}, device_id_type=MESH,
        )

    def owned_from(turn, part, o, source):
        return pltpu.make_async_remote_copy(
            src_ref=rs_send.at[turn, part, o], dst_ref=rs_slots.at[turn, part, source],
            send_sem=rs_out.at[turn, part, o], recv_sem=rs_in.at[turn, part, source],
            device_id={"cand": source, "mix": lead}, device_id_type=MESH,
        )

    def from_owner(turn, part, o, peer, core):
        return pltpu.make_async_remote_copy(
            src_ref=ag_slots.at[turn, part, o], dst_ref=ag_slots.at[turn, part, o],
            send_sem=ag_out.at[turn, part, peer], recv_sem=ag_in.at[turn, part, o],
            device_id={"cand": peer, "mix": core}, device_id_type=MESH,
        )

    def core_of(turn, part):
        return part * n_mix // parts if turn == ITERS else lead

    def takers(turn, part, o):
        away = core_of(turn, part) != lead
        return [z for z in range(n_cand) if away or z != owners[o]]

    def parts_of(core):
        return [part for part in range(parts) if core_of(ITERS, part) == core]

    def row_of(part):
        return pl.ds(part * group % mixes, group)

    halves = range(len(owners))
    each = range(parts)

    @pl.when(ci != lead)
    def _():
        weights[ci] = jnp.zeros(weights.shape[1:], F32)
        weights[ci, :, pl.ds(0, mixes)] = weight_ref[...]
        pl.semaphore_wait(barrier, n_tgt)
        sent = [row_copy(d, ci) for d in range(1, n_tgt)] + [weight_copy(ci)]
        for copy in sent:
            copy.start()
        cand_copy(ci).wait_recv()
        out_cand[...] = -jnp.log(cand_in[...])
        for core in range(lead):

            @pl.when(ci == core)
            def _():
                for part in parts_of(core):
                    for o in halves:
                        from_owner(ITERS, part, o, owners[o], lead).wait_recv()
                        out_tgt[row_of(part), half(o)] = ag_slots[ITERS, part, o]
        for copy in sent:
            copy.wait_send()

    @pl.when(ci == lead)
    def _():
        pl.semaphore_wait(barrier, n_tgt - 1 + n_mix * (n_cand - 1) + lead)
        pending = [row_copy(d, lead) for d in range(1, n_tgt)]
        for copy in pending:
            copy.start()
        for core in range(lead):
            for copy in cand_loads(core):
                copy.wait()
            for first in range(0, early, block):
                row_part[core, :, pl.ds(first, block)] = build(core * early + first)

        xs, zs = (x_send, x_recv), (z_send, z_recv)

        def send(src, dst, sems, phase, d, peer):
            copy = pltpu.make_async_remote_copy(
                src_ref=src, dst_ref=dst,
                send_sem=sems[0].at[phase, d - 1], recv_sem=sems[1].at[phase, d - 1],
                device_id=peer, device_id_type=MESH,
            )
            copy.start()
            pending.append(copy)
            return copy

        def x_sum(slots):
            total = slots[lax.rem(xi + n_tgt, n_tgt)]
            for k in range(1, n_tgt):
                total = total + slots[lax.rem(xi - k + n_tgt, n_tgt)]
            return total

        def z_sum(slots):
            total = slots[lax.rem(zi + n_cand, n_cand)]
            for k in range(1, n_cand):
                total = total + slots[lax.rem(zi - k + n_cand, n_cand)]
            return total

        def x_start(slots, phase):
            return [
                send(slots.at[0], slots.at[d], xs, phase, d, x_peer(d)) for d in range(1, n_tgt)
            ]

        def z_start(slots, phase):
            return [
                send(slots.at[0], slots.at[d], zs, phase, d, z_peer(d)) for d in range(1, n_cand)
            ]

        def arrive(copies):
            for copy in copies:
                copy.wait_recv()

        for d in range(1, n_tgt):
            for core in range(n_mix):
                row_copy(d, core).wait_recv()
        row_sums = []
        for core in range(n_mix):
            value = row_part[core]
            for d in range(1, n_tgt):
                value = value + row_slots[d, core]
            row_sums.append(value)
        scale_row = 1.0 / jnp.concatenate(row_sums, axis=1)
        place = lax.broadcasted_iota(jnp.int32, (16, rows), 0)
        head = scale_row.astype(BF16).astype(F32)
        lhs = jnp.where(place == 0, head, jnp.where(place == 1, scale_row - head, 0.0)).astype(BF16)
        part_sum = lax.dot_general(lhs, k_one[...], NN_DIMS, preferred_element_type=F32)
        col_slots[0] = part_sum[:1] + part_sum[1:2]
        copies = z_start(col_slots, 0)

        def square(b, carry):
            at = pl.ds(pl.multiple_of(b * 64, 64), 64)
            power = raised[at, :]
            k_two[at, :] = (power * power * (1.0 / tgt_total)).astype(BF16)
            return carry

        lax.fori_loop(0, rows // 64, square, 0)
        for core in range(lead):
            weight_copy(core).wait_recv()
        all_weights = jnp.concatenate(
            [weights[core, :, :mixes] for core in range(lead)] + [weight_ref[...]], axis=1
        )
        all_hot = member_ref[...] == lax.broadcasted_iota(jnp.int32, (tasks, tgt_total), 0)
        counts = jnp.sum(all_hot.astype(F32), axis=1, keepdims=True)
        totals = jnp.sum(all_weights * counts, axis=0, keepdims=True)
        scaled = all_weights * (float(cand_total) / totals)
        own = pl.ds(pl.multiple_of(xi * cols, cols), cols)
        own_hot = (
            member_ref[:, own] == lax.broadcasted_iota(jnp.int32, (tasks, cols), 0)
        ).astype(F32)
        mass[...] = lax.dot_general(
            scaled, own_hot, TN_DIMS, precision=lax.Precision.HIGHEST, preferred_element_type=F32
        )
        arrive(copies)
        col_sum = z_sum(col_slots)

        task_slots[0] = contract_last((own_hot / col_sum).astype(BF16), k_one[...])
        arrive(x_start(task_slots, 0))
        cand_sums[...] = lax.dot_general(
            scaled, x_sum(task_slots), TN_DIMS, precision=lax.Precision.HIGHEST,
            preferred_element_type=F32,
        )

        far = 1 - zi // owners[1]
        near = 1 - far

        def tgt_send(kernel, turn, part):
            lhs = (1.0 / cand_sums[of(part), :]).astype(BF16)
            for o in (far, near):
                rs_send[turn, part, o] = lax.dot_general(
                    lhs, kernel[:, half(o)], NN_DIMS, preferred_element_type=F32
                )
                if o is far:
                    to_owner(turn, part, o).start()
                    continue

                @pl.when(zi != owners[0] + o)
                def _():
                    to_owner(turn, part, o).start()

        def tgt_finish(turn, part, change):
            for o in halves:

                @pl.when(zi == owners[o])
                def _():
                    for z in range(n_cand):
                        if z != owners[o]:
                            owned_from(turn, part, o, z).wait_recv()
                    total = None
                    for z in range(n_cand):
                        own = z == owners[o]
                        value = rs_send[turn, part, o] if own else rs_slots[turn, part, z]
                        total = value if total is None else total + value
                    ag_slots[turn, part, o] = change(mass[of(part), half(o)] / total)
                    for z in takers(turn, part, o):
                        from_owner(turn, part, o, z, core_of(turn, part)).start()

        def gathered(turn, part, o):
            @pl.when(zi != owners[0] + o)
            def _():
                from_owner(turn, part, o, owners[0] + o, lead).wait_recv()

        def drain(turn, part):
            for o in halves:

                @pl.when(zi != owners[o])
                def _():
                    to_owner(turn, part, o).wait_send()

                @pl.when(zi == owners[o])
                def _():
                    for z in takers(turn, part, o):
                        from_owner(turn, part, o, z, core_of(turn, part)).wait_send()

        def cand_send(turn, part):
            total = None
            for o in (near, far):
                gathered(turn, part, o)
                value = contract_last(ag_slots[turn, part, o].astype(BF16), k_two[:, half(o)])
                total = value if total is None else total + value
            cand_slots[turn, part, 0] = total
            return x_start(cand_slots.at[turn, part], 1 + turn * parts + part)

        def cand_finish(copies, turn, part):
            arrive(copies)
            cand_sums[of(part), :] = x_sum(cand_slots.at[turn, part])

        def keep(scale):
            return scale

        for part in each:
            tgt_send(k_one, 0, part)
        changes = (jnp.square,) + (keep,) * (ITERS - 1)
        for turn in range(ITERS):
            for part in each:
                tgt_finish(turn, part, changes[turn])
            summed = [cand_send(turn, part) for part in each]
            for part in each:
                cand_finish(summed[part], turn, part)
                tgt_send(k_two, 1 + turn, part)
        for core in range(lead):
            cand_copy(core).start()
        out_cand[...] = -jnp.log(cand_sums[pl.ds(lead * mixes, mixes), :])
        for part in each:
            tgt_finish(ITERS, part, jnp.log)
        for part in parts_of(lead):
            for o in halves:
                gathered(ITERS, part, o)
                out_tgt[row_of(part), half(o)] = ag_slots[ITERS, part, o]
        for turn in range(1 + ITERS):
            for part in each:
                drain(turn, part)
        for core in range(lead):
            cand_copy(core).wait_send()
        for copy in pending:
            copy.wait_send()


def fused(candidates, targets, member, mix_weight):
    n_tgt, n_cand, n_mix = lax.axis_size("tgt"), lax.axis_size("cand"), lax.axis_size("mix")
    rows, width = candidates.shape
    cols = targets.shape[0]
    mixes, tasks = mix_weight.shape
    share = cols // 2
    parts = 2 * n_mix if mixes % 16 == 0 else n_mix
    group = mixes * n_mix // parts
    return tuple(pl.pallas_call(
        functools.partial(fused_kernel, n_tgt, n_cand, n_mix, parts),
        out_shape=(
            jax.ShapeDtypeStruct((mixes, rows), F32),
            jax.ShapeDtypeStruct((mixes, cols), F32),
        ),
        in_specs=[pl.BlockSpec(memory_space=pltpu.HBM)] * 2
        + [pl.BlockSpec(memory_space=pltpu.VMEM)] * 2,
        out_specs=(pl.BlockSpec(memory_space=pltpu.VMEM),) * 2,
        scratch_shapes=[
            pltpu.VMEM((rows, width), BF16),
            pltpu.VMEM((cols, width), BF16),
            pltpu.VMEM((cols, width), BF16),
            pltpu.VMEM((rows, cols), F32),
            pltpu.VMEM((rows, cols), BF16),
            pltpu.VMEM((rows, cols), BF16),
            pltpu.VMEM((mixes * n_mix, cols), F32),
            pltpu.VMEM((mixes * n_mix, rows), F32),
            pltpu.VMEM((n_mix, tasks, 128), F32),
            pltpu.VMEM((mixes, rows), F32),
            pltpu.VMEM((n_mix, 1, rows // n_mix), F32),
            pltpu.VMEM((n_tgt, n_mix, 1, rows // n_mix), F32),
            pltpu.VMEM((n_cand, 1, cols), F32),
            pltpu.VMEM((n_tgt, tasks, rows), F32),
            pltpu.VMEM((ITERS, parts, n_tgt, group, rows), F32),
            pltpu.VMEM((1 + ITERS, parts, 2, group, share), F32),
            pltpu.VMEM((1 + ITERS, parts, n_cand, group, share), F32),
            pltpu.VMEM((1 + ITERS, parts, 2, group, share), F32),
            pltpu.SemaphoreType.DMA((2, max(rows, cols) // 256)),
            pltpu.SemaphoreType.DMA((1 + ITERS * parts, n_tgt - 1)),
            pltpu.SemaphoreType.DMA((1 + ITERS * parts, n_tgt - 1)),
            pltpu.SemaphoreType.DMA((1, n_cand - 1)),
            pltpu.SemaphoreType.DMA((1, n_cand - 1)),
            pltpu.SemaphoreType.DMA((n_tgt - 1,)),
            pltpu.SemaphoreType.DMA((n_tgt - 1, n_mix)),
            pltpu.SemaphoreType.DMA((1 + ITERS, parts, 2)),
            pltpu.SemaphoreType.DMA((1 + ITERS, parts, n_cand)),
            pltpu.SemaphoreType.DMA((1 + ITERS, parts, n_cand)),
            pltpu.SemaphoreType.DMA((1 + ITERS, parts, 2)),
            pltpu.SemaphoreType.DMA((2, n_mix)),
            pltpu.SemaphoreType.DMA((2, n_mix)),
        ],
        compiler_params=pltpu.CompilerParams(
            collective_id=0, has_side_effects=True, vmem_limit_bytes=56 * 1024 * 1024
        ),
    )(candidates, targets, member.reshape(1, -1), mix_weight.T))


def target_mass(own_member, member, mix_weight, cand_total):
    task_ids = jnp.arange(mix_weight.shape[1], dtype=jnp.int32)
    counts = jnp.sum((member[None, :] == task_ids[:, None]).astype(jnp.float32), axis=1)
    weight_total = jnp.dot(mix_weight, counts, precision=lax.Precision.HIGHEST)
    onehot = (own_member[None, :] == task_ids[:, None]).astype(jnp.float32)
    per_target = jnp.dot(mix_weight, onehot, precision=lax.Precision.HIGHEST)
    return per_target * (cand_total / weight_total)[:, None]


def by_collectives(candidates, targets, member, mix_weight):
    cand_rows = candidates.shape[0]
    tgt_rows = targets.shape[0]
    tgt_total = tgt_rows * lax.axis_size("tgt")
    cand_total = cand_rows * lax.axis_size("cand")
    tgt_unit = unit_rows(targets)
    scores = contract_last(unit_rows(candidates), tgt_unit)
    own_member = lax.dynamic_slice_in_dim(member, lax.axis_index("tgt") * tgt_rows, tgt_rows, 0)
    mass = target_mass(own_member, member, mix_weight, float(cand_total))
    kernel_one = jnp.exp(scores / EPS_FIRST) / tgt_total
    kernel_two = jnp.exp(scores / EPS_SECOND) / tgt_total
    scale_tgt = jnp.ones((mix_weight.shape[0], tgt_rows), jnp.float32)
    scale_cand = jnp.ones((mix_weight.shape[0], cand_rows), jnp.float32)
    for section_index, kernel in enumerate((kernel_one, kernel_two)):
        if section_index == 1:
            scale_tgt = scale_tgt * scale_tgt
        for repeat in range(ITERS):
            partial_value = lax.dot_general(
                scale_tgt, kernel, (((1,), (1,)), ((), ())), precision=lax.Precision.HIGHEST
            )
            scale_cand = 1.0 / lax.psum(partial_value, "tgt")
            column_part = jnp.dot(scale_cand, kernel, precision=lax.Precision.HIGHEST)
            share_cols = tgt_rows // lax.axis_size("cand")
            summed = lax.psum_scatter(column_part, "cand", scatter_dimension=1, tiled=True)
            own_mass = lax.dynamic_slice_in_dim(
                mass, lax.axis_index("cand") * share_cols, share_cols, 1
            )
            scale_tgt = lax.all_gather(own_mass / summed, "cand", axis=1, tiled=True)
    return (jnp.log(scale_cand), jnp.log(scale_tgt))


def solution(mesh):
    in_specs = (
        P(("groups", "cand"), None),
        P(("groups", "tgt"), None),
        P("groups"),
        P("mix", "groups"),
    )
    out_specs = (P("mix", ("groups", "cand")), P("mix", ("groups", "tgt")))
    n_tgt, n_cand, n_mix = mesh.shape["tgt"], mesh.shape["cand"], mesh.shape["mix"]

    def local(candidates, targets, member, mix_weight):
        lanes = targets.shape[0] % (128 * n_cand) == 0 and candidates.shape[0] % 512 == 0
        paired = n_cand % 2 == 0 and n_tgt > 1 and n_mix == 2
        step = fused if lanes and paired else by_collectives
        return step(candidates, targets, member, mix_weight)

    return jax.shard_map(local, mesh=mesh, in_specs=in_specs, out_specs=out_specs, check_vma=False)
```

```python
import functools
import math

import jax
import jax.numpy as jnp
from jax import lax
from jax.experimental import pallas as pl
from jax.experimental.pallas import tpu as pltpu
from jax.sharding import PartitionSpec as P

ITERS = 2


EPS_FIRST = 0.05
EPS_SECOND = 0.025

MESH = pl.DeviceIdType.MESH
F32 = jnp.float32
BF16 = jnp.bfloat16
NT_DIMS = (((1,), (1,)), ((), ()))
TN_DIMS = (((0,), (0,)), ((), ()))
NN_DIMS = (((1,), (0,)), ((), ()))


def unit_rows(embedding):
    values = embedding.astype(jnp.float32)
    mean_sq = jnp.mean(values * values, axis=1, keepdims=True)
    return (values * (lax.rsqrt(mean_sq + 1e-06) * (1.0 / math.sqrt(values.shape[1])))).astype(
        jnp.bfloat16
    )


def contract_last(left, right):
    return lax.dot_general(left, right, NT_DIMS, preferred_element_type=jnp.float32)


def fused_kernel(
    n_tgt, n_cand, n_mix, parts, cand_hbm, tgt_hbm, member_ref, weight_ref, out_cand, out_tgt,
    cand_rows, tgt_rows, tgt_unit, raised, k_one, k_two, mass, cand_sums, weights, cand_in,
    row_part, row_slots, col_slots, task_slots, cand_slots, rs_send, rs_slots, ag_slots,
    load_sems, x_send, x_recv, z_send, z_recv, row_out, row_in, rs_out, rs_in, ag_out, ag_in,
    chip_out, chip_in,
):
    xi, zi, ci = lax.axis_index("tgt"), lax.axis_index("cand"), lax.axis_index("mix")
    rows, width = cand_hbm.shape
    cols = tgt_hbm.shape[0]
    tasks, mixes = weight_ref.shape
    lead = n_mix - 1
    owners = (n_cand // 2 - 1, n_cand // 2)
    share = cols // len(owners)
    group = mixes * n_mix // parts
    tgt_total, cand_total = cols * n_tgt, rows * n_cand
    block = 256
    early = rows // n_mix

    def load(src, dst, row, at):
        at = at if isinstance(at, int) else pl.multiple_of(at, block)
        return pltpu.make_async_copy(
            src.at[pl.ds(at, block)], dst.at[pl.ds(at, block)], load_sems.at[row, at // block]
        )

    def cand_loads(core):
        return [load(cand_hbm, cand_rows, 1, core * early + at) for at in range(0, early, block)]

    tgt_loads = [load(tgt_hbm, tgt_rows, 0, at) for at in range(0, cols, block)]
    for copy in tgt_loads + cand_loads(ci):
        copy.start()

    def x_peer(d):
        return {"tgt": lax.rem(xi + d, n_tgt), "mix": lead}

    def z_peer(d):
        return {"cand": lax.rem(zi + d, n_cand), "mix": lead}

    barrier = pltpu.get_barrier_semaphore()

    def hello(**peer):
        pl.semaphore_signal(barrier, inc=1, device_id=peer, device_id_type=MESH)

    for d in range(1, n_cand):
        hello(**z_peer(d))

    @pl.when(ci == lead)
    def _():
        for core in range(lead):
            for copy in cand_loads(core):
                copy.start()
            hello(mix=core)
        for d in range(1, n_tgt):
            for core in range(n_mix):
                hello(tgt=lax.rem(xi + d, n_tgt), mix=core)

    @pl.when(ci != lead)
    def _():
        hello(mix=lead)

    for index, copy in enumerate(tgt_loads):
        copy.wait()
        at = pl.ds(index * block, block)
        tgt_unit[at, :] = unit_rows(tgt_rows[at, :])
    for copy in cand_loads(ci):
        copy.wait()
    ones = jnp.ones((16, cols), BF16)

    def build(first):
        at = pl.ds(first if isinstance(first, int) else pl.multiple_of(first, block), block)
        scores = contract_last(unit_rows(cand_rows[at, :]), tgt_unit[...])
        power = jnp.exp(scores * (1.0 / EPS_FIRST))
        raised[at, :] = power
        kernel_rows = (power * (1.0 / tgt_total)).astype(BF16)
        k_one[at, :] = kernel_rows
        return contract_last(ones, kernel_rows)[:1]

    for first in range(0, early, block):
        row_part[ci, :, pl.ds(first, block)] = build(ci * early + first)

    def row_copy(d, core):
        return pltpu.make_async_remote_copy(
            src_ref=row_part.at[core], dst_ref=row_slots.at[d, core],
            send_sem=row_out.at[d - 1], recv_sem=row_in.at[d - 1, core],
            device_id=x_peer(d), device_id_type=MESH,
        )

    def weight_copy(core):
        return pltpu.make_async_remote_copy(
            src_ref=weights.at[core], dst_ref=weights.at[core],
            send_sem=chip_out.at[0, core], recv_sem=chip_in.at[0, core],
            device_id={"mix": lead}, device_id_type=MESH,
        )

    def cand_copy(core):
        return pltpu.make_async_remote_copy(
            src_ref=cand_sums.at[pl.ds(core * mixes, mixes)], dst_ref=cand_in,
            send_sem=chip_out.at[1, core], recv_sem=chip_in.at[1, core],
            device_id={"mix": core}, device_id_type=MESH,
        )

    def of(part):
        return pl.ds(part * group, group)

    def half(o):
        return pl.ds(o * share if isinstance(o, int) else pl.multiple_of(o * share, share), share)

    def to_owner(turn, part, o):
        return pltpu.make_async_remote_copy(
            src_ref=rs_send.at[turn, part, o], dst_ref=rs_slots.at[turn, part, zi],
            send_sem=rs_out.at[turn, part, o], recv_sem=rs_in.at[turn, part, zi],
            device_id={"cand": owners[0] + o, "mix": lead}, device_id_type=MESH,
        )

    def owned_from(turn, part, o, source):
        return pltpu.make_async_remote_copy(
            src_ref=rs_send.at[turn, part, o], dst_ref=rs_slots.at[turn, part, source],
            send_sem=rs_out.at[turn, part, o], recv_sem=rs_in.at[turn, part, source],
            device_id={"cand": source, "mix": lead}, device_id_type=MESH,
        )

    def from_owner(turn, part, o, peer, core):
        return pltpu.make_async_remote_copy(
            src_ref=ag_slots.at[turn, part, o], dst_ref=ag_slots.at[turn, part, o],
            send_sem=ag_out.at[turn, part, peer], recv_sem=ag_in.at[turn, part, o],
            device_id={"cand": peer, "mix": core}, device_id_type=MESH,
        )

    def core_of(turn, part):
        return part * n_mix // parts if turn == ITERS else lead

    def takers(turn, part, o):
        away = core_of(turn, part) != lead
        return [z for z in range(n_cand) if away or z != owners[o]]

    def parts_of(core):
        return [part for part in range(parts) if core_of(ITERS, part) == core]

    def row_of(part):
        return pl.ds(part * group % mixes, group)

    halves = range(len(owners))
    each = range(parts)

    @pl.when(ci != lead)
    def _():
        weights[ci] = jnp.zeros(weights.shape[1:], F32)
        weights[ci, :, pl.ds(0, mixes)] = weight_ref[...]
        pl.semaphore_wait(barrier, n_tgt)
        sent = [row_copy(d, ci) for d in range(1, n_tgt)] + [weight_copy(ci)]
        for copy in sent:
            copy.start()
        cand_copy(ci).wait_recv()
        out_cand[...] = cand_in[...]
        for core in range(lead):

            @pl.when(ci == core)
            def _():
                for part in parts_of(core):
                    for o in halves:
                        from_owner(ITERS, part, o, owners[o], lead).wait_recv()
                        out_tgt[row_of(part), half(o)] = ag_slots[ITERS, part, o]
        for copy in sent:
            copy.wait_send()

    @pl.when(ci == lead)
    def _():
        pl.semaphore_wait(barrier, n_tgt - 1 + n_mix * (n_cand - 1) + lead)
        pending = [row_copy(d, lead) for d in range(1, n_tgt)]
        for copy in pending:
            copy.start()
        for core in range(lead):
            for copy in cand_loads(core):
                copy.wait()
            for first in range(0, early, block):
                row_part[core, :, pl.ds(first, block)] = build(core * early + first)

        xs, zs = (x_send, x_recv), (z_send, z_recv)

        def send(src, dst, sems, phase, d, peer):
            copy = pltpu.make_async_remote_copy(
                src_ref=src, dst_ref=dst,
                send_sem=sems[0].at[phase, d - 1], recv_sem=sems[1].at[phase, d - 1],
                device_id=peer, device_id_type=MESH,
            )
            copy.start()
            pending.append(copy)
            return copy

        def x_sum(slots):
            total = slots[lax.rem(xi + n_tgt, n_tgt)]
            for k in range(1, n_tgt):
                total = total + slots[lax.rem(xi - k + n_tgt, n_tgt)]
            return total

        def z_sum(slots):
            total = slots[lax.rem(zi + n_cand, n_cand)]
            for k in range(1, n_cand):
                total = total + slots[lax.rem(zi - k + n_cand, n_cand)]
            return total

        def x_start(slots, phase):
            return [
                send(slots.at[0], slots.at[d], xs, phase, d, x_peer(d)) for d in range(1, n_tgt)
            ]

        def z_start(slots, phase):
            return [
                send(slots.at[0], slots.at[d], zs, phase, d, z_peer(d)) for d in range(1, n_cand)
            ]

        def arrive(copies):
            for copy in copies:
                copy.wait_recv()

        for d in range(1, n_tgt):
            for core in range(n_mix):
                row_copy(d, core).wait_recv()
        row_sums = []
        for core in range(n_mix):
            value = row_part[core]
            for d in range(1, n_tgt):
                value = value + row_slots[d, core]
            row_sums.append(value)
        scale_row = 1.0 / jnp.concatenate(row_sums, axis=1)
        place = lax.broadcasted_iota(jnp.int32, (16, rows), 0)
        head = scale_row.astype(BF16).astype(F32)
        lhs = jnp.where(place == 0, head, jnp.where(place == 1, scale_row - head, 0.0)).astype(BF16)
        part_sum = lax.dot_general(lhs, k_one[...], NN_DIMS, preferred_element_type=F32)
        col_slots[0] = part_sum[:1] + part_sum[1:2]
        copies = z_start(col_slots, 0)

        def square(b, carry):
            at = pl.ds(pl.multiple_of(b * 64, 64), 64)
            power = raised[at, :]
            k_two[at, :] = (power * power * (1.0 / tgt_total)).astype(BF16)
            return carry

        lax.fori_loop(0, rows // 64, square, 0)
        for core in range(lead):
            weight_copy(core).wait_recv()
        all_weights = jnp.concatenate(
            [weights[core, :, :mixes] for core in range(lead)] + [weight_ref[...]], axis=1
        )
        all_hot = member_ref[...] == lax.broadcasted_iota(jnp.int32, (tasks, tgt_total), 0)
        counts = jnp.sum(all_hot.astype(F32), axis=1, keepdims=True)
        totals = jnp.sum(all_weights * counts, axis=0, keepdims=True)
        scaled = all_weights * (float(cand_total) / totals)
        own = pl.ds(pl.multiple_of(xi * cols, cols), cols)
        own_hot = (
            member_ref[:, own] == lax.broadcasted_iota(jnp.int32, (tasks, cols), 0)
        ).astype(F32)
        mass[...] = lax.dot_general(
            scaled, own_hot, TN_DIMS, precision=lax.Precision.HIGHEST, preferred_element_type=F32
        )
        arrive(copies)
        col_sum = z_sum(col_slots)

        task_slots[0] = contract_last((own_hot / col_sum).astype(BF16), k_one[...])
        arrive(x_start(task_slots, 0))
        cand_sums[...] = lax.dot_general(
            scaled, x_sum(task_slots), TN_DIMS, precision=lax.Precision.HIGHEST,
            preferred_element_type=F32,
        )

        far = 1 - zi // owners[1]
        near = 1 - far

        def tgt_send(kernel, turn, part):
            lhs = (1.0 / cand_sums[of(part), :]).astype(BF16)
            for o in (far, near):
                rs_send[turn, part, o] = lax.dot_general(
                    lhs, kernel[:, half(o)], NN_DIMS, preferred_element_type=F32
                )
                if o is far:
                    to_owner(turn, part, o).start()
                    continue

                @pl.when(zi != owners[0] + o)
                def _():
                    to_owner(turn, part, o).start()

        def tgt_finish(turn, part, change):
            for o in halves:

                @pl.when(zi == owners[o])
                def _():
                    for z in range(n_cand):
                        if z != owners[o]:
                            owned_from(turn, part, o, z).wait_recv()
                    total = None
                    for z in range(n_cand):
                        own = z == owners[o]
                        value = rs_send[turn, part, o] if own else rs_slots[turn, part, z]
                        total = value if total is None else total + value
                    ag_slots[turn, part, o] = change(mass[of(part), half(o)] / total)
                    for z in takers(turn, part, o):
                        from_owner(turn, part, o, z, core_of(turn, part)).start()

        def gathered(turn, part, o):
            @pl.when(zi != owners[0] + o)
            def _():
                from_owner(turn, part, o, owners[0] + o, lead).wait_recv()

        def drain(turn, part):
            for o in halves:

                @pl.when(zi != owners[o])
                def _():
                    to_owner(turn, part, o).wait_send()

                @pl.when(zi == owners[o])
                def _():
                    for z in takers(turn, part, o):
                        from_owner(turn, part, o, z, core_of(turn, part)).wait_send()

        def cand_send(turn, part):
            total = None
            for o in (near, far):
                gathered(turn, part, o)
                value = contract_last(ag_slots[turn, part, o].astype(BF16), k_two[:, half(o)])
                total = value if total is None else total + value
            cand_slots[turn, part, 0] = total
            return x_start(cand_slots.at[turn, part], 1 + turn * parts + part)

        def cand_finish(copies, turn, part):
            arrive(copies)
            cand_sums[of(part), :] = x_sum(cand_slots.at[turn, part])

        def keep(scale):
            return scale

        for part in each:
            tgt_send(k_one, 0, part)
        changes = (jnp.square,) + (keep,) * (ITERS - 1)
        for turn in range(ITERS):
            for part in each:
                tgt_finish(turn, part, changes[turn])
            summed = [cand_send(turn, part) for part in each]
            for part in each:
                cand_finish(summed[part], turn, part)
                tgt_send(k_two, 1 + turn, part)
        for core in range(lead):
            cand_copy(core).start()
        out_cand[...] = cand_sums[pl.ds(lead * mixes, mixes), :]
        for part in each:
            tgt_finish(ITERS, part, keep)
        for part in parts_of(lead):
            for o in halves:
                gathered(ITERS, part, o)
                out_tgt[row_of(part), half(o)] = ag_slots[ITERS, part, o]
        for turn in range(1 + ITERS):
            for part in each:
                drain(turn, part)
        for core in range(lead):
            cand_copy(core).wait_send()
        for copy in pending:
            copy.wait_send()


def log_kernel(cand_sums, scale_tgt, out_cand, out_tgt):
    out_cand[...] = -jnp.log(cand_sums[...])
    out_tgt[...] = jnp.log(scale_tgt[...])


def fused(candidates, targets, member, mix_weight):
    n_tgt, n_cand, n_mix = lax.axis_size("tgt"), lax.axis_size("cand"), lax.axis_size("mix")
    rows, width = candidates.shape
    cols = targets.shape[0]
    mixes, tasks = mix_weight.shape
    share = cols // 2
    parts = 2 * n_mix if mixes % 16 == 0 else n_mix
    group = mixes * n_mix // parts
    cand_sums, scale_tgt = pl.pallas_call(
        functools.partial(fused_kernel, n_tgt, n_cand, n_mix, parts),
        out_shape=(pltpu.VMEM((mixes, rows), F32), pltpu.VMEM((mixes, cols), F32)),
        in_specs=[pl.BlockSpec(memory_space=pltpu.HBM)] * 2
        + [pl.BlockSpec(memory_space=pltpu.VMEM)] * 2,
        out_specs=(pl.BlockSpec(memory_space=pltpu.VMEM),) * 2,
        scratch_shapes=[
            pltpu.VMEM((rows, width), BF16),
            pltpu.VMEM((cols, width), BF16),
            pltpu.VMEM((cols, width), BF16),
            pltpu.VMEM((rows, cols), F32),
            pltpu.VMEM((rows, cols), BF16),
            pltpu.VMEM((rows, cols), BF16),
            pltpu.VMEM((mixes * n_mix, cols), F32),
            pltpu.VMEM((mixes * n_mix, rows), F32),
            pltpu.VMEM((n_mix, tasks, 128), F32),
            pltpu.VMEM((mixes, rows), F32),
            pltpu.VMEM((n_mix, 1, rows // n_mix), F32),
            pltpu.VMEM((n_tgt, n_mix, 1, rows // n_mix), F32),
            pltpu.VMEM((n_cand, 1, cols), F32),
            pltpu.VMEM((n_tgt, tasks, rows), F32),
            pltpu.VMEM((ITERS, parts, n_tgt, group, rows), F32),
            pltpu.VMEM((1 + ITERS, parts, 2, group, share), F32),
            pltpu.VMEM((1 + ITERS, parts, n_cand, group, share), F32),
            pltpu.VMEM((1 + ITERS, parts, 2, group, share), F32),
            pltpu.SemaphoreType.DMA((2, max(rows, cols) // 256)),
            pltpu.SemaphoreType.DMA((1 + ITERS * parts, n_tgt - 1)),
            pltpu.SemaphoreType.DMA((1 + ITERS * parts, n_tgt - 1)),
            pltpu.SemaphoreType.DMA((1, n_cand - 1)),
            pltpu.SemaphoreType.DMA((1, n_cand - 1)),
            pltpu.SemaphoreType.DMA((n_tgt - 1,)),
            pltpu.SemaphoreType.DMA((n_tgt - 1, n_mix)),
            pltpu.SemaphoreType.DMA((1 + ITERS, parts, 2)),
            pltpu.SemaphoreType.DMA((1 + ITERS, parts, n_cand)),
            pltpu.SemaphoreType.DMA((1 + ITERS, parts, n_cand)),
            pltpu.SemaphoreType.DMA((1 + ITERS, parts, 2)),
            pltpu.SemaphoreType.DMA((2, n_mix)),
            pltpu.SemaphoreType.DMA((2, n_mix)),
        ],
        compiler_params=pltpu.CompilerParams(
            collective_id=0, has_side_effects=True, vmem_limit_bytes=56 * 1024 * 1024
        ),
    )(candidates, targets, member.reshape(1, -1), mix_weight.T)
    return tuple(pl.pallas_call(
        log_kernel,
        out_shape=(
            jax.ShapeDtypeStruct((mixes, rows), F32),
            jax.ShapeDtypeStruct((mixes, cols), F32),
        ),
        in_specs=[pl.BlockSpec(memory_space=pltpu.VMEM)] * 2,
        out_specs=(pl.BlockSpec(memory_space=pltpu.VMEM),) * 2,
    )(*(pltpu.with_memory_space_constraint(x, pltpu.VMEM) for x in (cand_sums, scale_tgt))))


def target_mass(own_member, member, mix_weight, cand_total):
    task_ids = jnp.arange(mix_weight.shape[1], dtype=jnp.int32)
    counts = jnp.sum((member[None, :] == task_ids[:, None]).astype(jnp.float32), axis=1)
    weight_total = jnp.dot(mix_weight, counts, precision=lax.Precision.HIGHEST)
    onehot = (own_member[None, :] == task_ids[:, None]).astype(jnp.float32)
    per_target = jnp.dot(mix_weight, onehot, precision=lax.Precision.HIGHEST)
    return per_target * (cand_total / weight_total)[:, None]


def by_collectives(candidates, targets, member, mix_weight):
    cand_rows = candidates.shape[0]
    tgt_rows = targets.shape[0]
    tgt_total = tgt_rows * lax.axis_size("tgt")
    cand_total = cand_rows * lax.axis_size("cand")
    tgt_unit = unit_rows(targets)
    scores = contract_last(unit_rows(candidates), tgt_unit)
    own_member = lax.dynamic_slice_in_dim(member, lax.axis_index("tgt") * tgt_rows, tgt_rows, 0)
    mass = target_mass(own_member, member, mix_weight, float(cand_total))
    kernel_one = jnp.exp(scores / EPS_FIRST) / tgt_total
    kernel_two = jnp.exp(scores / EPS_SECOND) / tgt_total
    scale_tgt = jnp.ones((mix_weight.shape[0], tgt_rows), jnp.float32)
    scale_cand = jnp.ones((mix_weight.shape[0], cand_rows), jnp.float32)
    for section_index, kernel in enumerate((kernel_one, kernel_two)):
        if section_index == 1:
            scale_tgt = scale_tgt * scale_tgt
        for repeat in range(ITERS):
            partial_value = lax.dot_general(
                scale_tgt, kernel, (((1,), (1,)), ((), ())), precision=lax.Precision.HIGHEST
            )
            scale_cand = 1.0 / lax.psum(partial_value, "tgt")
            column_part = jnp.dot(scale_cand, kernel, precision=lax.Precision.HIGHEST)
            share_cols = tgt_rows // lax.axis_size("cand")
            summed = lax.psum_scatter(column_part, "cand", scatter_dimension=1, tiled=True)
            own_mass = lax.dynamic_slice_in_dim(
                mass, lax.axis_index("cand") * share_cols, share_cols, 1
            )
            scale_tgt = lax.all_gather(own_mass / summed, "cand", axis=1, tiled=True)
    return (jnp.log(scale_cand), jnp.log(scale_tgt))


def solution(mesh):
    in_specs = (
        P(("groups", "cand"), None),
        P(("groups", "tgt"), None),
        P("groups"),
        P("mix", "groups"),
    )
    out_specs = (P("mix", ("groups", "cand")), P("mix", ("groups", "tgt")))
    n_tgt, n_cand, n_mix = mesh.shape["tgt"], mesh.shape["cand"], mesh.shape["mix"]

    def local(candidates, targets, member, mix_weight):
        lanes = targets.shape[0] % (128 * n_cand) == 0 and candidates.shape[0] % 512 == 0
        paired = n_cand % 2 == 0 and n_tgt > 1 and n_mix == 2
        step = fused if lanes and paired else by_collectives
        return step(candidates, targets, member, mix_weight)

    return jax.shard_map(local, mesh=mesh, in_specs=in_specs, out_specs=out_specs, check_vma=False)
```

```python
import functools
import math

import jax
import jax.numpy as jnp
from jax import lax
from jax.experimental import pallas as pl
from jax.experimental.pallas import tpu as pltpu
from jax.sharding import PartitionSpec as P

ITERS = 2


EPS_FIRST = 0.05
EPS_SECOND = 0.025

MESH = pl.DeviceIdType.MESH
F32 = jnp.float32
BF16 = jnp.bfloat16
NT_DIMS = (((1,), (1,)), ((), ()))
TN_DIMS = (((0,), (0,)), ((), ()))
NN_DIMS = (((1,), (0,)), ((), ()))


def unit_rows(embedding):
    values = embedding.astype(jnp.float32)
    mean_sq = jnp.mean(values * values, axis=1, keepdims=True)
    return (values * (lax.rsqrt(mean_sq + 1e-06) * (1.0 / math.sqrt(values.shape[1])))).astype(
        jnp.bfloat16
    )


def contract_last(left, right):
    return lax.dot_general(left, right, NT_DIMS, preferred_element_type=jnp.float32)


def fused_kernel(
    n_tgt, n_cand, n_mix, parts, cand_hbm, tgt_hbm, member_hbm, weight_hbm, out_cand, out_tgt,
    cand_rows, tgt_rows, cand_unit, tgt_unit, raised_t, k_one_t, k_one, k_two_t, k_two,
    mass, cand_sums, member_ref, weight_ref, weights, cand_in,
    row_part, row_slots, col_slots, task_slots, cand_slots, rs_send, rs_slots, ag_slots,
    load_sems, small_sems, x_send, x_recv, z_send, z_recv, row_out, row_in, rs_out, rs_in, ag_out, ag_in,
    chip_out, chip_in,
):
    xi, zi, ci = lax.axis_index("tgt"), lax.axis_index("cand"), lax.axis_index("mix")
    rows, width = cand_hbm.shape
    cols = tgt_hbm.shape[0]
    tasks, mixes = weight_hbm.shape
    lead = n_mix - 1
    owners = (n_cand // 2 - 1, n_cand // 2)
    share = cols // len(owners)
    group = mixes * n_mix // parts
    tgt_total, cand_total = cols * n_tgt, rows * n_cand
    block = 256
    early = rows // n_mix

    def load(src, dst, row, at):
        at = at if isinstance(at, int) else pl.multiple_of(at, block)
        return pltpu.make_async_copy(
            src.at[pl.ds(at, block)], dst.at[pl.ds(at, block)], load_sems.at[row, at // block]
        )

    def cand_loads(core):
        return [load(cand_hbm, cand_rows, 1, core * early + at) for at in range(0, early, block)]

    tgt_loads = [load(tgt_hbm, tgt_rows, 0, at) for at in range(0, cols, block)]
    small_loads = [
        pltpu.make_async_copy(member_hbm, member_ref, small_sems.at[0]),
        pltpu.make_async_copy(weight_hbm, weight_ref, small_sems.at[1]),
    ]
    for copy in cand_loads(ci) + tgt_loads + small_loads:
        copy.start()

    def x_peer(d):
        return {"tgt": lax.rem(xi + d, n_tgt), "mix": lead}

    def z_peer(d):
        return {"cand": lax.rem(zi + d, n_cand), "mix": lead}

    barrier = pltpu.get_barrier_semaphore()

    def hello(**peer):
        pl.semaphore_signal(barrier, inc=1, device_id=peer, device_id_type=MESH)

    for d in range(1, n_cand):
        hello(**z_peer(d))

    @pl.when(ci == lead)
    def _():
        for core in range(lead):
            for copy in cand_loads(core):
                copy.start()
            hello(mix=core)
        for d in range(1, n_tgt):
            for core in range(n_mix):
                hello(tgt=lax.rem(xi + d, n_tgt), mix=core)

    @pl.when(ci != lead)
    def _():
        hello(mix=lead)

    def cand_ready(first):
        for at in range(0, early, block):
            at = pl.ds(pl.multiple_of(first + at, block), block)
            cand_unit[at, :] = unit_rows(cand_rows[at, :])

    def tgt_ready(index):
        tgt_loads[index].wait()
        at = pl.ds(index * block, block)
        tgt_unit[at, :] = unit_rows(tgt_rows[at, :])

    def tile(index, first):
        at = pl.ds(index * block, block)
        across = pl.ds(pl.multiple_of(first, early), early)
        power = jnp.exp(contract_last(tgt_unit[at, :], cand_unit[across, :]) * (1.0 / EPS_FIRST))
        raised_t[at, across] = power
        k_one_t[at, across] = (power * (1.0 / tgt_total)).astype(BF16)
        return jnp.sum(power, axis=0, keepdims=True) * (1.0 / tgt_total)

    for copy in cand_loads(ci):
        copy.wait()
    cand_ready(ci * early)
    tgt_ready(0)
    sums = []
    for index in range(1, cols // block):
        tgt_ready(index)
        sums.append(tile(index - 1, ci * early))
    sums.append(tile(cols // block - 1, ci * early))
    row_part[ci] = functools.reduce(jnp.add, sums)
    for copy in small_loads:
        copy.wait()

    def row_copy(d, core):
        return pltpu.make_async_remote_copy(
            src_ref=row_part.at[core], dst_ref=row_slots.at[d, core],
            send_sem=row_out.at[d - 1], recv_sem=row_in.at[d - 1, core],
            device_id=x_peer(d), device_id_type=MESH,
        )

    def weight_copy(core):
        return pltpu.make_async_remote_copy(
            src_ref=weights.at[core], dst_ref=weights.at[core],
            send_sem=chip_out.at[0, core], recv_sem=chip_in.at[0, core],
            device_id={"mix": lead}, device_id_type=MESH,
        )

    def cand_copy(core):
        return pltpu.make_async_remote_copy(
            src_ref=cand_sums.at[pl.ds(core * mixes, mixes)], dst_ref=cand_in,
            send_sem=chip_out.at[1, core], recv_sem=chip_in.at[1, core],
            device_id={"mix": core}, device_id_type=MESH,
        )

    def of(part):
        return pl.ds(part * group, group)

    def half(o):
        return pl.ds(o * share if isinstance(o, int) else pl.multiple_of(o * share, share), share)

    def to_owner(turn, part, o):
        return pltpu.make_async_remote_copy(
            src_ref=rs_send.at[turn, part, o], dst_ref=rs_slots.at[turn, part, zi],
            send_sem=rs_out.at[turn, part, o], recv_sem=rs_in.at[turn, part, zi],
            device_id={"cand": owners[0] + o, "mix": lead}, device_id_type=MESH,
        )

    def owned_from(turn, part, o, source):
        return pltpu.make_async_remote_copy(
            src_ref=rs_send.at[turn, part, o], dst_ref=rs_slots.at[turn, part, source],
            send_sem=rs_out.at[turn, part, o], recv_sem=rs_in.at[turn, part, source],
            device_id={"cand": source, "mix": lead}, device_id_type=MESH,
        )

    def from_owner(turn, part, o, peer, core):
        return pltpu.make_async_remote_copy(
            src_ref=ag_slots.at[turn, part, o], dst_ref=ag_slots.at[turn, part, o],
            send_sem=ag_out.at[turn, part, peer], recv_sem=ag_in.at[turn, part, o],
            device_id={"cand": peer, "mix": core}, device_id_type=MESH,
        )

    def core_of(turn, part):
        return part * n_mix // parts if turn == ITERS else lead

    def takers(turn, part, o):
        away = core_of(turn, part) != lead
        return [z for z in range(n_cand) if away or z != owners[o]]

    def parts_of(core):
        return [part for part in range(parts) if core_of(ITERS, part) == core]

    def row_of(part):
        return pl.ds(part * group % mixes, group)

    halves = range(len(owners))
    each = range(parts)

    @pl.when(ci != lead)
    def _():
        weights[ci] = jnp.zeros(weights.shape[1:], F32)
        weights[ci, :, pl.ds(0, mixes)] = weight_ref[...]
        pl.semaphore_wait(barrier, n_tgt)
        sent = [row_copy(d, ci) for d in range(1, n_tgt)] + [weight_copy(ci)]
        for copy in sent:
            copy.start()
        cand_copy(ci).wait_recv()
        out_cand[...] = -jnp.log(cand_in[...])
        for core in range(lead):

            @pl.when(ci == core)
            def _():
                for part in parts_of(core):
                    for o in halves:
                        from_owner(ITERS, part, o, owners[o], lead).wait_recv()
                        out_tgt[row_of(part), half(o)] = ag_slots[ITERS, part, o]
        for copy in sent:
            copy.wait_send()

    @pl.when(ci == lead)
    def _():
        pl.semaphore_wait(barrier, n_tgt - 1 + n_mix * (n_cand - 1) + lead)
        pending = [row_copy(d, lead) for d in range(1, n_tgt)]
        for copy in pending:
            copy.start()
        for core in range(lead):
            for copy in cand_loads(core):
                copy.wait()
            cand_ready(core * early)
            row_part[core] = functools.reduce(
                jnp.add, [tile(index, core * early) for index in range(cols // block)]
            )
        k_one[...] = k_one_t[...].T

        xs, zs = (x_send, x_recv), (z_send, z_recv)

        def send(src, dst, sems, phase, d, peer):
            copy = pltpu.make_async_remote_copy(
                src_ref=src, dst_ref=dst,
                send_sem=sems[0].at[phase, d - 1], recv_sem=sems[1].at[phase, d - 1],
                device_id=peer, device_id_type=MESH,
            )
            copy.start()
            pending.append(copy)
            return copy

        def x_sum(slots):
            total = slots[lax.rem(xi + n_tgt, n_tgt)]
            for k in range(1, n_tgt):
                total = total + slots[lax.rem(xi - k + n_tgt, n_tgt)]
            return total

        def z_sum(slots):
            total = slots[lax.rem(zi + n_cand, n_cand)]
            for k in range(1, n_cand):
                total = total + slots[lax.rem(zi - k + n_cand, n_cand)]
            return total

        def x_start(slots, phase):
            return [
                send(slots.at[0], slots.at[d], xs, phase, d, x_peer(d)) for d in range(1, n_tgt)
            ]

        def z_start(slots, phase):
            return [
                send(slots.at[0], slots.at[d], zs, phase, d, z_peer(d)) for d in range(1, n_cand)
            ]

        def arrive(copies):
            for copy in copies:
                copy.wait_recv()

        for d in range(1, n_tgt):
            for core in range(n_mix):
                row_copy(d, core).wait_recv()
        row_sums = []
        for core in range(n_mix):
            value = row_part[core]
            for d in range(1, n_tgt):
                value = value + row_slots[d, core]
            row_sums.append(value)
        scale_row = 1.0 / jnp.concatenate(row_sums, axis=1)
        place = lax.broadcasted_iota(jnp.int32, (16, rows), 0)
        head = scale_row.astype(BF16).astype(F32)
        lhs = jnp.where(place == 0, head, jnp.where(place == 1, scale_row - head, 0.0)).astype(BF16)
        part_sum = lax.dot_general(lhs, k_one[...], NN_DIMS, preferred_element_type=F32)
        col_slots[0] = part_sum[:1] + part_sum[1:2]
        copies = z_start(col_slots, 0)

        for at in range(0, cols, 64):
            power = raised_t[pl.ds(at, 64), :]
            k_two_t[pl.ds(at, 64), :] = (power * power * (1.0 / tgt_total)).astype(BF16)
        k_two[...] = k_two_t[...].T
        for core in range(lead):
            weight_copy(core).wait_recv()
        all_weights = jnp.concatenate(
            [weights[core, :, :mixes] for core in range(lead)] + [weight_ref[...]], axis=1
        )
        all_hot = member_ref[...] == lax.broadcasted_iota(jnp.int32, (tasks, tgt_total), 0)
        counts = jnp.sum(all_hot.astype(F32), axis=1, keepdims=True)
        totals = jnp.sum(all_weights * counts, axis=0, keepdims=True)
        scaled = all_weights * (float(cand_total) / totals)
        own = pl.ds(pl.multiple_of(xi * cols, cols), cols)
        own_hot = (
            member_ref[:, own] == lax.broadcasted_iota(jnp.int32, (tasks, cols), 0)
        ).astype(F32)
        mass[...] = lax.dot_general(
            scaled, own_hot, TN_DIMS, precision=lax.Precision.HIGHEST, preferred_element_type=F32
        )
        arrive(copies)
        col_sum = z_sum(col_slots)

        task_slots[0] = lax.dot_general(
            (own_hot / col_sum).astype(BF16), k_one_t[...], NN_DIMS, preferred_element_type=F32
        )
        arrive(x_start(task_slots, 0))
        cand_sums[...] = lax.dot_general(
            scaled, x_sum(task_slots), TN_DIMS, precision=lax.Precision.HIGHEST,
            preferred_element_type=F32,
        )

        far = 1 - zi // owners[1]
        near = 1 - far

        def tgt_send(kernel, turn, part):
            lhs = (1.0 / cand_sums[of(part), :]).astype(BF16)
            for o in (far, near):
                rs_send[turn, part, o] = lax.dot_general(
                    lhs, kernel[:, half(o)], NN_DIMS, preferred_element_type=F32
                )
                if o is far:
                    to_owner(turn, part, o).start()
                    continue

                @pl.when(zi != owners[0] + o)
                def _():
                    to_owner(turn, part, o).start()

        def tgt_finish(turn, part, change):
            for o in halves:

                @pl.when(zi == owners[o])
                def _():
                    for z in range(n_cand):
                        if z != owners[o]:
                            owned_from(turn, part, o, z).wait_recv()
                    total = None
                    for z in range(n_cand):
                        own = z == owners[o]
                        value = rs_send[turn, part, o] if own else rs_slots[turn, part, z]
                        total = value if total is None else total + value
                    ag_slots[turn, part, o] = change(mass[of(part), half(o)] / total)
                    for z in takers(turn, part, o):
                        from_owner(turn, part, o, z, core_of(turn, part)).start()

        def gathered(turn, part, o):
            @pl.when(zi != owners[0] + o)
            def _():
                from_owner(turn, part, o, owners[0] + o, lead).wait_recv()

        def drain(turn, part):
            for o in halves:

                @pl.when(zi != owners[o])
                def _():
                    to_owner(turn, part, o).wait_send()

                @pl.when(zi == owners[o])
                def _():
                    for z in takers(turn, part, o):
                        from_owner(turn, part, o, z, core_of(turn, part)).wait_send()

        def cand_send(turn, part):
            total = None
            for o in (near, far):
                gathered(turn, part, o)
                value = lax.dot_general(
                    ag_slots[turn, part, o].astype(BF16), k_two_t[half(o), :], NN_DIMS,
                    preferred_element_type=F32,
                )
                total = value if total is None else total + value
            cand_slots[turn, part, 0] = total
            return x_start(cand_slots.at[turn, part], 1 + turn * parts + part)

        def cand_finish(copies, turn, part):
            arrive(copies)
            cand_sums[of(part), :] = x_sum(cand_slots.at[turn, part])

        def keep(scale):
            return scale

        for part in each:
            tgt_send(k_one, 0, part)
        changes = (jnp.square,) + (keep,) * (ITERS - 1)
        for turn in range(ITERS):
            for part in each:
                tgt_finish(turn, part, changes[turn])
            summed = [cand_send(turn, part) for part in each]
            for part in each:
                cand_finish(summed[part], turn, part)
                tgt_send(k_two, 1 + turn, part)
        for core in range(lead):
            cand_copy(core).start()
        out_cand[...] = -jnp.log(cand_sums[pl.ds(lead * mixes, mixes), :])
        for part in each:
            tgt_finish(ITERS, part, jnp.log)
        for part in parts_of(lead):
            for o in halves:
                gathered(ITERS, part, o)
                out_tgt[row_of(part), half(o)] = ag_slots[ITERS, part, o]
        for turn in range(1 + ITERS):
            for part in each:
                drain(turn, part)
        for core in range(lead):
            cand_copy(core).wait_send()
        for copy in pending:
            copy.wait_send()


def write_kernel(cand_log, tgt_log, out_cand, out_tgt, sems):
    copies = [
        pltpu.make_async_copy(cand_log, out_cand, sems.at[0]),
        pltpu.make_async_copy(tgt_log, out_tgt, sems.at[1]),
    ]
    for copy in copies:
        copy.start()
    for copy in copies:
        copy.wait()


def fused(candidates, targets, member, mix_weight):
    n_tgt, n_cand, n_mix = lax.axis_size("tgt"), lax.axis_size("cand"), lax.axis_size("mix")
    rows, width = candidates.shape
    cols = targets.shape[0]
    mixes, tasks = mix_weight.shape
    share = cols // 2
    parts = 2 * n_mix if mixes % 16 == 0 else n_mix
    group = mixes * n_mix // parts
    logs = pl.pallas_call(
        functools.partial(fused_kernel, n_tgt, n_cand, n_mix, parts),
        out_shape=(pltpu.VMEM((mixes, rows), F32), pltpu.VMEM((mixes, cols), F32)),
        in_specs=[pl.BlockSpec(memory_space=pltpu.HBM)] * 4,
        out_specs=(pl.BlockSpec(memory_space=pltpu.VMEM),) * 2,
        scratch_shapes=[
            pltpu.VMEM((rows, width), BF16),
            pltpu.VMEM((cols, width), BF16),
            pltpu.VMEM((rows, width), BF16),
            pltpu.VMEM((cols, width), BF16),
            pltpu.VMEM((cols, rows), F32),
            pltpu.VMEM((cols, rows), BF16),
            pltpu.VMEM((rows, cols), BF16),
            pltpu.VMEM((cols, rows), BF16),
            pltpu.VMEM((rows, cols), BF16),
            pltpu.VMEM((mixes * n_mix, cols), F32),
            pltpu.VMEM((mixes * n_mix, rows), F32),
            pltpu.VMEM((1, cols * n_tgt), jnp.int32),
            pltpu.VMEM((tasks, mixes), F32),
            pltpu.VMEM((n_mix, tasks, 128), F32),
            pltpu.VMEM((mixes, rows), F32),
            pltpu.VMEM((n_mix, 1, rows // n_mix), F32),
            pltpu.VMEM((n_tgt, n_mix, 1, rows // n_mix), F32),
            pltpu.VMEM((n_cand, 1, cols), F32),
            pltpu.VMEM((n_tgt, tasks, rows), F32),
            pltpu.VMEM((ITERS, parts, n_tgt, group, rows), F32),
            pltpu.VMEM((1 + ITERS, parts, 2, group, share), F32),
            pltpu.VMEM((1 + ITERS, parts, n_cand, group, share), F32),
            pltpu.VMEM((1 + ITERS, parts, 2, group, share), F32),
            pltpu.SemaphoreType.DMA((2, max(rows, cols) // 256)),
            pltpu.SemaphoreType.DMA((2,)),
            pltpu.SemaphoreType.DMA((1 + ITERS * parts, n_tgt - 1)),
            pltpu.SemaphoreType.DMA((1 + ITERS * parts, n_tgt - 1)),
            pltpu.SemaphoreType.DMA((1, n_cand - 1)),
            pltpu.SemaphoreType.DMA((1, n_cand - 1)),
            pltpu.SemaphoreType.DMA((n_tgt - 1,)),
            pltpu.SemaphoreType.DMA((n_tgt - 1, n_mix)),
            pltpu.SemaphoreType.DMA((1 + ITERS, parts, 2)),
            pltpu.SemaphoreType.DMA((1 + ITERS, parts, n_cand)),
            pltpu.SemaphoreType.DMA((1 + ITERS, parts, n_cand)),
            pltpu.SemaphoreType.DMA((1 + ITERS, parts, 2)),
            pltpu.SemaphoreType.DMA((2, n_mix)),
            pltpu.SemaphoreType.DMA((2, n_mix)),
        ],
        compiler_params=pltpu.CompilerParams(
            collective_id=0, has_side_effects=True, vmem_limit_bytes=56 * 1024 * 1024
        ),
    )(candidates, targets, member.reshape(1, -1), mix_weight.T)
    return tuple(pl.pallas_call(
        write_kernel,
        out_shape=(
            jax.ShapeDtypeStruct((mixes, rows), F32),
            jax.ShapeDtypeStruct((mixes, cols), F32),
        ),
        in_specs=[pl.BlockSpec(memory_space=pltpu.VMEM)] * 2,
        out_specs=(pl.BlockSpec(memory_space=pltpu.HBM),) * 2,
        scratch_shapes=[pltpu.SemaphoreType.DMA((2,))],
    )(*(pltpu.with_memory_space_constraint(log, pltpu.VMEM) for log in logs)))


def target_mass(own_member, member, mix_weight, cand_total):
    task_ids = jnp.arange(mix_weight.shape[1], dtype=jnp.int32)
    counts = jnp.sum((member[None, :] == task_ids[:, None]).astype(jnp.float32), axis=1)
    weight_total = jnp.dot(mix_weight, counts, precision=lax.Precision.HIGHEST)
    onehot = (own_member[None, :] == task_ids[:, None]).astype(jnp.float32)
    per_target = jnp.dot(mix_weight, onehot, precision=lax.Precision.HIGHEST)
    return per_target * (cand_total / weight_total)[:, None]


def by_collectives(candidates, targets, member, mix_weight):
    cand_rows = candidates.shape[0]
    tgt_rows = targets.shape[0]
    tgt_total = tgt_rows * lax.axis_size("tgt")
    cand_total = cand_rows * lax.axis_size("cand")
    tgt_unit = unit_rows(targets)
    scores = contract_last(unit_rows(candidates), tgt_unit)
    own_member = lax.dynamic_slice_in_dim(member, lax.axis_index("tgt") * tgt_rows, tgt_rows, 0)
    mass = target_mass(own_member, member, mix_weight, float(cand_total))
    kernel_one = jnp.exp(scores / EPS_FIRST) / tgt_total
    kernel_two = jnp.exp(scores / EPS_SECOND) / tgt_total
    scale_tgt = jnp.ones((mix_weight.shape[0], tgt_rows), jnp.float32)
    scale_cand = jnp.ones((mix_weight.shape[0], cand_rows), jnp.float32)
    for section_index, kernel in enumerate((kernel_one, kernel_two)):
        if section_index == 1:
            scale_tgt = scale_tgt * scale_tgt
        for repeat in range(ITERS):
            partial_value = lax.dot_general(
                scale_tgt, kernel, (((1,), (1,)), ((), ())), precision=lax.Precision.HIGHEST
            )
            scale_cand = 1.0 / lax.psum(partial_value, "tgt")
            column_part = jnp.dot(scale_cand, kernel, precision=lax.Precision.HIGHEST)
            share_cols = tgt_rows // lax.axis_size("cand")
            summed = lax.psum_scatter(column_part, "cand", scatter_dimension=1, tiled=True)
            own_mass = lax.dynamic_slice_in_dim(
                mass, lax.axis_index("cand") * share_cols, share_cols, 1
            )
            scale_tgt = lax.all_gather(own_mass / summed, "cand", axis=1, tiled=True)
    return (jnp.log(scale_cand), jnp.log(scale_tgt))


def solution(mesh):
    in_specs = (
        P(("groups", "cand"), None),
        P(("groups", "tgt"), None),
        P("groups"),
        P("mix", "groups"),
    )
    out_specs = (P("mix", ("groups", "cand")), P("mix", ("groups", "tgt")))
    n_tgt, n_cand, n_mix = mesh.shape["tgt"], mesh.shape["cand"], mesh.shape["mix"]

    def local(candidates, targets, member, mix_weight):
        lanes = targets.shape[0] % (128 * n_cand) == 0 and candidates.shape[0] % 512 == 0
        paired = n_cand % 2 == 0 and n_tgt > 1 and n_mix == 2
        step = fused if lanes and paired else by_collectives
        return step(candidates, targets, member, mix_weight)

    return jax.shard_map(local, mesh=mesh, in_specs=in_specs, out_specs=out_specs, check_vma=False)
```

```python
import functools
import math

import jax
import jax.numpy as jnp
from jax import lax
from jax.experimental import pallas as pl
from jax.experimental.pallas import tpu as pltpu
from jax.sharding import PartitionSpec as P

ITERS = 2


EPS_FIRST = 0.05
EPS_SECOND = 0.025

MESH = pl.DeviceIdType.MESH
F32 = jnp.float32
BF16 = jnp.bfloat16
NT_DIMS = (((1,), (1,)), ((), ()))
TN_DIMS = (((0,), (0,)), ((), ()))
NN_DIMS = (((1,), (0,)), ((), ()))


def unit_rows(embedding):
    values = embedding.astype(jnp.float32)
    mean_sq = jnp.mean(values * values, axis=1, keepdims=True)
    return (values * (lax.rsqrt(mean_sq + 1e-06) * (1.0 / math.sqrt(values.shape[1])))).astype(
        jnp.bfloat16
    )


def contract_last(left, right):
    return lax.dot_general(left, right, NT_DIMS, preferred_element_type=jnp.float32)


def fused_kernel(
    n_tgt, n_cand, n_mix, parts, cand_hbm, tgt_hbm, member_hbm, weight_hbm, out_cand, out_tgt,
    cand_rows, tgt_rows, cand_unit, tgt_unit, raised_t, k_one_t, k_one, k_two_t, k_two,
    mass, cand_sums, member_ref, weight_ref, weights, cand_in,
    row_part, row_slots, col_slots, task_slots, cand_slots, rs_send, rs_slots, ag_slots,
    load_sems, x_send, x_recv, z_sems, row_out, row_in, rs_out, rs_in, ag_out, ag_in,
    chip_out, chip_in,
):
    xi, zi, ci = lax.axis_index("tgt"), lax.axis_index("cand"), lax.axis_index("mix")
    rows, width = cand_hbm.shape
    cols = tgt_hbm.shape[0]
    tasks, mixes = weight_hbm.shape
    lead = n_mix - 1
    owners = (n_cand // 2 - 1, n_cand // 2)
    share = cols // len(owners)
    group = mixes * n_mix // parts
    tgt_total, cand_total = cols * n_tgt, rows * n_cand
    block = 256
    early = rows // n_mix

    def load(src, dst, sem, *at):
        if at:
            src, dst = src.at[pl.ds(*at)], dst.at[pl.ds(*at)]
        return pltpu.make_async_copy(src, dst, load_sems.at[sem])

    tgt_parts, cand_parts = cols // block, early // block
    tgt_loads = [load(tgt_hbm, tgt_rows, k, k * block, block) for k in range(tgt_parts)]
    cand_loads = [
        load(cand_hbm, cand_rows, tgt_parts + k,
             pl.multiple_of(ci * early + k * block, block), block)
        for k in range(cand_parts)
    ]
    late_loads = [
        load(cand_hbm, cand_rows, tgt_parts + cand_parts + core, core * early, early)
        for core in range(lead)
    ]
    small_loads = [
        load(src, dst, tgt_parts + cand_parts + lead + k)
        for k, (src, dst) in enumerate(((member_hbm, member_ref), (weight_hbm, weight_ref)))
    ]
    for copy in cand_loads + tgt_loads + small_loads:
        copy.start()

    def x_peer(d):
        return {"tgt": lax.rem(xi + d, n_tgt), "mix": lead}

    def z_peer(d):
        return {"cand": lax.rem(zi + d, n_cand), "mix": lead}

    barrier = pltpu.get_barrier_semaphore()

    def hello(**peer):
        pl.semaphore_signal(barrier, inc=1, device_id=peer, device_id_type=MESH)

    for d in range(1, n_cand):
        hello(**z_peer(d))

    @pl.when(ci == lead)
    def _():
        for core in range(lead):
            late_loads[core].start()
            hello(mix=core)
        for d in range(1, n_tgt):
            for core in range(n_mix):
                hello(tgt=lax.rem(xi + d, n_tgt), mix=core)

    @pl.when(ci != lead)
    def _():
        hello(mix=lead)

    def cand_ready(first):
        for at in range(0, early, block):
            at = pl.ds(pl.multiple_of(first + at, block), block)
            cand_unit[at, :] = unit_rows(cand_rows[at, :])

    def tgt_ready(index):
        tgt_loads[index].wait()
        at = pl.ds(index * block, block)
        tgt_unit[at, :] = unit_rows(tgt_rows[at, :])

    def tile(index, first):
        at = pl.ds(index * block, block)
        across = pl.ds(pl.multiple_of(first, early), early)
        power = jnp.exp(contract_last(tgt_unit[at, :], cand_unit[across, :]) * (1.0 / EPS_FIRST))
        raised_t[at, across] = power
        k_one_t[at, across] = (power * (1.0 / tgt_total)).astype(BF16)
        return jnp.sum(power, axis=0, keepdims=True) * (1.0 / tgt_total)

    for copy in cand_loads:
        copy.wait()
    cand_ready(ci * early)
    tgt_ready(0)
    sums = []
    for index in range(1, tgt_parts):
        tgt_ready(index)
        sums.append(tile(index - 1, ci * early))
    sums.append(tile(tgt_parts - 1, ci * early))
    row_part[ci] = functools.reduce(jnp.add, sums)
    for copy in small_loads:
        copy.wait()

    def row_copy(d, core):
        return pltpu.make_async_remote_copy(
            src_ref=row_part.at[core], dst_ref=row_slots.at[d, core],
            send_sem=row_out.at[d - 1], recv_sem=row_in.at[d - 1, core],
            device_id=x_peer(d), device_id_type=MESH,
        )

    def weight_copy(core):
        return pltpu.make_async_remote_copy(
            src_ref=weights.at[core], dst_ref=weights.at[core],
            send_sem=chip_out.at[0, core], recv_sem=chip_in.at[0, core],
            device_id={"mix": lead}, device_id_type=MESH,
        )

    def cand_copy(core):
        return pltpu.make_async_remote_copy(
            src_ref=cand_sums.at[pl.ds(core * mixes, mixes)], dst_ref=cand_in,
            send_sem=chip_out.at[1, core], recv_sem=chip_in.at[1, core],
            device_id={"mix": core}, device_id_type=MESH,
        )

    def of(part):
        return pl.ds(part * group, group)

    def half(o):
        return pl.ds(o * share if isinstance(o, int) else pl.multiple_of(o * share, share), share)

    def to_owner(turn, part, o):
        return pltpu.make_async_remote_copy(
            src_ref=rs_send.at[turn, part, o], dst_ref=rs_slots.at[turn, part, zi],
            send_sem=rs_out.at[part, o], recv_sem=rs_in.at[part],
            device_id={"cand": owners[0] + o, "mix": lead}, device_id_type=MESH,
        )

    def together(slots, sems):
        return pltpu.make_async_remote_copy(
            src_ref=slots, dst_ref=slots, send_sem=sems[0], recv_sem=sems[1],
            device_id={"tgt": lax.rem(xi + 1, n_tgt), "mix": lead}, device_id_type=MESH,
        )

    def owned_all(turn, part):
        return together(
            rs_slots.at[turn, part, pl.ds(0, n_cand - 1)], (ag_out.at[part], rs_in.at[part])
        )

    def taken_all(turn, part, o):
        return together(
            rs_slots.at[turn, part, pl.ds(0, len(takers(turn, part, o)))],
            (ag_out.at[part], rs_in.at[part]),
        )

    def from_owner(turn, part, o, peer, core):
        return pltpu.make_async_remote_copy(
            src_ref=ag_slots.at[turn, part, o], dst_ref=ag_slots.at[turn, part, o],
            send_sem=ag_out.at[part], recv_sem=ag_in.at[part, o],
            device_id={"cand": peer, "mix": core}, device_id_type=MESH,
        )

    def core_of(turn, part):
        return part * n_mix // parts if turn == ITERS else lead

    def takers(turn, part, o):
        away = core_of(turn, part) != lead
        return [z for z in range(n_cand) if away or z != owners[o]]

    def parts_of(core):
        return [part for part in range(parts) if core_of(ITERS, part) == core]

    def row_of(part):
        return pl.ds(part * group % mixes, group)

    halves = range(len(owners))
    each = range(parts)

    @pl.when(ci != lead)
    def _():
        weights[ci] = jnp.zeros(weights.shape[1:], F32)
        weights[ci, :, pl.ds(0, mixes)] = weight_ref[...]
        pl.semaphore_wait(barrier, n_tgt)
        sent = [row_copy(d, ci) for d in range(1, n_tgt)] + [weight_copy(ci)]
        for copy in sent:
            copy.start()
        cand_copy(ci).wait_recv()
        out_cand[...] = -jnp.log(cand_in[...])
        for core in range(lead):

            @pl.when(ci == core)
            def _():
                for part in parts_of(core):
                    for o in halves:
                        from_owner(ITERS, part, o, owners[o], lead).wait_recv()
                        out_tgt[row_of(part), half(o)] = ag_slots[ITERS, part, o]
        for copy in sent:
            copy.wait_send()

    @pl.when(ci == lead)
    def _():
        pl.semaphore_wait(barrier, n_tgt - 1 + n_mix * (n_cand - 1) + lead)
        pending = [row_copy(d, lead) for d in range(1, n_tgt)]
        for copy in pending:
            copy.start()
        for core in range(lead):
            late_loads[core].wait()
            cand_ready(core * early)
            row_part[core] = functools.reduce(
                jnp.add, [tile(index, core * early) for index in range(tgt_parts)]
            )
        k_one[...] = k_one_t[...].T

        in_flight = {}

        def x_sum(slots):
            total = slots[lax.rem(xi + n_tgt, n_tgt)]
            for k in range(1, n_tgt):
                total = total + slots[lax.rem(xi - k + n_tgt, n_tgt)]
            return total

        def z_sum(slots):
            total = slots[lax.rem(zi + n_cand, n_cand)]
            for k in range(1, n_cand):
                total = total + slots[lax.rem(zi - k + n_cand, n_cand)]
            return total

        def x_start(slots, lane, turn):
            copies = []
            for d in range(1, n_tgt):
                if (lane, d) in in_flight:
                    in_flight[lane, d].wait_send()
                in_flight[lane, d] = copy = pltpu.make_async_remote_copy(
                    src_ref=slots.at[0], dst_ref=slots.at[d],
                    send_sem=x_send.at[lane, d - 1], recv_sem=x_recv.at[turn % 2, lane, d - 1],
                    device_id=x_peer(d), device_id_type=MESH,
                )
                copy.start()
                copies.append(copy)
            return copies

        def arrive(copies):
            for copy in copies:
                copy.wait_recv()

        for d in range(1, n_tgt):
            for core in range(n_mix):
                row_copy(d, core).wait_recv()
        row_sums = []
        for core in range(n_mix):
            value = row_part[core]
            for d in range(1, n_tgt):
                value = value + row_slots[d, core]
            row_sums.append(value)
        scale_row = 1.0 / jnp.concatenate(row_sums, axis=1)
        place = lax.broadcasted_iota(jnp.int32, (16, rows), 0)
        head = scale_row.astype(BF16).astype(F32)
        lhs = jnp.where(place == 0, head, jnp.where(place == 1, scale_row - head, 0.0)).astype(BF16)
        part_sum = lax.dot_general(lhs, k_one[...], NN_DIMS, preferred_element_type=F32)
        col_slots[0] = part_sum[:1] + part_sum[1:2]
        for d in range(1, n_cand):
            pltpu.make_async_remote_copy(
                src_ref=col_slots.at[0], dst_ref=col_slots.at[d],
                send_sem=z_sems.at[0], recv_sem=z_sems.at[1],
                device_id=z_peer(d), device_id_type=MESH,
            ).start()
        z_all = together(col_slots.at[pl.ds(1, n_cand - 1)], (z_sems.at[0], z_sems.at[1]))

        for at in range(0, cols, 64):
            power = raised_t[pl.ds(at, 64), :]
            k_two_t[pl.ds(at, 64), :] = (power * power * (1.0 / tgt_total)).astype(BF16)
        k_two[...] = k_two_t[...].T
        for core in range(lead):
            weight_copy(core).wait_recv()
        all_weights = jnp.concatenate(
            [weights[core, :, :mixes] for core in range(lead)] + [weight_ref[...]], axis=1
        )
        all_hot = member_ref[...] == lax.broadcasted_iota(jnp.int32, (tasks, tgt_total), 0)
        counts = jnp.sum(all_hot.astype(F32), axis=1, keepdims=True)
        totals = jnp.sum(all_weights * counts, axis=0, keepdims=True)
        scaled = all_weights * (float(cand_total) / totals)
        own = pl.ds(pl.multiple_of(xi * cols, cols), cols)
        own_hot = (
            member_ref[:, own] == lax.broadcasted_iota(jnp.int32, (tasks, cols), 0)
        ).astype(F32)
        mass[...] = lax.dot_general(
            scaled, own_hot, TN_DIMS, precision=lax.Precision.HIGHEST, preferred_element_type=F32
        )
        z_all.wait_recv()
        col_sum = z_sum(col_slots)

        task_slots[0] = lax.dot_general(
            (own_hot / col_sum).astype(BF16), k_one_t[...], NN_DIMS, preferred_element_type=F32
        )
        arrive(x_start(task_slots, 0, 1))
        cand_sums[...] = lax.dot_general(
            scaled, x_sum(task_slots), TN_DIMS, precision=lax.Precision.HIGHEST,
            preferred_element_type=F32,
        )

        far = 1 - zi // owners[1]
        near = 1 - far

        def tgt_send(kernel, turn, part):
            lhs = (1.0 / cand_sums[of(part), :]).astype(BF16)
            for o in (far, near):
                rs_send[turn, part, o] = lax.dot_general(
                    lhs, kernel[:, half(o)], NN_DIMS, preferred_element_type=F32
                )
                if o is far:
                    if turn > 0:
                        to_owner(turn - 1, part, o).wait_send()
                    to_owner(turn, part, o).start()
                    continue

                @pl.when(zi != owners[0] + o)
                def _():
                    if turn > 0:
                        to_owner(turn - 1, part, o).wait_send()
                    to_owner(turn, part, o).start()

        def tgt_finish(turn, part, change):
            for o in halves:

                @pl.when(zi == owners[o])
                def _():
                    owned_all(turn, part).wait_recv()
                    total = None
                    for z in range(n_cand):
                        own = z == owners[o]
                        value = rs_send[turn, part, o] if own else rs_slots[turn, part, z]
                        total = value if total is None else total + value
                    ag_slots[turn, part, o] = change(mass[of(part), half(o)] / total)
                    if turn > 0:
                        taken_all(turn - 1, part, o).wait_send()
                    for z in takers(turn, part, o):
                        from_owner(turn, part, o, z, core_of(turn, part)).start()

        def gathered(turn, part, o):
            @pl.when(zi != owners[0] + o)
            def _():
                from_owner(turn, part, o, owners[0] + o, lead).wait_recv()

        def drain(turn, part):
            for o in halves:

                @pl.when(zi != owners[o])
                def _():
                    to_owner(turn, part, o).wait_send()

                @pl.when(zi == owners[o])
                def _():
                    taken_all(turn, part, o).wait_send()

        def cand_send(turn, part):
            total = None
            for o in (near, far):
                gathered(turn, part, o)
                value = lax.dot_general(
                    ag_slots[turn, part, o].astype(BF16), k_two_t[half(o), :], NN_DIMS,
                    preferred_element_type=F32,
                )
                total = value if total is None else total + value
            cand_slots[turn, part, 0] = total
            return x_start(cand_slots.at[turn, part], part, turn)

        def cand_finish(copies, turn, part):
            arrive(copies)
            cand_sums[of(part), :] = x_sum(cand_slots.at[turn, part])

        def keep(scale):
            return scale

        for part in each:
            tgt_send(k_one, 0, part)
        changes = (jnp.square,) + (keep,) * (ITERS - 1)
        for turn in range(ITERS):
            for part in each:
                tgt_finish(turn, part, changes[turn])
            summed = [cand_send(turn, part) for part in each]
            for part in each:
                cand_finish(summed[part], turn, part)
                tgt_send(k_two, 1 + turn, part)
        for core in range(lead):
            cand_copy(core).start()
        out_cand[...] = -jnp.log(cand_sums[pl.ds(lead * mixes, mixes), :])
        for part in each:
            tgt_finish(ITERS, part, jnp.log)
        for part in parts_of(lead):
            for o in halves:
                gathered(ITERS, part, o)
                out_tgt[row_of(part), half(o)] = ag_slots[ITERS, part, o]
        for part in each:
            drain(ITERS, part)
        for core in range(lead):
            cand_copy(core).wait_send()
        z_all.wait_send()
        for copy in pending + list(in_flight.values()):
            copy.wait_send()


def write_kernel(cand_log, tgt_log, out_cand, out_tgt, sems):
    copies = [
        pltpu.make_async_copy(cand_log, out_cand, sems.at[0]),
        pltpu.make_async_copy(tgt_log, out_tgt, sems.at[1]),
    ]
    for copy in copies:
        copy.start()
    for copy in copies:
        copy.wait()


def fused(candidates, targets, member, mix_weight):
    n_tgt, n_cand, n_mix = lax.axis_size("tgt"), lax.axis_size("cand"), lax.axis_size("mix")
    rows, width = candidates.shape
    cols = targets.shape[0]
    mixes, tasks = mix_weight.shape
    share = cols // 2
    parts = 2 * n_mix if mixes % 16 == 0 else n_mix
    group = mixes * n_mix // parts
    logs = pl.pallas_call(
        functools.partial(fused_kernel, n_tgt, n_cand, n_mix, parts),
        out_shape=(pltpu.VMEM((mixes, rows), F32), pltpu.VMEM((mixes, cols), F32)),
        in_specs=[pl.BlockSpec(memory_space=pltpu.HBM)] * 4,
        out_specs=(pl.BlockSpec(memory_space=pltpu.VMEM),) * 2,
        scratch_shapes=[
            pltpu.VMEM((rows, width), BF16),
            pltpu.VMEM((cols, width), BF16),
            pltpu.VMEM((rows, width), BF16),
            pltpu.VMEM((cols, width), BF16),
            pltpu.VMEM((cols, rows), F32),
            pltpu.VMEM((cols, rows), BF16),
            pltpu.VMEM((rows, cols), BF16),
            pltpu.VMEM((cols, rows), BF16),
            pltpu.VMEM((rows, cols), BF16),
            pltpu.VMEM((mixes * n_mix, cols), F32),
            pltpu.VMEM((mixes * n_mix, rows), F32),
            pltpu.VMEM((1, cols * n_tgt), jnp.int32),
            pltpu.VMEM((tasks, mixes), F32),
            pltpu.VMEM((n_mix, tasks, 128), F32),
            pltpu.VMEM((mixes, rows), F32),
            pltpu.VMEM((n_mix, 1, rows // n_mix), F32),
            pltpu.VMEM((n_tgt, n_mix, 1, rows // n_mix), F32),
            pltpu.VMEM((n_cand, 1, cols), F32),
            pltpu.VMEM((n_tgt, tasks, rows), F32),
            pltpu.VMEM((ITERS, parts, n_tgt, group, rows), F32),
            pltpu.VMEM((1 + ITERS, parts, 2, group, share), F32),
            pltpu.VMEM((1 + ITERS, parts, n_cand, group, share), F32),
            pltpu.VMEM((1 + ITERS, parts, 2, group, share), F32),
            pltpu.SemaphoreType.DMA((cols // 256 + rows // n_mix // 256 + n_mix + 1,)),
            pltpu.SemaphoreType.DMA((parts, n_tgt - 1)),
            pltpu.SemaphoreType.DMA((2, parts, n_tgt - 1)),
            pltpu.SemaphoreType.DMA((2,)),
            pltpu.SemaphoreType.DMA((n_tgt - 1,)),
            pltpu.SemaphoreType.DMA((n_tgt - 1, n_mix)),
            pltpu.SemaphoreType.DMA((parts, 2)),
            pltpu.SemaphoreType.DMA((parts,)),
            pltpu.SemaphoreType.DMA((parts,)),
            pltpu.SemaphoreType.DMA((parts, 2)),
            pltpu.SemaphoreType.DMA((2, n_mix - 1)),
            pltpu.SemaphoreType.DMA((2, n_mix - 1)),
        ],
        compiler_params=pltpu.CompilerParams(
            collective_id=0, has_side_effects=True, vmem_limit_bytes=56 * 1024 * 1024
        ),
    )(candidates, targets, member.reshape(1, -1), mix_weight.T)
    return tuple(pl.pallas_call(
        write_kernel,
        out_shape=(
            jax.ShapeDtypeStruct((mixes, rows), F32),
            jax.ShapeDtypeStruct((mixes, cols), F32),
        ),
        in_specs=[pl.BlockSpec(memory_space=pltpu.VMEM)] * 2,
        out_specs=(pl.BlockSpec(memory_space=pltpu.HBM),) * 2,
        scratch_shapes=[pltpu.SemaphoreType.DMA((2,))],
    )(*(pltpu.with_memory_space_constraint(log, pltpu.VMEM) for log in logs)))


def target_mass(own_member, member, mix_weight, cand_total):
    task_ids = jnp.arange(mix_weight.shape[1], dtype=jnp.int32)
    counts = jnp.sum((member[None, :] == task_ids[:, None]).astype(jnp.float32), axis=1)
    weight_total = jnp.dot(mix_weight, counts, precision=lax.Precision.HIGHEST)
    onehot = (own_member[None, :] == task_ids[:, None]).astype(jnp.float32)
    per_target = jnp.dot(mix_weight, onehot, precision=lax.Precision.HIGHEST)
    return per_target * (cand_total / weight_total)[:, None]


def by_collectives(candidates, targets, member, mix_weight):
    cand_rows = candidates.shape[0]
    tgt_rows = targets.shape[0]
    tgt_total = tgt_rows * lax.axis_size("tgt")
    cand_total = cand_rows * lax.axis_size("cand")
    tgt_unit = unit_rows(targets)
    scores = contract_last(unit_rows(candidates), tgt_unit)
    own_member = lax.dynamic_slice_in_dim(member, lax.axis_index("tgt") * tgt_rows, tgt_rows, 0)
    mass = target_mass(own_member, member, mix_weight, float(cand_total))
    kernel_one = jnp.exp(scores / EPS_FIRST) / tgt_total
    kernel_two = jnp.exp(scores / EPS_SECOND) / tgt_total
    scale_tgt = jnp.ones((mix_weight.shape[0], tgt_rows), jnp.float32)
    scale_cand = jnp.ones((mix_weight.shape[0], cand_rows), jnp.float32)
    for section_index, kernel in enumerate((kernel_one, kernel_two)):
        if section_index == 1:
            scale_tgt = scale_tgt * scale_tgt
        for repeat in range(ITERS):
            partial_value = lax.dot_general(
                scale_tgt, kernel, (((1,), (1,)), ((), ())), precision=lax.Precision.HIGHEST
            )
            scale_cand = 1.0 / lax.psum(partial_value, "tgt")
            column_part = jnp.dot(scale_cand, kernel, precision=lax.Precision.HIGHEST)
            share_cols = tgt_rows // lax.axis_size("cand")
            summed = lax.psum_scatter(column_part, "cand", scatter_dimension=1, tiled=True)
            own_mass = lax.dynamic_slice_in_dim(
                mass, lax.axis_index("cand") * share_cols, share_cols, 1
            )
            scale_tgt = lax.all_gather(own_mass / summed, "cand", axis=1, tiled=True)
    return (jnp.log(scale_cand), jnp.log(scale_tgt))


def solution(mesh):
    in_specs = (
        P(("groups", "cand"), None),
        P(("groups", "tgt"), None),
        P("groups"),
        P("mix", "groups"),
    )
    out_specs = (P("mix", ("groups", "cand")), P("mix", ("groups", "tgt")))
    n_tgt, n_cand, n_mix = mesh.shape["tgt"], mesh.shape["cand"], mesh.shape["mix"]

    def local(candidates, targets, member, mix_weight):
        lanes = targets.shape[0] % (128 * n_cand) == 0 and candidates.shape[0] % 512 == 0
        paired = n_cand % 2 == 0 and n_tgt > 1 and n_mix == 2
        step = fused if lanes and paired else by_collectives
        return step(candidates, targets, member, mix_weight)

    return jax.shard_map(local, mesh=mesh, in_specs=in_specs, out_specs=out_specs, check_vma=False)
```

```python
import functools
import math

import jax
import jax.numpy as jnp
from jax import lax
from jax.experimental import pallas as pl
from jax.experimental.pallas import tpu as pltpu
from jax.sharding import PartitionSpec as P

ITERS = 2


EPS_FIRST = 0.05
EPS_SECOND = 0.025

MESH = pl.DeviceIdType.MESH
F32 = jnp.float32
BF16 = jnp.bfloat16
NT_DIMS = (((1,), (1,)), ((), ()))
TN_DIMS = (((0,), (0,)), ((), ()))
NN_DIMS = (((1,), (0,)), ((), ()))


def unit_rows(embedding):
    values = embedding.astype(jnp.float32)
    mean_sq = jnp.mean(values * values, axis=1, keepdims=True)
    return (values * (lax.rsqrt(mean_sq + 1e-06) * (1.0 / math.sqrt(values.shape[1])))).astype(
        jnp.bfloat16
    )


def contract_last(left, right):
    return lax.dot_general(left, right, NT_DIMS, preferred_element_type=jnp.float32)


def fused_kernel(
    n_tgt, n_cand, n_mix, parts, cand_hbm, tgt_hbm, member_hbm, weight_hbm, out_cand, out_tgt,
    cand_rows, tgt_rows, cand_unit, tgt_unit, raised_t, k_one_t, k_one, k_two_t, k_two,
    mass, cand_sums, task_all, member_ref, weight_ref, weights, cand_in,
    row_part, row_slots, col_slots, task_slots, cand_slots, rs_send, rs_slots, ag_slots,
    load_sems, x_recv, z_sems, row_out, row_in, rs_in, ag_in,
    chip_out, chip_in,
):
    xi, zi, ci = lax.axis_index("tgt"), lax.axis_index("cand"), lax.axis_index("mix")
    rows, width = cand_hbm.shape
    cols = tgt_hbm.shape[0]
    tasks, mixes = weight_hbm.shape
    lead = n_mix - 1
    owners = (n_cand // 2 - 1, n_cand // 2)
    x_send, rs_out, ag_out = ([load_sems.at[k * parts + p] for p in range(parts)] for k in range(3))
    share = cols // len(owners)
    subs = 2
    piece, strip = share // subs, rows // subs
    group = mixes * n_mix // parts
    tgt_total, cand_total = cols * n_tgt, rows * n_cand
    block = 256
    early = rows // n_mix

    def load(src, dst, sem, *at):
        if at:
            src, dst = src.at[pl.ds(*at)], dst.at[pl.ds(*at)]
        return pltpu.make_async_copy(src, dst, load_sems.at[sem])

    tgt_parts, cand_parts = cols // block, early // block
    tgt_loads = [load(tgt_hbm, tgt_rows, k, k * block, block) for k in range(tgt_parts)]
    cand_loads = [
        load(cand_hbm, cand_rows, tgt_parts + k,
             pl.multiple_of(ci * early + k * block, block), block)
        for k in range(cand_parts)
    ]
    late_loads = [
        load(cand_hbm, cand_rows, tgt_parts + cand_parts + core, core * early, early)
        for core in range(lead)
    ]
    small_loads = [
        load(src, dst, tgt_parts + cand_parts + lead + k)
        for k, (src, dst) in enumerate(((member_hbm, member_ref), (weight_hbm, weight_ref)))
    ]
    for copy in cand_loads + tgt_loads + small_loads:
        copy.start()

    def x_peer(d):
        return {"tgt": lax.rem(xi + d, n_tgt), "mix": lead}

    def z_peer(d):
        return {"cand": lax.rem(zi + d, n_cand), "mix": lead}

    barrier = pltpu.get_barrier_semaphore()

    def hello(**peer):
        pl.semaphore_signal(barrier, inc=1, device_id=peer, device_id_type=MESH)

    for d in range(1, n_cand):
        hello(**z_peer(d))

    @pl.when(ci == lead)
    def _():
        for core in range(lead):
            late_loads[core].start()
            hello(mix=core)
        for d in range(1, n_tgt):
            for core in range(n_mix):
                hello(tgt=lax.rem(xi + d, n_tgt), mix=core)

    @pl.when(ci != lead)
    def _():
        hello(mix=lead)

    def cand_ready(first):
        for at in range(0, early, block):
            at = pl.ds(pl.multiple_of(first + at, block), block)
            cand_unit[at, :] = unit_rows(cand_rows[at, :])

    def tgt_ready(index):
        tgt_loads[index].wait()
        at = pl.ds(index * block, block)
        tgt_unit[at, :] = unit_rows(tgt_rows[at, :])

    def tile(index, first):
        at = pl.ds(index * block, block)
        across = pl.ds(pl.multiple_of(first, early), early)
        power = jnp.exp(contract_last(tgt_unit[at, :], cand_unit[across, :]) * (1.0 / EPS_FIRST))
        raised_t[at, across] = power
        k_one_t[at, across] = (power * (1.0 / tgt_total)).astype(BF16)
        return jnp.sum(power, axis=0, keepdims=True) * (1.0 / tgt_total)

    for copy in cand_loads:
        copy.wait()
    cand_ready(ci * early)
    tgt_ready(0)
    sums = []
    for index in range(1, tgt_parts):
        tgt_ready(index)
        sums.append(tile(index - 1, ci * early))
    sums.append(tile(tgt_parts - 1, ci * early))
    row_part[ci] = functools.reduce(jnp.add, sums)
    for copy in small_loads:
        copy.wait()

    def row_copy(d, core):
        return pltpu.make_async_remote_copy(
            src_ref=row_part.at[core], dst_ref=row_slots.at[d, core],
            send_sem=row_out.at[d - 1], recv_sem=row_in.at[d - 1, core],
            device_id=x_peer(d), device_id_type=MESH,
        )

    def weight_copy(core):
        return pltpu.make_async_remote_copy(
            src_ref=weights.at[core], dst_ref=weights.at[core],
            send_sem=chip_out.at[0, core], recv_sem=chip_in.at[0, core],
            device_id={"mix": lead}, device_id_type=MESH,
        )

    def cand_copy(core):
        return pltpu.make_async_remote_copy(
            src_ref=cand_sums.at[pl.ds(core * mixes, mixes)], dst_ref=cand_in,
            send_sem=chip_out.at[1, core], recv_sem=chip_in.at[1, core],
            device_id={"mix": core}, device_id_type=MESH,
        )

    def of(part):
        return pl.ds(part * group, group)

    def half(o):
        return pl.ds(o * share if isinstance(o, int) else pl.multiple_of(o * share, share), share)

    def span(o, s):
        at = o * share + s * piece
        return pl.ds(at if isinstance(at, int) else pl.multiple_of(at, piece), piece)

    def to_owner(turn, part, o, s):
        owner = owners[0] + o
        return pltpu.make_async_remote_copy(
            src_ref=rs_send.at[turn, part, o, s],
            dst_ref=rs_slots.at[turn, part, s, lax.rem(zi - owner + n_cand, n_cand) - 1],
            send_sem=rs_out[part], recv_sem=rs_in.at[part, s],
            device_id={"cand": owner, "mix": lead}, device_id_type=MESH,
        )

    def together(slots, sems):
        return pltpu.make_async_remote_copy(
            src_ref=slots, dst_ref=slots, send_sem=sems[0], recv_sem=sems[1],
            device_id={"tgt": lax.rem(xi + 1, n_tgt), "mix": lead}, device_id_type=MESH,
        )

    def owned_all(turn, part, s):
        return together(
            rs_slots.at[turn, part, s, pl.ds(0, n_cand - 1)], (rs_out[part], rs_in.at[part, s])
        )

    def sent_all(turn, part, owner):
        slots = rs_send.at[turn, part, 0] if owner else rs_send.at[turn, part]
        return together(slots, (rs_out[part], rs_in.at[part, 0]))

    def taken_all(turn, part):
        return together(
            rs_slots.at[turn, part, :, pl.ds(0, len(takers(turn, part)))],
            (ag_out[part], rs_in.at[part, 0]),
        )

    def from_owner(turn, part, o, s, peer, core):
        return pltpu.make_async_remote_copy(
            src_ref=ag_slots.at[turn, part, o, s], dst_ref=ag_slots.at[turn, part, o, s],
            send_sem=ag_out[part], recv_sem=ag_in.at[part, o, s],
            device_id={"cand": peer, "mix": core}, device_id_type=MESH,
        )

    def core_of(turn, part):
        return part * n_mix // parts if turn == ITERS else lead

    def takers(turn, part):
        away = core_of(turn, part) != lead
        order = sorted(range(1, n_cand), key=lambda d: abs(n_cand // 2 - d))
        return order + [0] * away

    def parts_of(core):
        return [part for part in range(parts) if core_of(ITERS, part) == core]

    def row_of(part):
        return pl.ds(part * group % mixes, group)

    halves = range(len(owners))
    each = range(parts)

    @pl.when(ci != lead)
    def _():
        weights[ci] = jnp.zeros(weights.shape[1:], F32)
        weights[ci, :, pl.ds(0, mixes)] = weight_ref[...]
        pl.semaphore_wait(barrier, n_tgt)
        sent = [row_copy(d, ci) for d in range(1, n_tgt)] + [weight_copy(ci)]
        for copy in sent:
            copy.start()
        cand_copy(ci).wait_recv()
        out_cand[...] = -jnp.log(cand_in[...])
        for core in range(lead):

            @pl.when(ci == core)
            def _():
                for part in parts_of(core):
                    for o in halves:
                        for s in range(subs):
                            from_owner(ITERS, part, o, s, owners[o], lead).wait_recv()
                            out_tgt[row_of(part), span(o, s)] = ag_slots[ITERS, part, o, s]
        for copy in sent:
            copy.wait_send()

    @pl.when(ci == lead)
    def _():
        pl.semaphore_wait(barrier, n_tgt - 1 + n_mix * (n_cand - 1) + lead)
        pending = [row_copy(d, lead) for d in range(1, n_tgt)]
        for copy in pending:
            copy.start()
        for core in range(lead):
            late_loads[core].wait()
            cand_ready(core * early)
            row_part[core] = functools.reduce(
                jnp.add, [tile(index, core * early) for index in range(tgt_parts)]
            )
        k_one[...] = k_one_t[...].T

        def x_sum(slots):
            total = slots[lax.rem(xi + n_tgt, n_tgt)]
            for k in range(1, n_tgt):
                total = total + slots[lax.rem(xi - k + n_tgt, n_tgt)]
            return total

        def z_sum(slots):
            total = slots[lax.rem(zi + n_cand, n_cand)]
            for k in range(1, n_cand):
                total = total + slots[lax.rem(zi - k + n_cand, n_cand)]
            return total

        def x_copy(slots, lane, turn, d):
            return pltpu.make_async_remote_copy(
                src_ref=slots.at[0], dst_ref=slots.at[d],
                send_sem=x_send[lane], recv_sem=x_recv.at[turn % 2, lane, d - 1],
                device_id=x_peer(d), device_id_type=MESH,
            )

        def x_start(slots, lane, turn):
            for d in range(1, n_tgt):
                x_copy(slots, lane, turn, d).start()

        def x_arrive(slots, lane, turn):
            for d in range(1, n_tgt):
                x_copy(slots, lane, turn, d).wait_recv()

        def x_sent(slots, lane):
            together(slots.at[pl.ds(0, n_tgt - 1)], (x_send[lane], rs_in.at[0, 0])).wait_send()

        for d in range(1, n_tgt):
            for core in range(n_mix):
                row_copy(d, core).wait_recv()
        row_sums = []
        for core in range(n_mix):
            value = row_part[core]
            for d in range(1, n_tgt):
                value = value + row_slots[d, core]
            row_sums.append(value)
        scale_row = 1.0 / jnp.concatenate(row_sums, axis=1)
        place = lax.broadcasted_iota(jnp.int32, (16, rows), 0)
        head = scale_row.astype(BF16).astype(F32)
        lhs = jnp.where(place == 0, head, jnp.where(place == 1, scale_row - head, 0.0)).astype(BF16)
        part_sum = lax.dot_general(lhs, k_one[...], NN_DIMS, preferred_element_type=F32)
        col_slots[0] = part_sum[:1] + part_sum[1:2]
        for d in range(1, n_cand):
            pltpu.make_async_remote_copy(
                src_ref=col_slots.at[0], dst_ref=col_slots.at[d],
                send_sem=z_sems.at[0], recv_sem=z_sems.at[1],
                device_id=z_peer(d), device_id_type=MESH,
            ).start()
        z_all = together(col_slots.at[pl.ds(1, n_cand - 1)], (z_sems.at[0], z_sems.at[1]))

        for at in range(0, cols, 64):
            power = raised_t[pl.ds(at, 64), :]
            k_two_t[pl.ds(at, 64), :] = (power * power * (1.0 / tgt_total)).astype(BF16)
        k_two[...] = k_two_t[...].T
        for core in range(lead):
            weight_copy(core).wait_recv()
        all_weights = jnp.concatenate(
            [weights[core, :, :mixes] for core in range(lead)] + [weight_ref[...]], axis=1
        )
        all_hot = member_ref[...] == lax.broadcasted_iota(jnp.int32, (tasks, tgt_total), 0)
        counts = jnp.sum(all_hot.astype(F32), axis=1, keepdims=True)
        totals = jnp.sum(all_weights * counts, axis=0, keepdims=True)
        scaled = all_weights * (float(cand_total) / totals)
        own = pl.ds(pl.multiple_of(xi * cols, cols), cols)
        own_hot = (
            member_ref[:, own] == lax.broadcasted_iota(jnp.int32, (tasks, cols), 0)
        ).astype(F32)
        mass[...] = lax.dot_general(
            scaled, own_hot, TN_DIMS, precision=lax.Precision.HIGHEST, preferred_element_type=F32
        )
        z_all.wait_recv()
        col_sum = z_sum(col_slots)

        task_sums = lax.dot_general(
            (own_hot / col_sum).astype(BF16), k_one_t[...], NN_DIMS, preferred_element_type=F32
        )
        for h in range(subs):
            task_slots[h, 0] = task_sums[:, h * strip:(h + 1) * strip]
            x_start(task_slots.at[h], h, 1)
        for h in range(subs):
            x_arrive(task_slots.at[h], h, 1)
            task_all[:, pl.ds(h * strip, strip)] = x_sum(task_slots.at[h])
        for h in range(subs):
            x_sent(task_slots.at[h], h)

        near = zi // owners[1]
        far = 1 - near

        def tgt_send(kernel, turn, part, owner):
            lhs = (1.0 / cand_sums[of(part), :]).astype(BF16)
            if turn > 0:
                sent_all(turn - 1, part, owner).wait_send()
            for o in (far, near):
                value = lax.dot_general(
                    lhs, kernel[:, half(o)], NN_DIMS, preferred_element_type=F32
                )
                for s in range(subs):
                    rs_send[turn, part, o, s] = value[:, s * piece:(s + 1) * piece]
                    if o is far or not owner:
                        to_owner(turn, part, o, s).start()

        def tgt_finish(turn, part, change):
            if turn > 0:
                taken_all(turn - 1, part).wait_send()
            for s in range(subs):
                owned_all(turn, part, s).wait_recv()
                total = rs_send[turn, part, near, s]
                for d in range(n_cand - 1):
                    total = total + rs_slots[turn, part, s, d]
                ag_slots[turn, part, near, s] = change(mass[of(part), span(near, s)] / total)
                for d in takers(turn, part):
                    peer = lax.rem(zi + d, n_cand)
                    from_owner(turn, part, near, s, peer, core_of(turn, part)).start()

        def gathered(turn, part, o, s):
            from_owner(turn, part, o, s, owners[0] + o, lead).wait_recv()

        def cand_send(turn, part, owner):
            total = None
            for o in (near, far):
                for s in range(subs):
                    if o is far or not owner:
                        gathered(turn, part, o, s)
                    value = lax.dot_general(
                        ag_slots[turn, part, o, s].astype(BF16), k_two_t[span(o, s), :],
                        NN_DIMS, preferred_element_type=F32,
                    )
                    total = value if total is None else total + value
            if turn > 0:
                x_sent(cand_slots.at[turn - 1, part], part)
            cand_slots[turn, part, 0] = total
            x_start(cand_slots.at[turn, part], part, turn)

        def cand_finish(turn, part):
            x_arrive(cand_slots.at[turn, part], part, turn)
            cand_sums[of(part), :] = x_sum(cand_slots.at[turn, part])

        def keep(scale):
            return scale

        changes = (jnp.square,) + (keep,) * (ITERS - 1)

        def iterate(owner):
            for part in each:
                cand_sums[of(part), :] = lax.dot_general(
                    scaled[:, part * group:(part + 1) * group], task_all[...], TN_DIMS,
                    precision=lax.Precision.HIGHEST, preferred_element_type=F32,
                )
                tgt_send(k_one, 0, part, owner)
            for turn in range(ITERS):
                if owner:
                    for part in each:
                        tgt_finish(turn, part, changes[turn])
                for part in each:
                    cand_send(turn, part, owner)
                for part in each:
                    cand_finish(turn, part)
                    tgt_send(k_two, 1 + turn, part, owner)
            for core in range(lead):
                cand_copy(core).start()
            out_cand[...] = -jnp.log(cand_sums[pl.ds(lead * mixes, mixes), :])
            if owner:
                for part in each:
                    tgt_finish(ITERS, part, jnp.log)
            for part in parts_of(lead):
                for o in (near, far):
                    for s in range(subs):
                        if o is far or not owner:
                            gathered(ITERS, part, o, s)
                        out_tgt[row_of(part), span(o, s)] = ag_slots[ITERS, part, o, s]
            for part in each:
                sent_all(ITERS, part, owner).wait_send()
                if owner:
                    taken_all(ITERS, part).wait_send()
                x_sent(cand_slots.at[ITERS - 1, part], part)

        owning = (zi == owners[0]) | (zi == owners[1])

        @pl.when(owning)
        def _():
            iterate(True)

        @pl.when(jnp.logical_not(owning))
        def _():
            iterate(False)

        for core in range(lead):
            cand_copy(core).wait_send()
        z_all.wait_send()
        for copy in pending:
            copy.wait_send()


def write_kernel(cand_log, tgt_log, out_cand, out_tgt, sems):
    copies = [
        pltpu.make_async_copy(cand_log, out_cand, sems.at[0]),
        pltpu.make_async_copy(tgt_log, out_tgt, sems.at[1]),
    ]
    for copy in copies:
        copy.start()
    for copy in copies:
        copy.wait()


def fused(candidates, targets, member, mix_weight):
    n_tgt, n_cand, n_mix = lax.axis_size("tgt"), lax.axis_size("cand"), lax.axis_size("mix")
    rows, width = candidates.shape
    cols = targets.shape[0]
    mixes, tasks = mix_weight.shape
    piece, strip = cols // 4, rows // 2
    parts = 2 * n_mix if mixes % 16 == 0 else n_mix
    loads = cols // 256 + rows // n_mix // 256 + n_mix + 1
    group = mixes * n_mix // parts
    logs = pl.pallas_call(
        functools.partial(fused_kernel, n_tgt, n_cand, n_mix, parts),
        out_shape=(pltpu.VMEM((mixes, rows), F32), pltpu.VMEM((mixes, cols), F32)),
        in_specs=[pl.BlockSpec(memory_space=pltpu.HBM)] * 4,
        out_specs=(pl.BlockSpec(memory_space=pltpu.VMEM),) * 2,
        scratch_shapes=[
            pltpu.VMEM((rows, width), BF16),
            pltpu.VMEM((cols, width), BF16),
            pltpu.VMEM((rows, width), BF16),
            pltpu.VMEM((cols, width), BF16),
            pltpu.VMEM((cols, rows), F32),
            pltpu.VMEM((cols, rows), BF16),
            pltpu.VMEM((rows, cols), BF16),
            pltpu.VMEM((cols, rows), BF16),
            pltpu.VMEM((rows, cols), BF16),
            pltpu.VMEM((mixes * n_mix, cols), F32),
            pltpu.VMEM((mixes * n_mix, rows), F32),
            pltpu.VMEM((tasks, rows), F32),
            pltpu.VMEM((1, cols * n_tgt), jnp.int32),
            pltpu.VMEM((tasks, mixes), F32),
            pltpu.VMEM((n_mix, tasks, 128), F32),
            pltpu.VMEM((mixes, rows), F32),
            pltpu.VMEM((n_mix, 1, rows // n_mix), F32),
            pltpu.VMEM((n_tgt, n_mix, 1, rows // n_mix), F32),
            pltpu.VMEM((n_cand, 1, cols), F32),
            pltpu.VMEM((2, n_tgt, tasks, strip), F32),
            pltpu.VMEM((ITERS, parts, n_tgt, group, rows), F32),
            pltpu.VMEM((1 + ITERS, parts, 2, 2, group, piece), F32),
            pltpu.VMEM((1 + ITERS, parts, 2, n_cand, group, piece), F32),
            pltpu.VMEM((1 + ITERS, parts, 2, 2, group, piece), F32),
            pltpu.SemaphoreType.DMA((max(loads, 3 * parts),)),
            pltpu.SemaphoreType.DMA((2, parts, n_tgt - 1)),
            pltpu.SemaphoreType.DMA((2,)),
            pltpu.SemaphoreType.DMA((n_tgt - 1,)),
            pltpu.SemaphoreType.DMA((n_tgt - 1, n_mix)),
            pltpu.SemaphoreType.DMA((parts, 2)),
            pltpu.SemaphoreType.DMA((parts, 2, 2)),
            pltpu.SemaphoreType.DMA((2, n_mix - 1)),
            pltpu.SemaphoreType.DMA((2, n_mix - 1)),
        ],
        compiler_params=pltpu.CompilerParams(
            collective_id=0, has_side_effects=True, vmem_limit_bytes=56 * 1024 * 1024
        ),
    )(candidates, targets, member.reshape(1, -1), mix_weight.T)
    return tuple(pl.pallas_call(
        write_kernel,
        out_shape=(
            jax.ShapeDtypeStruct((mixes, rows), F32),
            jax.ShapeDtypeStruct((mixes, cols), F32),
        ),
        in_specs=[pl.BlockSpec(memory_space=pltpu.VMEM)] * 2,
        out_specs=(pl.BlockSpec(memory_space=pltpu.HBM),) * 2,
        scratch_shapes=[pltpu.SemaphoreType.DMA((2,))],
    )(*(pltpu.with_memory_space_constraint(log, pltpu.VMEM) for log in logs)))


def target_mass(own_member, member, mix_weight, cand_total):
    task_ids = jnp.arange(mix_weight.shape[1], dtype=jnp.int32)
    counts = jnp.sum((member[None, :] == task_ids[:, None]).astype(jnp.float32), axis=1)
    weight_total = jnp.dot(mix_weight, counts, precision=lax.Precision.HIGHEST)
    onehot = (own_member[None, :] == task_ids[:, None]).astype(jnp.float32)
    per_target = jnp.dot(mix_weight, onehot, precision=lax.Precision.HIGHEST)
    return per_target * (cand_total / weight_total)[:, None]


def by_collectives(candidates, targets, member, mix_weight):
    cand_rows = candidates.shape[0]
    tgt_rows = targets.shape[0]
    tgt_total = tgt_rows * lax.axis_size("tgt")
    cand_total = cand_rows * lax.axis_size("cand")
    tgt_unit = unit_rows(targets)
    scores = contract_last(unit_rows(candidates), tgt_unit)
    own_member = lax.dynamic_slice_in_dim(member, lax.axis_index("tgt") * tgt_rows, tgt_rows, 0)
    mass = target_mass(own_member, member, mix_weight, float(cand_total))
    kernel_one = jnp.exp(scores / EPS_FIRST) / tgt_total
    kernel_two = jnp.exp(scores / EPS_SECOND) / tgt_total
    scale_tgt = jnp.ones((mix_weight.shape[0], tgt_rows), jnp.float32)
    scale_cand = jnp.ones((mix_weight.shape[0], cand_rows), jnp.float32)
    for section_index, kernel in enumerate((kernel_one, kernel_two)):
        if section_index == 1:
            scale_tgt = scale_tgt * scale_tgt
        for repeat in range(ITERS):
            partial_value = lax.dot_general(
                scale_tgt, kernel, (((1,), (1,)), ((), ())), precision=lax.Precision.HIGHEST
            )
            scale_cand = 1.0 / lax.psum(partial_value, "tgt")
            column_part = jnp.dot(scale_cand, kernel, precision=lax.Precision.HIGHEST)
            share_cols = tgt_rows // lax.axis_size("cand")
            summed = lax.psum_scatter(column_part, "cand", scatter_dimension=1, tiled=True)
            own_mass = lax.dynamic_slice_in_dim(
                mass, lax.axis_index("cand") * share_cols, share_cols, 1
            )
            scale_tgt = lax.all_gather(own_mass / summed, "cand", axis=1, tiled=True)
    return (jnp.log(scale_cand), jnp.log(scale_tgt))


def solution(mesh):
    in_specs = (
        P(("groups", "cand"), None),
        P(("groups", "tgt"), None),
        P("groups"),
        P("mix", "groups"),
    )
    out_specs = (P("mix", ("groups", "cand")), P("mix", ("groups", "tgt")))
    n_tgt, n_cand, n_mix = mesh.shape["tgt"], mesh.shape["cand"], mesh.shape["mix"]

    def local(candidates, targets, member, mix_weight):
        lanes = targets.shape[0] % (128 * n_cand) == 0 and candidates.shape[0] % 512 == 0
        paired = n_cand % 2 == 0 and n_tgt > 1 and n_mix == 2
        step = fused if lanes and paired else by_collectives
        return step(candidates, targets, member, mix_weight)

    return jax.shard_map(local, mesh=mesh, in_specs=in_specs, out_specs=out_specs, check_vma=False)
```

```python
import functools
import math

import jax
import jax.numpy as jnp
from jax import lax
from jax.experimental import pallas as pl
from jax.experimental.pallas import tpu as pltpu
from jax.sharding import PartitionSpec as P

ITERS = 2


EPS_FIRST = 0.05
EPS_SECOND = 0.025

MESH = pl.DeviceIdType.MESH
F32 = jnp.float32
BF16 = jnp.bfloat16
NT_DIMS = (((1,), (1,)), ((), ()))
TN_DIMS = (((0,), (0,)), ((), ()))
NN_DIMS = (((1,), (0,)), ((), ()))


def unit_rows(embedding):
    values = embedding.astype(jnp.float32)
    mean_sq = jnp.mean(values * values, axis=1, keepdims=True)
    return (values * (lax.rsqrt(mean_sq + 1e-06) * (1.0 / math.sqrt(values.shape[1])))).astype(
        jnp.bfloat16
    )


def contract_last(left, right):
    return lax.dot_general(left, right, NT_DIMS, preferred_element_type=jnp.float32)


def fused_kernel(
    n_tgt, n_cand, n_mix, parts, cand_hbm, tgt_hbm, member_hbm, weight_hbm, out_cand, out_tgt,
    cand_rows, tgt_rows, cand_unit, tgt_unit, raised_t, k_one_t, k_one, k_two_t, k_two,
    mass, cand_sums, task_all, member_ref, weight_ref, weights, cand_in,
    row_part, row_slots, col_slots, task_slots, cand_slots, rs_send, rs_slots, ag_slots,
    load_sems, x_recv, z_sems, row_out, row_in, rs_in, ag_in,
    chip_out, chip_in,
):
    xi, zi, ci = lax.axis_index("tgt"), lax.axis_index("cand"), lax.axis_index("mix")
    rows, width = cand_hbm.shape
    cols = tgt_hbm.shape[0]
    tasks, mixes = weight_hbm.shape
    lead = n_mix - 1
    owners = (n_cand // 2 - 1, n_cand // 2)

    class Sems:
        def __init__(self, first):
            self.first = first

        def __getitem__(self, part):
            return load_sems.at[self.first + part]

    x_send, rs_out, ag_out = (Sems(k * parts) for k in range(3))
    share = cols // len(owners)
    subs = 2
    piece, strip = share // subs, rows // subs
    group = mixes * n_mix // parts
    tgt_total, cand_total = cols * n_tgt, rows * n_cand
    block = 256
    early = rows // n_mix

    def load(src, dst, sem, *at):
        if at:
            src, dst = src.at[pl.ds(*at)], dst.at[pl.ds(*at)]
        return pltpu.make_async_copy(src, dst, load_sems.at[sem])

    tgt_parts, cand_parts = cols // block, early // block
    tgt_loads = [load(tgt_hbm, tgt_rows, k, k * block, block) for k in range(tgt_parts)]
    cand_loads = [
        load(cand_hbm, cand_rows, tgt_parts + k,
             pl.multiple_of(ci * early + k * block, block), block)
        for k in range(cand_parts)
    ]
    late_loads = [
        load(cand_hbm, cand_rows, tgt_parts + cand_parts + core, core * early, early)
        for core in range(lead)
    ]
    small_loads = [
        load(src, dst, tgt_parts + cand_parts + lead + k)
        for k, (src, dst) in enumerate(((member_hbm, member_ref), (weight_hbm, weight_ref)))
    ]
    for copy in cand_loads + tgt_loads + small_loads:
        copy.start()

    def x_peer(d):
        return {"tgt": lax.rem(xi + d, n_tgt), "mix": lead}

    def z_peer(d):
        return {"cand": lax.rem(zi + d, n_cand), "mix": lead}

    barrier = pltpu.get_barrier_semaphore()

    def hello(**peer):
        pl.semaphore_signal(barrier, inc=1, device_id=peer, device_id_type=MESH)

    for d in range(1, n_cand):
        hello(**z_peer(d))

    @pl.when(ci == lead)
    def _():
        for core in range(lead):
            late_loads[core].start()
            hello(mix=core)
        for d in range(1, n_tgt):
            for core in range(n_mix):
                hello(tgt=lax.rem(xi + d, n_tgt), mix=core)

    @pl.when(ci != lead)
    def _():
        hello(mix=lead)

    def cand_ready(first):
        for at in range(0, early, block):
            at = pl.ds(pl.multiple_of(first + at, block), block)
            cand_unit[at, :] = unit_rows(cand_rows[at, :])

    def tgt_ready(index):
        tgt_loads[index].wait()
        at = pl.ds(index * block, block)
        tgt_unit[at, :] = unit_rows(tgt_rows[at, :])

    def tile(index, first):
        at = pl.ds(index * block if isinstance(index, int) else pl.multiple_of(index * block, block), block)
        across = pl.ds(pl.multiple_of(first, early), early)
        power = jnp.exp(contract_last(tgt_unit[at, :], cand_unit[across, :]) * (1.0 / EPS_FIRST))
        raised_t[at, across] = power
        k_one_t[at, across] = (power * (1.0 / tgt_total)).astype(BF16)
        return jnp.sum(power, axis=0, keepdims=True) * (1.0 / tgt_total)

    for copy in cand_loads:
        copy.wait()
    cand_ready(ci * early)
    tgt_ready(0)
    sums = []
    for index in range(1, tgt_parts):
        tgt_ready(index)
        sums.append(tile(index - 1, ci * early))
    sums.append(tile(tgt_parts - 1, ci * early))
    row_part[ci] = functools.reduce(jnp.add, sums)
    for copy in small_loads:
        copy.wait()

    def row_copy(d, core):
        return pltpu.make_async_remote_copy(
            src_ref=row_part.at[core], dst_ref=row_slots.at[d, core],
            send_sem=row_out.at[d - 1], recv_sem=row_in.at[d - 1, core],
            device_id=x_peer(d), device_id_type=MESH,
        )

    def weight_copy(core):
        return pltpu.make_async_remote_copy(
            src_ref=weights.at[core], dst_ref=weights.at[core],
            send_sem=chip_out.at[0, core], recv_sem=chip_in.at[0, core],
            device_id={"mix": lead}, device_id_type=MESH,
        )

    def cand_copy(core):
        return pltpu.make_async_remote_copy(
            src_ref=cand_sums.at[pl.ds(core * mixes, mixes)], dst_ref=cand_in,
            send_sem=chip_out.at[1, core], recv_sem=chip_in.at[1, core],
            device_id={"mix": core}, device_id_type=MESH,
        )

    def of(part):
        at = part * group
        return pl.ds(at if isinstance(at, int) else pl.multiple_of(at, group), group)

    def half(o):
        return pl.ds(o * share if isinstance(o, int) else pl.multiple_of(o * share, share), share)

    def span(o, s):
        at = o * share + s * piece
        return pl.ds(at if isinstance(at, int) else pl.multiple_of(at, piece), piece)

    def to_owner(turn, part, o, s):
        owner = owners[0] + o
        return pltpu.make_async_remote_copy(
            src_ref=rs_send.at[turn, part, o, s],
            dst_ref=rs_slots.at[turn, part, s, lax.rem(zi - owner + n_cand, n_cand) - 1],
            send_sem=rs_out[part], recv_sem=rs_in.at[part, s],
            device_id={"cand": owner, "mix": lead}, device_id_type=MESH,
        )

    def together(slots, sems):
        return pltpu.make_async_remote_copy(
            src_ref=slots, dst_ref=slots, send_sem=sems[0], recv_sem=sems[1],
            device_id={"tgt": lax.rem(xi + 1, n_tgt), "mix": lead}, device_id_type=MESH,
        )

    def owned_all(turn, part, s):
        return together(
            rs_slots.at[turn, part, s, pl.ds(0, n_cand - 1)], (rs_out[part], rs_in.at[part, s])
        )

    def sent_all(turn, part, owner):
        slots = rs_send.at[turn, part, 0] if owner else rs_send.at[turn, part]
        return together(slots, (rs_out[part], rs_in.at[part, 0]))

    def taken_all(turn, part, core):
        return together(
            rs_slots.at[turn, part, :, pl.ds(0, len(takers(core)))],
            (ag_out[part], rs_in.at[part, 0]),
        )

    def from_owner(turn, part, o, s, peer, core):
        return pltpu.make_async_remote_copy(
            src_ref=ag_slots.at[turn, part, o, s], dst_ref=ag_slots.at[turn, part, o, s],
            send_sem=ag_out[part], recv_sem=ag_in.at[part, o, s],
            device_id={"cand": peer, "mix": core}, device_id_type=MESH,
        )

    def core_of(turn, part):
        return part * n_mix // parts if turn == ITERS else lead

    def takers(core):
        away = core != lead
        order = sorted(range(1, n_cand), key=lambda d: abs(n_cand // 2 - d))
        return order + [0] * away

    def parts_of(core):
        return [part for part in range(parts) if core_of(ITERS, part) == core]

    def row_of(part):
        return pl.ds(part * group % mixes, group)

    halves = range(len(owners))
    each = range(parts)

    @pl.when(ci != lead)
    def _():
        weights[ci] = jnp.zeros(weights.shape[1:], F32)
        weights[ci, :, pl.ds(0, mixes)] = weight_ref[...]
        pl.semaphore_wait(barrier, n_tgt)
        sent = [row_copy(d, ci) for d in range(1, n_tgt)] + [weight_copy(ci)]
        for copy in sent:
            copy.start()
        cand_copy(ci).wait_recv()
        out_cand[...] = -jnp.log(cand_in[...])
        for core in range(lead):

            @pl.when(ci == core)
            def _():
                for part in parts_of(core):
                    for o in halves:
                        for s in range(subs):
                            from_owner(ITERS, part, o, s, owners[o], lead).wait_recv()
                            out_tgt[row_of(part), span(o, s)] = ag_slots[ITERS, part, o, s]
        for copy in sent:
            copy.wait_send()

    @pl.when(ci == lead)
    def _():
        pl.semaphore_wait(barrier, n_tgt - 1 + n_mix * (n_cand - 1) + lead)
        pending = [row_copy(d, lead) for d in range(1, n_tgt)]
        for copy in pending:
            copy.start()
        for core in range(lead):
            late_loads[core].wait()
            cand_ready(core * early)
            row_part[core] = functools.reduce(
                jnp.add, [tile(index, core * early) for index in range(tgt_parts)]
            )
        k_one[...] = k_one_t[...].T

        def x_sum(slots):
            total = slots[lax.rem(xi + n_tgt, n_tgt)]
            for k in range(1, n_tgt):
                total = total + slots[lax.rem(xi - k + n_tgt, n_tgt)]
            return total

        def z_sum(slots):
            total = slots[lax.rem(zi + n_cand, n_cand)]
            for k in range(1, n_cand):
                total = total + slots[lax.rem(zi - k + n_cand, n_cand)]
            return total

        def x_copy(slots, lane, turn, d):
            return pltpu.make_async_remote_copy(
                src_ref=slots.at[0], dst_ref=slots.at[d],
                send_sem=x_send[lane], recv_sem=x_recv.at[turn % 2, lane, d - 1],
                device_id=x_peer(d), device_id_type=MESH,
            )

        def x_start(slots, lane, turn):
            for d in range(1, n_tgt):
                x_copy(slots, lane, turn, d).start()

        def x_arrive(slots, lane, turn):
            for d in range(1, n_tgt):
                x_copy(slots, lane, turn, d).wait_recv()

        def x_sent(slots, lane):
            together(slots.at[pl.ds(0, n_tgt - 1)], (x_send[lane], rs_in.at[0, 0])).wait_send()

        for d in range(1, n_tgt):
            for core in range(n_mix):
                row_copy(d, core).wait_recv()
        row_sums = []
        for core in range(n_mix):
            value = row_part[core]
            for d in range(1, n_tgt):
                value = value + row_slots[d, core]
            row_sums.append(value)
        scale_row = 1.0 / jnp.concatenate(row_sums, axis=1)
        place = lax.broadcasted_iota(jnp.int32, (16, rows), 0)
        head = scale_row.astype(BF16).astype(F32)
        lhs = jnp.where(place == 0, head, jnp.where(place == 1, scale_row - head, 0.0)).astype(BF16)
        part_sum = lax.dot_general(lhs, k_one[...], NN_DIMS, preferred_element_type=F32)
        col_slots[0] = part_sum[:1] + part_sum[1:2]
        for d in range(1, n_cand):
            pltpu.make_async_remote_copy(
                src_ref=col_slots.at[0], dst_ref=col_slots.at[d],
                send_sem=z_sems.at[0], recv_sem=z_sems.at[1],
                device_id=z_peer(d), device_id_type=MESH,
            ).start()
        z_all = together(col_slots.at[pl.ds(1, n_cand - 1)], (z_sems.at[0], z_sems.at[1]))

        for at in range(0, cols, 64):
            power = raised_t[pl.ds(at, 64), :]
            k_two_t[pl.ds(at, 64), :] = (power * power * (1.0 / tgt_total)).astype(BF16)
        k_two[...] = k_two_t[...].T
        for core in range(lead):
            weight_copy(core).wait_recv()
        all_weights = jnp.concatenate(
            [weights[core, :, :mixes] for core in range(lead)] + [weight_ref[...]], axis=1
        )
        all_hot = member_ref[...] == lax.broadcasted_iota(jnp.int32, (tasks, tgt_total), 0)
        counts = jnp.sum(all_hot.astype(F32), axis=1, keepdims=True)
        totals = jnp.sum(all_weights * counts, axis=0, keepdims=True)
        scaled = all_weights * (float(cand_total) / totals)
        own = pl.ds(pl.multiple_of(xi * cols, cols), cols)
        own_hot = (
            member_ref[:, own] == lax.broadcasted_iota(jnp.int32, (tasks, cols), 0)
        ).astype(F32)
        mass[...] = lax.dot_general(
            scaled, own_hot, TN_DIMS, precision=lax.Precision.HIGHEST, preferred_element_type=F32
        )
        z_all.wait_recv()
        col_sum = z_sum(col_slots)

        task_sums = lax.dot_general(
            (own_hot / col_sum).astype(BF16), k_one_t[...], NN_DIMS, preferred_element_type=F32
        )
        for h in range(subs):
            task_slots[h, 0] = task_sums[:, h * strip:(h + 1) * strip]
            x_start(task_slots.at[h], h, 1)
        for h in range(subs):
            x_arrive(task_slots.at[h], h, 1)
            task_all[:, pl.ds(h * strip, strip)] = x_sum(task_slots.at[h])
        for h in range(subs):
            x_sent(task_slots.at[h], h)

        near = zi // owners[1]
        far = 1 - near

        def tgt_send(kernel, turn, part, owner):
            lhs = (1.0 / cand_sums[of(part), :]).astype(BF16)
            if turn > 0:
                sent_all(turn - 1, part, owner).wait_send()
            for o in (far, near):
                value = lax.dot_general(
                    lhs, kernel[:, half(o)], NN_DIMS, preferred_element_type=F32
                )
                for s in range(subs):
                    rs_send[turn, part, o, s] = value[:, s * piece:(s + 1) * piece]
                    if o is far or not owner:
                        to_owner(turn, part, o, s).start()

        def tgt_finish(turn, part, core, change):
            if turn > 0:
                taken_all(turn - 1, part, lead).wait_send()
            for s in range(subs):
                owned_all(turn, part, s).wait_recv()
                total = rs_send[turn, part, near, s]
                for d in range(n_cand - 1):
                    total = total + rs_slots[turn, part, s, d]
                ag_slots[turn, part, near, s] = change(mass[of(part), span(near, s)] / total)
                for d in takers(core):
                    peer = lax.rem(zi + d, n_cand)
                    from_owner(turn, part, near, s, peer, core).start()

        def gathered(turn, part, o, s):
            from_owner(turn, part, o, s, owners[0] + o, lead).wait_recv()

        def cand_send(turn, part, owner):
            total = None
            for o in (near, far):
                for s in range(subs):
                    if o is far or not owner:
                        gathered(turn, part, o, s)
                    value = lax.dot_general(
                        ag_slots[turn, part, o, s].astype(BF16), k_two_t[span(o, s), :],
                        NN_DIMS, preferred_element_type=F32,
                    )
                    total = value if total is None else total + value
            if turn > 0:
                x_sent(cand_slots.at[turn - 1, part], part)
            cand_slots[turn, part, 0] = total
            x_start(cand_slots.at[turn, part], part, turn)

        def cand_finish(turn, part):
            x_arrive(cand_slots.at[turn, part], part, turn)
            cand_sums[of(part), :] = x_sum(cand_slots.at[turn, part])

        def keep(scale):
            return scale

        changes = (jnp.square,) + (keep,) * (ITERS - 1)

        def over(group_of_parts, step):
            def body(part, carry):
                step(part)
                return carry

            lax.fori_loop(group_of_parts[0], group_of_parts[-1] + 1, body, 0)

        def iterate(owner):
            for part in each:
                cand_sums[of(part), :] = lax.dot_general(
                    scaled[:, part * group:(part + 1) * group], task_all[...], TN_DIMS,
                    precision=lax.Precision.HIGHEST, preferred_element_type=F32,
                )
                tgt_send(k_one, 0, part, owner)
            for turn in range(ITERS):
                if owner:
                    over(each, lambda part: tgt_finish(turn, part, lead, changes[turn]))
                over(each, lambda part: cand_send(turn, part, owner))

                def across(part):
                    cand_finish(turn, part)
                    tgt_send(k_two, 1 + turn, part, owner)

                over(each, across)
            for core in range(lead):
                cand_copy(core).start()
            out_cand[...] = -jnp.log(cand_sums[pl.ds(lead * mixes, mixes), :])
            if owner:
                for core in range(n_mix):
                    over(parts_of(core), lambda part: tgt_finish(ITERS, part, core, jnp.log))
            for part in parts_of(lead):
                for o in (near, far):
                    for s in range(subs):
                        if o is far or not owner:
                            gathered(ITERS, part, o, s)
                        out_tgt[row_of(part), span(o, s)] = ag_slots[ITERS, part, o, s]
            for part in each:
                sent_all(ITERS, part, owner).wait_send()
                if owner:
                    taken_all(ITERS, part, core_of(ITERS, part)).wait_send()
                x_sent(cand_slots.at[ITERS - 1, part], part)

        owning = (zi == owners[0]) | (zi == owners[1])

        @pl.when(owning)
        def _():
            iterate(True)

        @pl.when(jnp.logical_not(owning))
        def _():
            iterate(False)

        for core in range(lead):
            cand_copy(core).wait_send()
        z_all.wait_send()
        for copy in pending:
            copy.wait_send()


def write_kernel(cand_log, tgt_log, out_cand, out_tgt, sems):
    copies = [
        pltpu.make_async_copy(cand_log, out_cand, sems.at[0]),
        pltpu.make_async_copy(tgt_log, out_tgt, sems.at[1]),
    ]
    for copy in copies:
        copy.start()
    for copy in copies:
        copy.wait()


def fused(candidates, targets, member, mix_weight):
    n_tgt, n_cand, n_mix = lax.axis_size("tgt"), lax.axis_size("cand"), lax.axis_size("mix")
    rows, width = candidates.shape
    cols = targets.shape[0]
    mixes, tasks = mix_weight.shape
    piece, strip = cols // 4, rows // 2
    parts = 2 * n_mix if mixes % 16 == 0 else n_mix
    loads = cols // 256 + rows // n_mix // 256 + n_mix + 1
    group = mixes * n_mix // parts
    logs = pl.pallas_call(
        functools.partial(fused_kernel, n_tgt, n_cand, n_mix, parts),
        out_shape=(pltpu.VMEM((mixes, rows), F32), pltpu.VMEM((mixes, cols), F32)),
        in_specs=[pl.BlockSpec(memory_space=pltpu.HBM)] * 4,
        out_specs=(pl.BlockSpec(memory_space=pltpu.VMEM),) * 2,
        scratch_shapes=[
            pltpu.VMEM((rows, width), BF16),
            pltpu.VMEM((cols, width), BF16),
            pltpu.VMEM((rows, width), BF16),
            pltpu.VMEM((cols, width), BF16),
            pltpu.VMEM((cols, rows), F32),
            pltpu.VMEM((cols, rows), BF16),
            pltpu.VMEM((rows, cols), BF16),
            pltpu.VMEM((cols, rows), BF16),
            pltpu.VMEM((rows, cols), BF16),
            pltpu.VMEM((mixes * n_mix, cols), F32),
            pltpu.VMEM((mixes * n_mix, rows), F32),
            pltpu.VMEM((tasks, rows), F32),
            pltpu.VMEM((1, cols * n_tgt), jnp.int32),
            pltpu.VMEM((tasks, mixes), F32),
            pltpu.VMEM((n_mix, tasks, 128), F32),
            pltpu.VMEM((mixes, rows), F32),
            pltpu.VMEM((n_mix, 1, rows // n_mix), F32),
            pltpu.VMEM((n_tgt, n_mix, 1, rows // n_mix), F32),
            pltpu.VMEM((n_cand, 1, cols), F32),
            pltpu.VMEM((2, n_tgt, tasks, strip), F32),
            pltpu.VMEM((ITERS, parts, n_tgt, group, rows), F32),
            pltpu.VMEM((1 + ITERS, parts, 2, 2, group, piece), F32),
            pltpu.VMEM((1 + ITERS, parts, 2, n_cand, group, piece), F32),
            pltpu.VMEM((1 + ITERS, parts, 2, 2, group, piece), F32),
            pltpu.SemaphoreType.DMA((max(loads, 3 * parts),)),
            pltpu.SemaphoreType.DMA((2, parts, n_tgt - 1)),
            pltpu.SemaphoreType.DMA((2,)),
            pltpu.SemaphoreType.DMA((n_tgt - 1,)),
            pltpu.SemaphoreType.DMA((n_tgt - 1, n_mix)),
            pltpu.SemaphoreType.DMA((parts, 2)),
            pltpu.SemaphoreType.DMA((parts, 2, 2)),
            pltpu.SemaphoreType.DMA((2, n_mix - 1)),
            pltpu.SemaphoreType.DMA((2, n_mix - 1)),
        ],
        compiler_params=pltpu.CompilerParams(
            collective_id=0, has_side_effects=True, vmem_limit_bytes=56 * 1024 * 1024
        ),
    )(candidates, targets, member.reshape(1, -1), mix_weight.T)
    return tuple(pl.pallas_call(
        write_kernel,
        out_shape=(
            jax.ShapeDtypeStruct((mixes, rows), F32),
            jax.ShapeDtypeStruct((mixes, cols), F32),
        ),
        in_specs=[pl.BlockSpec(memory_space=pltpu.VMEM)] * 2,
        out_specs=(pl.BlockSpec(memory_space=pltpu.HBM),) * 2,
        scratch_shapes=[pltpu.SemaphoreType.DMA((2,))],
    )(*(pltpu.with_memory_space_constraint(log, pltpu.VMEM) for log in logs)))


def target_mass(own_member, member, mix_weight, cand_total):
    task_ids = jnp.arange(mix_weight.shape[1], dtype=jnp.int32)
    counts = jnp.sum((member[None, :] == task_ids[:, None]).astype(jnp.float32), axis=1)
    weight_total = jnp.dot(mix_weight, counts, precision=lax.Precision.HIGHEST)
    onehot = (own_member[None, :] == task_ids[:, None]).astype(jnp.float32)
    per_target = jnp.dot(mix_weight, onehot, precision=lax.Precision.HIGHEST)
    return per_target * (cand_total / weight_total)[:, None]


def by_collectives(candidates, targets, member, mix_weight):
    cand_rows = candidates.shape[0]
    tgt_rows = targets.shape[0]
    tgt_total = tgt_rows * lax.axis_size("tgt")
    cand_total = cand_rows * lax.axis_size("cand")
    tgt_unit = unit_rows(targets)
    scores = contract_last(unit_rows(candidates), tgt_unit)
    own_member = lax.dynamic_slice_in_dim(member, lax.axis_index("tgt") * tgt_rows, tgt_rows, 0)
    mass = target_mass(own_member, member, mix_weight, float(cand_total))
    kernel_one = jnp.exp(scores / EPS_FIRST) / tgt_total
    kernel_two = jnp.exp(scores / EPS_SECOND) / tgt_total
    scale_tgt = jnp.ones((mix_weight.shape[0], tgt_rows), jnp.float32)
    scale_cand = jnp.ones((mix_weight.shape[0], cand_rows), jnp.float32)
    for section_index, kernel in enumerate((kernel_one, kernel_two)):
        if section_index == 1:
            scale_tgt = scale_tgt * scale_tgt
        for repeat in range(ITERS):
            partial_value = lax.dot_general(
                scale_tgt, kernel, (((1,), (1,)), ((), ())), precision=lax.Precision.HIGHEST
            )
            scale_cand = 1.0 / lax.psum(partial_value, "tgt")
            column_part = jnp.dot(scale_cand, kernel, precision=lax.Precision.HIGHEST)
            share_cols = tgt_rows // lax.axis_size("cand")
            summed = lax.psum_scatter(column_part, "cand", scatter_dimension=1, tiled=True)
            own_mass = lax.dynamic_slice_in_dim(
                mass, lax.axis_index("cand") * share_cols, share_cols, 1
            )
            scale_tgt = lax.all_gather(own_mass / summed, "cand", axis=1, tiled=True)
    return (jnp.log(scale_cand), jnp.log(scale_tgt))


def solution(mesh):
    in_specs = (
        P(("groups", "cand"), None),
        P(("groups", "tgt"), None),
        P("groups"),
        P("mix", "groups"),
    )
    out_specs = (P("mix", ("groups", "cand")), P("mix", ("groups", "tgt")))
    n_tgt, n_cand, n_mix = mesh.shape["tgt"], mesh.shape["cand"], mesh.shape["mix"]

    def local(candidates, targets, member, mix_weight):
        lanes = targets.shape[0] % (128 * n_cand) == 0 and candidates.shape[0] % 512 == 0
        paired = n_cand % 2 == 0 and n_tgt > 1 and n_mix == 2
        step = fused if lanes and paired else by_collectives
        return step(candidates, targets, member, mix_weight)

    return jax.shard_map(local, mesh=mesh, in_specs=in_specs, out_specs=out_specs, check_vma=False)
```

```python
import functools
import math

import jax
import jax.numpy as jnp
from jax import lax
from jax.experimental import pallas as pl
from jax.experimental.pallas import tpu as pltpu
from jax.sharding import PartitionSpec as P

ITERS = 2


EPS_FIRST = 0.05
EPS_SECOND = 0.025

MESH = pl.DeviceIdType.MESH
F32 = jnp.float32
BF16 = jnp.bfloat16
NT_DIMS = (((1,), (1,)), ((), ()))
TN_DIMS = (((0,), (0,)), ((), ()))
NN_DIMS = (((1,), (0,)), ((), ()))


def unit_rows(embedding):
    values = embedding.astype(jnp.float32)
    mean_sq = jnp.mean(values * values, axis=1, keepdims=True)
    return (values * (lax.rsqrt(mean_sq + 1e-06) * (1.0 / math.sqrt(values.shape[1])))).astype(
        jnp.bfloat16
    )


def contract_last(left, right):
    return lax.dot_general(left, right, NT_DIMS, preferred_element_type=jnp.float32)


def fused_kernel(
    n_tgt, n_cand, n_mix, parts, cand_hbm, tgt_hbm, member_hbm, weight_hbm, out_cand, out_tgt,
    cand_rows, tgt_rows, cand_unit, tgt_unit, raised_t, k_one_t, k_one, k_two_t, k_two,
    mass, cand_sums, task_all, member_ref, weight_ref, weights, cand_in,
    row_part, row_slots, col_slots, task_slots, cand_slots, rs_send, rs_slots, ag_slots,
    load_sems, x_recv, z_sems, row_out, row_in, rs_in, ag_in,
    chip_out, chip_in,
):
    xi, zi, ci = lax.axis_index("tgt"), lax.axis_index("cand"), lax.axis_index("mix")
    rows, width = cand_hbm.shape
    cols = tgt_hbm.shape[0]
    tasks, mixes = weight_hbm.shape
    lead = n_mix - 1
    owners = (n_cand // 2 - 1, n_cand // 2)

    class Sems:
        def __init__(self, first):
            self.first = first

        def __getitem__(self, part):
            return load_sems.at[self.first + part]

    x_send, rs_out, ag_out = (Sems(k * parts) for k in range(3))
    share = cols // len(owners)
    subs = 2
    piece, strip = share // subs, rows // subs
    group = mixes * n_mix // parts
    tgt_total, cand_total = cols * n_tgt, rows * n_cand
    block = 256
    early = rows // n_mix

    def load(src, dst, sem, *at):
        if at:
            src, dst = src.at[pl.ds(*at)], dst.at[pl.ds(*at)]
        return pltpu.make_async_copy(src, dst, load_sems.at[sem])

    tgt_parts, cand_parts = cols // block, early // block
    tgt_loads = [load(tgt_hbm, tgt_rows, k, k * block, block) for k in range(tgt_parts)]
    cand_loads = [
        load(cand_hbm, cand_rows, tgt_parts + k,
             pl.multiple_of(ci * early + k * block, block), block)
        for k in range(cand_parts)
    ]
    late_loads = [
        load(cand_hbm, cand_rows, tgt_parts + cand_parts + core, core * early, early)
        for core in range(lead)
    ]
    small_loads = [
        load(src, dst, tgt_parts + cand_parts + lead + k)
        for k, (src, dst) in enumerate(((member_hbm, member_ref), (weight_hbm, weight_ref)))
    ]
    for copy in cand_loads + tgt_loads + small_loads:
        copy.start()

    def x_peer(d):
        return {"tgt": lax.rem(xi + d, n_tgt), "mix": lead}

    def z_peer(d):
        return {"cand": lax.rem(zi + d, n_cand), "mix": lead}

    barrier = pltpu.get_barrier_semaphore()

    def hello(**peer):
        pl.semaphore_signal(barrier, inc=1, device_id=peer, device_id_type=MESH)

    for d in range(1, n_cand):
        hello(**z_peer(d))

    @pl.when(ci == lead)
    def _():
        for core in range(lead):
            late_loads[core].start()
            hello(mix=core)
        for d in range(1, n_tgt):
            for core in range(n_mix):
                hello(tgt=lax.rem(xi + d, n_tgt), mix=core)

    @pl.when(ci != lead)
    def _():
        hello(mix=lead)

    def cand_ready(first):
        for at in range(0, early, block):
            at = pl.ds(pl.multiple_of(first + at, block), block)
            cand_unit[at, :] = unit_rows(cand_rows[at, :])

    def tgt_ready(index):
        tgt_loads[index].wait()
        at = pl.ds(index * block, block)
        tgt_unit[at, :] = unit_rows(tgt_rows[at, :])

    def tile(index, first):
        at = pl.ds(index * block if isinstance(index, int) else pl.multiple_of(index * block, block), block)
        across = pl.ds(pl.multiple_of(first, early), early)
        power = jnp.exp(contract_last(tgt_unit[at, :], cand_unit[across, :]) * (1.0 / EPS_FIRST))
        raised_t[at, across] = power
        k_one_t[at, across] = (power * (1.0 / tgt_total)).astype(BF16)
        return jnp.sum(power, axis=0, keepdims=True) * (1.0 / tgt_total)

    for copy in cand_loads:
        copy.wait()
    cand_ready(ci * early)
    tgt_ready(0)
    sums = []
    for index in range(1, tgt_parts):
        tgt_ready(index)
        sums.append(tile(index - 1, ci * early))
    sums.append(tile(tgt_parts - 1, ci * early))
    row_part[ci] = functools.reduce(jnp.add, sums)
    for copy in small_loads:
        copy.wait()

    def row_copy(d, core):
        return pltpu.make_async_remote_copy(
            src_ref=row_part.at[core], dst_ref=row_slots.at[d, core],
            send_sem=row_out.at[d - 1], recv_sem=row_in.at[d - 1, core],
            device_id=x_peer(d), device_id_type=MESH,
        )

    def weight_copy(core):
        return pltpu.make_async_remote_copy(
            src_ref=weights.at[core], dst_ref=weights.at[core],
            send_sem=chip_out.at[0, core], recv_sem=chip_in.at[0, core],
            device_id={"mix": lead}, device_id_type=MESH,
        )

    def cand_copy(core):
        return pltpu.make_async_remote_copy(
            src_ref=cand_sums.at[pl.ds(core * mixes, mixes)], dst_ref=cand_in,
            send_sem=chip_out.at[1, core], recv_sem=chip_in.at[1, core],
            device_id={"mix": core}, device_id_type=MESH,
        )

    def of(part):
        at = part * group
        return pl.ds(at if isinstance(at, int) else pl.multiple_of(at, group), group)

    def half(o):
        return pl.ds(o * share if isinstance(o, int) else pl.multiple_of(o * share, share), share)

    def span(o, s):
        at = o * share + s * piece
        return pl.ds(at if isinstance(at, int) else pl.multiple_of(at, piece), piece)

    def to_owner(turn, part, o, s):
        owner = owners[0] + o
        return pltpu.make_async_remote_copy(
            src_ref=rs_send.at[turn, part, o, s],
            dst_ref=rs_slots.at[turn, part, s, lax.rem(zi - owner + n_cand, n_cand) - 1],
            send_sem=rs_out[part], recv_sem=rs_in.at[part, s],
            device_id={"cand": owner, "mix": lead}, device_id_type=MESH,
        )

    def together(slots, sems):
        return pltpu.make_async_remote_copy(
            src_ref=slots, dst_ref=slots, send_sem=sems[0], recv_sem=sems[1],
            device_id={"tgt": lax.rem(xi + 1, n_tgt), "mix": lead}, device_id_type=MESH,
        )

    def owned_all(turn, part, s):
        return together(
            rs_slots.at[turn, part, s, pl.ds(0, n_cand - 1)], (rs_out[part], rs_in.at[part, s])
        )

    def sent_all(turn, part, owner):
        slots = rs_send.at[turn, part, 0] if owner else rs_send.at[turn, part]
        return together(slots, (rs_out[part], rs_in.at[part, 0]))

    def taken_all(turn, part, core):
        return together(
            rs_slots.at[turn, part, :, pl.ds(0, len(takers(core)))],
            (ag_out[part], rs_in.at[part, 0]),
        )

    def from_owner(turn, part, o, s, peer, core):
        return pltpu.make_async_remote_copy(
            src_ref=ag_slots.at[turn, part, o, s], dst_ref=ag_slots.at[turn, part, o, s],
            send_sem=ag_out[part], recv_sem=ag_in.at[part, o, s],
            device_id={"cand": peer, "mix": core}, device_id_type=MESH,
        )

    def core_of(turn, part):
        return part * n_mix // parts if turn == ITERS else lead

    def takers(core):
        away = core != lead
        order = sorted(range(1, n_cand), key=lambda d: abs(n_cand // 2 - d))
        return order + [0] * away

    def parts_of(core):
        return [part for part in range(parts) if core_of(ITERS, part) == core]

    def row_of(part):
        return pl.ds(part * group % mixes, group)

    halves = range(len(owners))
    each = range(parts)

    @pl.when(ci != lead)
    def _():
        weights[ci] = jnp.zeros(weights.shape[1:], F32)
        weights[ci, :, pl.ds(0, mixes)] = weight_ref[...]
        pl.semaphore_wait(barrier, n_tgt)
        sent = [row_copy(d, ci) for d in range(1, n_tgt)] + [weight_copy(ci)]
        for copy in sent:
            copy.start()
        cand_copy(ci).wait_recv()
        out_cand[...] = -jnp.log(cand_in[...])
        for core in range(lead):

            @pl.when(ci == core)
            def _():
                for part in parts_of(core):
                    for o in halves:
                        for s in range(subs):
                            from_owner(ITERS, part, o, s, owners[o], lead).wait_recv()
                            out_tgt[row_of(part), span(o, s)] = ag_slots[ITERS, part, o, s]
        for copy in sent:
            copy.wait_send()

    @pl.when(ci == lead)
    def _():
        pl.semaphore_wait(barrier, n_tgt - 1 + n_mix * (n_cand - 1) + lead)
        pending = [row_copy(d, lead) for d in range(1, n_tgt)]
        for copy in pending:
            copy.start()
        for core in range(lead):
            late_loads[core].wait()
            cand_ready(core * early)
            row_part[core] = functools.reduce(
                jnp.add, [tile(index, core * early) for index in range(tgt_parts)]
            )
        k_one[...] = k_one_t[...].T

        def x_sum(slots):
            total = slots[lax.rem(xi + n_tgt, n_tgt)]
            for k in range(1, n_tgt):
                total = total + slots[lax.rem(xi - k + n_tgt, n_tgt)]
            return total

        def z_sum(slots):
            total = slots[lax.rem(zi + n_cand, n_cand)]
            for k in range(1, n_cand):
                total = total + slots[lax.rem(zi - k + n_cand, n_cand)]
            return total

        def x_copy(slots, lane, turn, d):
            return pltpu.make_async_remote_copy(
                src_ref=slots.at[0], dst_ref=slots.at[d],
                send_sem=x_send[lane], recv_sem=x_recv.at[turn % 2, lane, d - 1],
                device_id=x_peer(d), device_id_type=MESH,
            )

        def x_start(slots, lane, turn):
            for d in range(1, n_tgt):
                x_copy(slots, lane, turn, d).start()

        def x_arrive(slots, lane, turn):
            for d in range(1, n_tgt):
                x_copy(slots, lane, turn, d).wait_recv()

        def x_sent(slots, lane):
            together(slots.at[pl.ds(0, n_tgt - 1)], (x_send[lane], rs_in.at[0, 0])).wait_send()

        place = lax.broadcasted_iota(jnp.int32, (16, early), 0)
        part_sum = None
        for core in reversed(range(n_mix)):
            value = row_part[core]
            for d in range(1, n_tgt):
                row_copy(d, core).wait_recv()
                value = value + row_slots[d, core]
            scale_row = 1.0 / value
            head = scale_row.astype(BF16).astype(F32)
            lhs = jnp.where(place == 0, head, jnp.where(place == 1, scale_row - head, 0.0))
            value = lax.dot_general(
                lhs.astype(BF16), k_one[core * early:(core + 1) * early, :], NN_DIMS,
                preferred_element_type=F32,
            )
            part_sum = value if part_sum is None else part_sum + value
        col_slots[0] = part_sum[:1] + part_sum[1:2]
        for d in range(1, n_cand):
            pltpu.make_async_remote_copy(
                src_ref=col_slots.at[0], dst_ref=col_slots.at[d],
                send_sem=z_sems.at[0], recv_sem=z_sems.at[1],
                device_id=z_peer(d), device_id_type=MESH,
            ).start()
        z_all = together(col_slots.at[pl.ds(1, n_cand - 1)], (z_sems.at[0], z_sems.at[1]))

        for at in range(0, cols, 64):
            power = raised_t[pl.ds(at, 64), :]
            k_two_t[pl.ds(at, 64), :] = (power * power * (1.0 / tgt_total)).astype(BF16)
        k_two[...] = k_two_t[...].T
        for core in range(lead):
            weight_copy(core).wait_recv()
        all_weights = jnp.concatenate(
            [weights[core, :, :mixes] for core in range(lead)] + [weight_ref[...]], axis=1
        )
        all_hot = member_ref[...] == lax.broadcasted_iota(jnp.int32, (tasks, tgt_total), 0)
        counts = jnp.sum(all_hot.astype(F32), axis=1, keepdims=True)
        totals = jnp.sum(all_weights * counts, axis=0, keepdims=True)
        scaled = all_weights * (float(cand_total) / totals)
        own = pl.ds(pl.multiple_of(xi * cols, cols), cols)
        own_hot = (
            member_ref[:, own] == lax.broadcasted_iota(jnp.int32, (tasks, cols), 0)
        ).astype(F32)
        mass[...] = lax.dot_general(
            scaled, own_hot, TN_DIMS, precision=lax.Precision.HIGHEST, preferred_element_type=F32
        )
        z_all.wait_recv()
        col_sum = z_sum(col_slots)

        task_sums = lax.dot_general(
            (own_hot / col_sum).astype(BF16), k_one_t[...], NN_DIMS, preferred_element_type=F32
        )
        for h in range(subs):
            task_slots[h, 0] = task_sums[:, h * strip:(h + 1) * strip]
            x_start(task_slots.at[h], h, 1)
        for h in range(subs):
            x_arrive(task_slots.at[h], h, 1)
            task_all[:, pl.ds(h * strip, strip)] = x_sum(task_slots.at[h])
        for h in range(subs):
            x_sent(task_slots.at[h], h)

        near = zi // owners[1]
        far = 1 - near

        def tgt_send(kernel, turn, part, owner):
            lhs = (1.0 / cand_sums[of(part), :]).astype(BF16)
            if turn > 0:
                sent_all(turn - 1, part, owner).wait_send()
            for o in (far, near):
                value = lax.dot_general(
                    lhs, kernel[:, half(o)], NN_DIMS, preferred_element_type=F32
                )
                for s in range(subs):
                    rs_send[turn, part, o, s] = value[:, s * piece:(s + 1) * piece]
                    if o is far or not owner:
                        to_owner(turn, part, o, s).start()

        def tgt_finish(turn, part, core, change):
            if turn > 0:
                taken_all(turn - 1, part, lead).wait_send()
            for s in range(subs):
                owned_all(turn, part, s).wait_recv()
                total = rs_send[turn, part, near, s]
                for d in range(n_cand - 1):
                    total = total + rs_slots[turn, part, s, d]
                ag_slots[turn, part, near, s] = change(mass[of(part), span(near, s)] / total)
                for d in takers(core):
                    peer = lax.rem(zi + d, n_cand)
                    from_owner(turn, part, near, s, peer, core).start()

        def gathered(turn, part, o, s):
            from_owner(turn, part, o, s, owners[0] + o, lead).wait_recv()

        def cand_send(turn, part, owner):
            total = None
            for o in (near, far):
                for s in range(subs):
                    if o is far or not owner:
                        gathered(turn, part, o, s)
                    value = lax.dot_general(
                        ag_slots[turn, part, o, s].astype(BF16), k_two_t[span(o, s), :],
                        NN_DIMS, preferred_element_type=F32,
                    )
                    total = value if total is None else total + value
            if turn > 0:
                x_sent(cand_slots.at[turn - 1, part], part)
            cand_slots[turn, part, 0] = total
            x_start(cand_slots.at[turn, part], part, turn)

        def cand_finish(turn, part):
            x_arrive(cand_slots.at[turn, part], part, turn)
            cand_sums[of(part), :] = x_sum(cand_slots.at[turn, part])

        def keep(scale):
            return scale

        changes = (jnp.square,) + (keep,) * (ITERS - 1)

        def over(group_of_parts, step):
            def body(part, carry):
                step(part)
                return carry

            lax.fori_loop(group_of_parts[0], group_of_parts[-1] + 1, body, 0)

        def iterate(owner):
            for part in each:
                cand_sums[of(part), :] = lax.dot_general(
                    scaled[:, part * group:(part + 1) * group], task_all[...], TN_DIMS,
                    precision=lax.Precision.HIGHEST, preferred_element_type=F32,
                )
                tgt_send(k_one, 0, part, owner)
            for turn in range(ITERS):
                if owner:
                    over(each, lambda part: tgt_finish(turn, part, lead, changes[turn]))
                over(each, lambda part: cand_send(turn, part, owner))

                def across(part):
                    cand_finish(turn, part)
                    tgt_send(k_two, 1 + turn, part, owner)

                over(each, across)
            for core in range(lead):
                cand_copy(core).start()
            out_cand[...] = -jnp.log(cand_sums[pl.ds(lead * mixes, mixes), :])
            if owner:
                for core in range(n_mix):
                    over(parts_of(core), lambda part: tgt_finish(ITERS, part, core, jnp.log))
            for part in parts_of(lead):
                for o in (near, far):
                    for s in range(subs):
                        if o is far or not owner:
                            gathered(ITERS, part, o, s)
                        out_tgt[row_of(part), span(o, s)] = ag_slots[ITERS, part, o, s]
            for part in each:
                sent_all(ITERS, part, owner).wait_send()
                if owner:
                    taken_all(ITERS, part, core_of(ITERS, part)).wait_send()
                x_sent(cand_slots.at[ITERS - 1, part], part)

        owning = (zi == owners[0]) | (zi == owners[1])

        @pl.when(owning)
        def _():
            iterate(True)

        @pl.when(jnp.logical_not(owning))
        def _():
            iterate(False)

        for core in range(lead):
            cand_copy(core).wait_send()
        z_all.wait_send()
        for copy in pending:
            copy.wait_send()


def write_kernel(cand_log, tgt_log, out_cand, out_tgt, sems):
    copies = [
        pltpu.make_async_copy(cand_log, out_cand, sems.at[0]),
        pltpu.make_async_copy(tgt_log, out_tgt, sems.at[1]),
    ]
    for copy in copies:
        copy.start()
    for copy in copies:
        copy.wait()


def fused(candidates, targets, member, mix_weight):
    n_tgt, n_cand, n_mix = lax.axis_size("tgt"), lax.axis_size("cand"), lax.axis_size("mix")
    rows, width = candidates.shape
    cols = targets.shape[0]
    mixes, tasks = mix_weight.shape
    piece, strip = cols // 4, rows // 2
    parts = 2 * n_mix if mixes % 16 == 0 else n_mix
    loads = cols // 256 + rows // n_mix // 256 + n_mix + 1
    group = mixes * n_mix // parts
    logs = pl.pallas_call(
        functools.partial(fused_kernel, n_tgt, n_cand, n_mix, parts),
        out_shape=(pltpu.VMEM((mixes, rows), F32), pltpu.VMEM((mixes, cols), F32)),
        in_specs=[pl.BlockSpec(memory_space=pltpu.HBM)] * 4,
        out_specs=(pl.BlockSpec(memory_space=pltpu.VMEM),) * 2,
        scratch_shapes=[
            pltpu.VMEM((rows, width), BF16),
            pltpu.VMEM((cols, width), BF16),
            pltpu.VMEM((rows, width), BF16),
            pltpu.VMEM((cols, width), BF16),
            pltpu.VMEM((cols, rows), F32),
            pltpu.VMEM((cols, rows), BF16),
            pltpu.VMEM((rows, cols), BF16),
            pltpu.VMEM((cols, rows), BF16),
            pltpu.VMEM((rows, cols), BF16),
            pltpu.VMEM((mixes * n_mix, cols), F32),
            pltpu.VMEM((mixes * n_mix, rows), F32),
            pltpu.VMEM((tasks, rows), F32),
            pltpu.VMEM((1, cols * n_tgt), jnp.int32),
            pltpu.VMEM((tasks, mixes), F32),
            pltpu.VMEM((n_mix, tasks, 128), F32),
            pltpu.VMEM((mixes, rows), F32),
            pltpu.VMEM((n_mix, 1, rows // n_mix), F32),
            pltpu.VMEM((n_tgt, n_mix, 1, rows // n_mix), F32),
            pltpu.VMEM((n_cand, 1, cols), F32),
            pltpu.VMEM((2, n_tgt, tasks, strip), F32),
            pltpu.VMEM((ITERS, parts, n_tgt, group, rows), F32),
            pltpu.VMEM((1 + ITERS, parts, 2, 2, group, piece), F32),
            pltpu.VMEM((1 + ITERS, parts, 2, n_cand, group, piece), F32),
            pltpu.VMEM((1 + ITERS, parts, 2, 2, group, piece), F32),
            pltpu.SemaphoreType.DMA((max(loads, 3 * parts),)),
            pltpu.SemaphoreType.DMA((2, parts, n_tgt - 1)),
            pltpu.SemaphoreType.DMA((2,)),
            pltpu.SemaphoreType.DMA((n_tgt - 1,)),
            pltpu.SemaphoreType.DMA((n_tgt - 1, n_mix)),
            pltpu.SemaphoreType.DMA((parts, 2)),
            pltpu.SemaphoreType.DMA((parts, 2, 2)),
            pltpu.SemaphoreType.DMA((2, n_mix - 1)),
            pltpu.SemaphoreType.DMA((2, n_mix - 1)),
        ],
        compiler_params=pltpu.CompilerParams(
            collective_id=0, has_side_effects=True, vmem_limit_bytes=56 * 1024 * 1024
        ),
    )(candidates, targets, member.reshape(1, -1), mix_weight.T)
    return tuple(pl.pallas_call(
        write_kernel,
        out_shape=(
            jax.ShapeDtypeStruct((mixes, rows), F32),
            jax.ShapeDtypeStruct((mixes, cols), F32),
        ),
        in_specs=[pl.BlockSpec(memory_space=pltpu.VMEM)] * 2,
        out_specs=(pl.BlockSpec(memory_space=pltpu.HBM),) * 2,
        scratch_shapes=[pltpu.SemaphoreType.DMA((2,))],
    )(*(pltpu.with_memory_space_constraint(log, pltpu.VMEM) for log in logs)))


def target_mass(own_member, member, mix_weight, cand_total):
    task_ids = jnp.arange(mix_weight.shape[1], dtype=jnp.int32)
    counts = jnp.sum((member[None, :] == task_ids[:, None]).astype(jnp.float32), axis=1)
    weight_total = jnp.dot(mix_weight, counts, precision=lax.Precision.HIGHEST)
    onehot = (own_member[None, :] == task_ids[:, None]).astype(jnp.float32)
    per_target = jnp.dot(mix_weight, onehot, precision=lax.Precision.HIGHEST)
    return per_target * (cand_total / weight_total)[:, None]


def by_collectives(candidates, targets, member, mix_weight):
    cand_rows = candidates.shape[0]
    tgt_rows = targets.shape[0]
    tgt_total = tgt_rows * lax.axis_size("tgt")
    cand_total = cand_rows * lax.axis_size("cand")
    tgt_unit = unit_rows(targets)
    scores = contract_last(unit_rows(candidates), tgt_unit)
    own_member = lax.dynamic_slice_in_dim(member, lax.axis_index("tgt") * tgt_rows, tgt_rows, 0)
    mass = target_mass(own_member, member, mix_weight, float(cand_total))
    kernel_one = jnp.exp(scores / EPS_FIRST) / tgt_total
    kernel_two = jnp.exp(scores / EPS_SECOND) / tgt_total
    scale_tgt = jnp.ones((mix_weight.shape[0], tgt_rows), jnp.float32)
    scale_cand = jnp.ones((mix_weight.shape[0], cand_rows), jnp.float32)
    for section_index, kernel in enumerate((kernel_one, kernel_two)):
        if section_index == 1:
            scale_tgt = scale_tgt * scale_tgt
        for repeat in range(ITERS):
            partial_value = lax.dot_general(
                scale_tgt, kernel, (((1,), (1,)), ((), ())), precision=lax.Precision.HIGHEST
            )
            scale_cand = 1.0 / lax.psum(partial_value, "tgt")
            column_part = jnp.dot(scale_cand, kernel, precision=lax.Precision.HIGHEST)
            share_cols = tgt_rows // lax.axis_size("cand")
            summed = lax.psum_scatter(column_part, "cand", scatter_dimension=1, tiled=True)
            own_mass = lax.dynamic_slice_in_dim(
                mass, lax.axis_index("cand") * share_cols, share_cols, 1
            )
            scale_tgt = lax.all_gather(own_mass / summed, "cand", axis=1, tiled=True)
    return (jnp.log(scale_cand), jnp.log(scale_tgt))


def solution(mesh):
    in_specs = (
        P(("groups", "cand"), None),
        P(("groups", "tgt"), None),
        P("groups"),
        P("mix", "groups"),
    )
    out_specs = (P("mix", ("groups", "cand")), P("mix", ("groups", "tgt")))
    n_tgt, n_cand, n_mix = mesh.shape["tgt"], mesh.shape["cand"], mesh.shape["mix"]

    def local(candidates, targets, member, mix_weight):
        lanes = targets.shape[0] % (128 * n_cand) == 0 and candidates.shape[0] % 512 == 0
        paired = n_cand % 2 == 0 and n_tgt > 1 and n_mix == 2
        step = fused if lanes and paired else by_collectives
        return step(candidates, targets, member, mix_weight)

    return jax.shard_map(local, mesh=mesh, in_specs=in_specs, out_specs=out_specs, check_vma=False)
```

```python
import functools
import math

import jax
import jax.numpy as jnp
from jax import lax
from jax.experimental import pallas as pl
from jax.experimental.pallas import tpu as pltpu
from jax.sharding import PartitionSpec as P

ITERS = 2


EPS_FIRST = 0.05
EPS_SECOND = 0.025

MESH = pl.DeviceIdType.MESH
F32 = jnp.float32
BF16 = jnp.bfloat16
NT_DIMS = (((1,), (1,)), ((), ()))
TN_DIMS = (((0,), (0,)), ((), ()))
NN_DIMS = (((1,), (0,)), ((), ()))


def unit_rows(embedding):
    values = embedding.astype(jnp.float32)
    mean_sq = jnp.mean(values * values, axis=1, keepdims=True)
    return (values * (lax.rsqrt(mean_sq + 1e-06) * (1.0 / math.sqrt(values.shape[1])))).astype(
        jnp.bfloat16
    )


def contract_last(left, right):
    return lax.dot_general(left, right, NT_DIMS, preferred_element_type=jnp.float32)


def fused_kernel(
    n_tgt, n_cand, n_mix, parts, cand_hbm, tgt_hbm, member_hbm, weight_hbm, out_cand, out_tgt,
    cand_rows, tgt_rows, cand_unit, tgt_unit, raised_t, k_one_t, k_one, k_two_t, k_two,
    mass, cand_sums, task_all, member_ref, weight_ref, weights, cand_in,
    row_part, row_slots, col_slots, task_slots, cand_slots, rs_send, rs_slots, ag_slots,
    load_sems, x_recv, z_sems, row_out, row_in, rs_in, ag_in,
    chip_out, chip_in,
):
    xi, zi, ci = lax.axis_index("tgt"), lax.axis_index("cand"), lax.axis_index("mix")
    rows, width = cand_hbm.shape
    cols = tgt_hbm.shape[0]
    tasks, mixes = weight_hbm.shape
    lead = n_mix - 1
    owners = (n_cand // 2 - 1, n_cand // 2)

    class Sems:
        def __init__(self, first):
            self.first = first

        def __getitem__(self, part):
            return load_sems.at[self.first + part]

    x_send, rs_out, ag_out = (Sems(k * parts) for k in range(3))
    share = cols // len(owners)
    subs = 2
    piece, strip = share // subs, rows // subs
    group = mixes * n_mix // parts
    tgt_total, cand_total = cols * n_tgt, rows * n_cand
    block = 256
    early = rows // n_mix

    def load(src, dst, sem, *at):
        if at:
            src, dst = src.at[pl.ds(*at)], dst.at[pl.ds(*at)]
        return pltpu.make_async_copy(src, dst, load_sems.at[sem])

    tgt_parts, cand_parts = cols // block, early // block
    tgt_loads = [load(tgt_hbm, tgt_rows, k, k * block, block) for k in range(tgt_parts)]
    cand_loads = [
        load(cand_hbm, cand_rows, tgt_parts + k,
             pl.multiple_of(ci * early + k * block, block), block)
        for k in range(cand_parts)
    ]
    late_loads = [
        load(cand_hbm, cand_rows, tgt_parts + cand_parts + core, core * early, early)
        for core in range(lead)
    ]
    small_loads = [
        load(src, dst, tgt_parts + cand_parts + lead + k)
        for k, (src, dst) in enumerate(((member_hbm, member_ref), (weight_hbm, weight_ref)))
    ]
    for copy in cand_loads + tgt_loads + small_loads:
        copy.start()

    def x_peer(d):
        return {"tgt": lax.rem(xi + d, n_tgt), "mix": lead}

    def z_peer(d):
        return {"cand": lax.rem(zi + d, n_cand), "mix": lead}

    barrier = pltpu.get_barrier_semaphore()

    def hello(**peer):
        pl.semaphore_signal(barrier, inc=1, device_id=peer, device_id_type=MESH)

    for d in range(1, n_cand):
        hello(**z_peer(d))

    @pl.when(ci == lead)
    def _():
        for core in range(lead):
            late_loads[core].start()
            hello(mix=core)
        for d in range(1, n_tgt):
            for core in range(n_mix):
                hello(tgt=lax.rem(xi + d, n_tgt), mix=core)

    @pl.when(ci != lead)
    def _():
        hello(mix=lead)

    def cand_ready(first):
        for at in range(0, early, block):
            at = pl.ds(pl.multiple_of(first + at, block), block)
            cand_unit[at, :] = unit_rows(cand_rows[at, :])

    def tgt_ready(index):
        tgt_loads[index].wait()
        at = pl.ds(index * block, block)
        tgt_unit[at, :] = unit_rows(tgt_rows[at, :])

    def tile(index, first, keep=True):
        at = pl.ds(index * block if isinstance(index, int) else pl.multiple_of(index * block, block), block)
        across = pl.ds(pl.multiple_of(first, early), early)
        power = jnp.exp(contract_last(tgt_unit[at, :], cand_unit[across, :]) * (1.0 / EPS_FIRST))
        if keep:
            raised_t[at, across] = power
            k_one_t[at, across] = (power * (1.0 / tgt_total)).astype(BF16)
        return jnp.sum(power, axis=0, keepdims=True) * (1.0 / tgt_total)

    for copy in cand_loads:
        copy.wait()
    cand_ready(ci * early)
    tgt_ready(0)

    def first_half(keep):
        sums = []
        for index in range(1, tgt_parts):
            tgt_ready(index)
            sums.append(tile(index - 1, ci * early, keep))
        sums.append(tile(tgt_parts - 1, ci * early, keep))
        row_part[ci] = functools.reduce(jnp.add, sums)

    @pl.when(ci == lead)
    def _():
        first_half(True)

    @pl.when(ci != lead)
    def _():
        first_half(False)

    for copy in small_loads:
        copy.wait()

    def row_copy(d, core):
        return pltpu.make_async_remote_copy(
            src_ref=row_part.at[core], dst_ref=row_slots.at[d, core],
            send_sem=row_out.at[d - 1], recv_sem=row_in.at[d - 1, core],
            device_id=x_peer(d), device_id_type=MESH,
        )

    def weight_copy(core):
        return pltpu.make_async_remote_copy(
            src_ref=weights.at[core], dst_ref=weights.at[core],
            send_sem=chip_out.at[0, core], recv_sem=chip_in.at[0, core],
            device_id={"mix": lead}, device_id_type=MESH,
        )

    def cand_copy(core):
        return pltpu.make_async_remote_copy(
            src_ref=cand_sums.at[pl.ds(core * mixes, mixes)], dst_ref=cand_in,
            send_sem=chip_out.at[1, core], recv_sem=chip_in.at[1, core],
            device_id={"mix": core}, device_id_type=MESH,
        )

    def of(part):
        at = part * group
        return pl.ds(at if isinstance(at, int) else pl.multiple_of(at, group), group)

    def half(o):
        return pl.ds(o * share if isinstance(o, int) else pl.multiple_of(o * share, share), share)

    def span(o, s):
        at = o * share + s * piece
        return pl.ds(at if isinstance(at, int) else pl.multiple_of(at, piece), piece)

    def to_owner(turn, part, o, s):
        owner = owners[0] + o
        return pltpu.make_async_remote_copy(
            src_ref=rs_send.at[turn, part, o, s],
            dst_ref=rs_slots.at[turn, part, s, lax.rem(zi - owner + n_cand, n_cand) - 1],
            send_sem=rs_out[part], recv_sem=rs_in.at[part, s],
            device_id={"cand": owner, "mix": lead}, device_id_type=MESH,
        )

    def together(slots, sems):
        return pltpu.make_async_remote_copy(
            src_ref=slots, dst_ref=slots, send_sem=sems[0], recv_sem=sems[1],
            device_id={"tgt": lax.rem(xi + 1, n_tgt), "mix": lead}, device_id_type=MESH,
        )

    def owned_all(turn, part, s):
        return together(
            rs_slots.at[turn, part, s, pl.ds(0, n_cand - 1)], (rs_out[part], rs_in.at[part, s])
        )

    def sent_all(turn, part, owner):
        slots = rs_send.at[turn, part, 0] if owner else rs_send.at[turn, part]
        return together(slots, (rs_out[part], rs_in.at[part, 0]))

    def taken_all(turn, part, core):
        return together(
            rs_slots.at[turn, part, :, pl.ds(0, len(takers(core)))],
            (ag_out[part], rs_in.at[part, 0]),
        )

    def from_owner(turn, part, o, s, peer, core):
        return pltpu.make_async_remote_copy(
            src_ref=ag_slots.at[turn, part, o, s], dst_ref=ag_slots.at[turn, part, o, s],
            send_sem=ag_out[part], recv_sem=ag_in.at[part, o, s],
            device_id={"cand": peer, "mix": core}, device_id_type=MESH,
        )

    def core_of(turn, part):
        return part * n_mix // parts if turn == ITERS else lead

    def takers(core):
        away = core != lead
        order = sorted(range(1, n_cand), key=lambda d: abs(n_cand // 2 - d))
        return order + [0] * away

    def parts_of(core):
        return [part for part in range(parts) if core_of(ITERS, part) == core]

    def row_of(part):
        return pl.ds(part * group % mixes, group)

    halves = range(len(owners))
    each = range(parts)

    @pl.when(ci != lead)
    def _():
        weights[ci] = jnp.zeros(weights.shape[1:], F32)
        weights[ci, :, pl.ds(0, mixes)] = weight_ref[...]
        pl.semaphore_wait(barrier, n_tgt)
        sent = [row_copy(d, ci) for d in range(1, n_tgt)] + [weight_copy(ci)]
        for copy in sent:
            copy.start()
        cand_copy(ci).wait_recv()
        out_cand[...] = -jnp.log(cand_in[...])
        for core in range(lead):

            @pl.when(ci == core)
            def _():
                for part in parts_of(core):
                    for o in halves:
                        for s in range(subs):
                            from_owner(ITERS, part, o, s, owners[o], lead).wait_recv()
                            out_tgt[row_of(part), span(o, s)] = ag_slots[ITERS, part, o, s]
        for copy in sent:
            copy.wait_send()

    @pl.when(ci == lead)
    def _():
        pl.semaphore_wait(barrier, n_tgt - 1 + n_mix * (n_cand - 1) + lead)
        pending = [row_copy(d, lead) for d in range(1, n_tgt)]
        for copy in pending:
            copy.start()
        for core in range(lead):
            late_loads[core].wait()
            cand_ready(core * early)
            row_part[core] = functools.reduce(
                jnp.add, [tile(index, core * early) for index in range(tgt_parts)]
            )
        k_one[...] = k_one_t[...].T

        def x_sum(slots):
            total = slots[lax.rem(xi + n_tgt, n_tgt)]
            for k in range(1, n_tgt):
                total = total + slots[lax.rem(xi - k + n_tgt, n_tgt)]
            return total

        def z_sum(slots):
            total = slots[lax.rem(zi + n_cand, n_cand)]
            for k in range(1, n_cand):
                total = total + slots[lax.rem(zi - k + n_cand, n_cand)]
            return total

        def x_copy(slots, lane, turn, d):
            return pltpu.make_async_remote_copy(
                src_ref=slots.at[0], dst_ref=slots.at[d],
                send_sem=x_send[lane], recv_sem=x_recv.at[turn % 2, lane, d - 1],
                device_id=x_peer(d), device_id_type=MESH,
            )

        def x_start(slots, lane, turn):
            for d in range(1, n_tgt):
                x_copy(slots, lane, turn, d).start()

        def x_arrive(slots, lane, turn):
            for d in range(1, n_tgt):
                x_copy(slots, lane, turn, d).wait_recv()

        def x_sent(slots, lane):
            together(slots.at[pl.ds(0, n_tgt - 1)], (x_send[lane], rs_in.at[0, 0])).wait_send()

        place = lax.broadcasted_iota(jnp.int32, (16, early), 0)
        part_sum = None
        for core in reversed(range(n_mix)):
            value = row_part[core]
            for d in range(1, n_tgt):
                row_copy(d, core).wait_recv()
                value = value + row_slots[d, core]
            scale_row = 1.0 / value
            head = scale_row.astype(BF16).astype(F32)
            lhs = jnp.where(place == 0, head, jnp.where(place == 1, scale_row - head, 0.0))
            value = lax.dot_general(
                lhs.astype(BF16), k_one[core * early:(core + 1) * early, :], NN_DIMS,
                preferred_element_type=F32,
            )
            part_sum = value if part_sum is None else part_sum + value
        col_slots[0] = part_sum[:1] + part_sum[1:2]
        for d in range(1, n_cand):
            pltpu.make_async_remote_copy(
                src_ref=col_slots.at[0], dst_ref=col_slots.at[d],
                send_sem=z_sems.at[0], recv_sem=z_sems.at[1],
                device_id=z_peer(d), device_id_type=MESH,
            ).start()
        z_all = together(col_slots.at[pl.ds(1, n_cand - 1)], (z_sems.at[0], z_sems.at[1]))

        for at in range(0, cols, 64):
            power = raised_t[pl.ds(at, 64), :]
            k_two_t[pl.ds(at, 64), :] = (power * power * (1.0 / tgt_total)).astype(BF16)
        k_two[...] = k_two_t[...].T
        for core in range(lead):
            weight_copy(core).wait_recv()
        all_weights = jnp.concatenate(
            [weights[core, :, :mixes] for core in range(lead)] + [weight_ref[...]], axis=1
        )
        all_hot = member_ref[...] == lax.broadcasted_iota(jnp.int32, (tasks, tgt_total), 0)
        counts = jnp.sum(all_hot.astype(F32), axis=1, keepdims=True)
        totals = jnp.sum(all_weights * counts, axis=0, keepdims=True)
        scaled = all_weights * (float(cand_total) / totals)
        own = pl.ds(pl.multiple_of(xi * cols, cols), cols)
        own_hot = (
            member_ref[:, own] == lax.broadcasted_iota(jnp.int32, (tasks, cols), 0)
        ).astype(F32)
        mass[...] = lax.dot_general(
            scaled, own_hot, TN_DIMS, precision=lax.Precision.HIGHEST, preferred_element_type=F32
        )
        z_all.wait_recv()
        col_sum = z_sum(col_slots)

        task_sums = lax.dot_general(
            (own_hot / col_sum).astype(BF16), k_one_t[...], NN_DIMS, preferred_element_type=F32
        )
        for h in range(subs):
            task_slots[h, 0] = task_sums[:, h * strip:(h + 1) * strip]
            x_start(task_slots.at[h], h, 1)
        for h in range(subs):
            x_arrive(task_slots.at[h], h, 1)
            task_all[:, pl.ds(h * strip, strip)] = x_sum(task_slots.at[h])
        for h in range(subs):
            x_sent(task_slots.at[h], h)

        near = zi // owners[1]
        far = 1 - near

        def tgt_send(kernel, turn, part, owner):
            lhs = (1.0 / cand_sums[of(part), :]).astype(BF16)
            if turn > 0:
                sent_all(turn - 1, part, owner).wait_send()
            for o in (far, near):
                value = lax.dot_general(
                    lhs, kernel[:, half(o)], NN_DIMS, preferred_element_type=F32
                )
                for s in range(subs):
                    rs_send[turn, part, o, s] = value[:, s * piece:(s + 1) * piece]
                    if o is far or not owner:
                        to_owner(turn, part, o, s).start()

        def tgt_finish(turn, part, core, change):
            if turn > 0:
                taken_all(turn - 1, part, lead).wait_send()
            for s in range(subs):
                owned_all(turn, part, s).wait_recv()
                total = rs_send[turn, part, near, s]
                for d in range(n_cand - 1):
                    total = total + rs_slots[turn, part, s, d]
                ag_slots[turn, part, near, s] = change(mass[of(part), span(near, s)] / total)
                for d in takers(core):
                    peer = lax.rem(zi + d, n_cand)
                    from_owner(turn, part, near, s, peer, core).start()

        def gathered(turn, part, o, s):
            from_owner(turn, part, o, s, owners[0] + o, lead).wait_recv()

        def cand_send(turn, part, owner):
            total = None
            for o in (near, far):
                for s in range(subs):
                    if o is far or not owner:
                        gathered(turn, part, o, s)
                    value = lax.dot_general(
                        ag_slots[turn, part, o, s].astype(BF16), k_two_t[span(o, s), :],
                        NN_DIMS, preferred_element_type=F32,
                    )
                    total = value if total is None else total + value
            if turn > 0:
                x_sent(cand_slots.at[turn - 1, part], part)
            cand_slots[turn, part, 0] = total
            x_start(cand_slots.at[turn, part], part, turn)

        def cand_finish(turn, part):
            x_arrive(cand_slots.at[turn, part], part, turn)
            cand_sums[of(part), :] = x_sum(cand_slots.at[turn, part])

        def keep(scale):
            return scale

        changes = (jnp.square,) + (keep,) * (ITERS - 1)

        def over(group_of_parts, step):
            def body(part, carry):
                step(part)
                return carry

            lax.fori_loop(group_of_parts[0], group_of_parts[-1] + 1, body, 0)

        def iterate(owner):
            for part in each:
                cand_sums[of(part), :] = lax.dot_general(
                    scaled[:, part * group:(part + 1) * group], task_all[...], TN_DIMS,
                    precision=lax.Precision.HIGHEST, preferred_element_type=F32,
                )
                tgt_send(k_one, 0, part, owner)
            for turn in range(ITERS):
                if owner:
                    over(each, lambda part: tgt_finish(turn, part, lead, changes[turn]))
                over(each, lambda part: cand_send(turn, part, owner))

                def across(part):
                    cand_finish(turn, part)
                    tgt_send(k_two, 1 + turn, part, owner)

                over(each, across)
            for core in range(lead):
                cand_copy(core).start()
            out_cand[...] = -jnp.log(cand_sums[pl.ds(lead * mixes, mixes), :])
            if owner:
                for core in range(n_mix):
                    over(parts_of(core), lambda part: tgt_finish(ITERS, part, core, jnp.log))
            for part in parts_of(lead):
                for o in (near, far):
                    for s in range(subs):
                        if o is far or not owner:
                            gathered(ITERS, part, o, s)
                        out_tgt[row_of(part), span(o, s)] = ag_slots[ITERS, part, o, s]
            for part in each:
                sent_all(ITERS, part, owner).wait_send()
                if owner:
                    taken_all(ITERS, part, core_of(ITERS, part)).wait_send()
                x_sent(cand_slots.at[ITERS - 1, part], part)

        owning = (zi == owners[0]) | (zi == owners[1])

        @pl.when(owning)
        def _():
            iterate(True)

        @pl.when(jnp.logical_not(owning))
        def _():
            iterate(False)

        for core in range(lead):
            cand_copy(core).wait_send()
        z_all.wait_send()
        for copy in pending:
            copy.wait_send()


def write_kernel(cand_log, tgt_log, out_cand, out_tgt, sems):
    copies = [
        pltpu.make_async_copy(cand_log, out_cand, sems.at[0]),
        pltpu.make_async_copy(tgt_log, out_tgt, sems.at[1]),
    ]
    for copy in copies:
        copy.start()
    for copy in copies:
        copy.wait()


def fused(candidates, targets, member, mix_weight):
    n_tgt, n_cand, n_mix = lax.axis_size("tgt"), lax.axis_size("cand"), lax.axis_size("mix")
    rows, width = candidates.shape
    cols = targets.shape[0]
    mixes, tasks = mix_weight.shape
    piece, strip = cols // 4, rows // 2
    parts = 2 * n_mix if mixes % 16 == 0 else n_mix
    loads = cols // 256 + rows // n_mix // 256 + n_mix + 1
    group = mixes * n_mix // parts
    logs = pl.pallas_call(
        functools.partial(fused_kernel, n_tgt, n_cand, n_mix, parts),
        out_shape=(pltpu.VMEM((mixes, rows), F32), pltpu.VMEM((mixes, cols), F32)),
        in_specs=[pl.BlockSpec(memory_space=pltpu.HBM)] * 4,
        out_specs=(pl.BlockSpec(memory_space=pltpu.VMEM),) * 2,
        scratch_shapes=[
            pltpu.VMEM((rows, width), BF16),
            pltpu.VMEM((cols, width), BF16),
            pltpu.VMEM((rows, width), BF16),
            pltpu.VMEM((cols, width), BF16),
            pltpu.VMEM((cols, rows), F32),
            pltpu.VMEM((cols, rows), BF16),
            pltpu.VMEM((rows, cols), BF16),
            pltpu.VMEM((cols, rows), BF16),
            pltpu.VMEM((rows, cols), BF16),
            pltpu.VMEM((mixes * n_mix, cols), F32),
            pltpu.VMEM((mixes * n_mix, rows), F32),
            pltpu.VMEM((tasks, rows), F32),
            pltpu.VMEM((1, cols * n_tgt), jnp.int32),
            pltpu.VMEM((tasks, mixes), F32),
            pltpu.VMEM((n_mix, tasks, 128), F32),
            pltpu.VMEM((mixes, rows), F32),
            pltpu.VMEM((n_mix, 1, rows // n_mix), F32),
            pltpu.VMEM((n_tgt, n_mix, 1, rows // n_mix), F32),
            pltpu.VMEM((n_cand, 1, cols), F32),
            pltpu.VMEM((2, n_tgt, tasks, strip), F32),
            pltpu.VMEM((ITERS, parts, n_tgt, group, rows), F32),
            pltpu.VMEM((1 + ITERS, parts, 2, 2, group, piece), F32),
            pltpu.VMEM((1 + ITERS, parts, 2, n_cand, group, piece), F32),
            pltpu.VMEM((1 + ITERS, parts, 2, 2, group, piece), F32),
            pltpu.SemaphoreType.DMA((max(loads, 3 * parts),)),
            pltpu.SemaphoreType.DMA((2, parts, n_tgt - 1)),
            pltpu.SemaphoreType.DMA((2,)),
            pltpu.SemaphoreType.DMA((n_tgt - 1,)),
            pltpu.SemaphoreType.DMA((n_tgt - 1, n_mix)),
            pltpu.SemaphoreType.DMA((parts, 2)),
            pltpu.SemaphoreType.DMA((parts, 2, 2)),
            pltpu.SemaphoreType.DMA((2, n_mix - 1)),
            pltpu.SemaphoreType.DMA((2, n_mix - 1)),
        ],
        compiler_params=pltpu.CompilerParams(
            collective_id=0, has_side_effects=True, vmem_limit_bytes=56 * 1024 * 1024
        ),
    )(candidates, targets, member.reshape(1, -1), mix_weight.T)
    return tuple(pl.pallas_call(
        write_kernel,
        out_shape=(
            jax.ShapeDtypeStruct((mixes, rows), F32),
            jax.ShapeDtypeStruct((mixes, cols), F32),
        ),
        in_specs=[pl.BlockSpec(memory_space=pltpu.VMEM)] * 2,
        out_specs=(pl.BlockSpec(memory_space=pltpu.HBM),) * 2,
        scratch_shapes=[pltpu.SemaphoreType.DMA((2,))],
    )(*(pltpu.with_memory_space_constraint(log, pltpu.VMEM) for log in logs)))


def target_mass(own_member, member, mix_weight, cand_total):
    task_ids = jnp.arange(mix_weight.shape[1], dtype=jnp.int32)
    counts = jnp.sum((member[None, :] == task_ids[:, None]).astype(jnp.float32), axis=1)
    weight_total = jnp.dot(mix_weight, counts, precision=lax.Precision.HIGHEST)
    onehot = (own_member[None, :] == task_ids[:, None]).astype(jnp.float32)
    per_target = jnp.dot(mix_weight, onehot, precision=lax.Precision.HIGHEST)
    return per_target * (cand_total / weight_total)[:, None]


def by_collectives(candidates, targets, member, mix_weight):
    cand_rows = candidates.shape[0]
    tgt_rows = targets.shape[0]
    tgt_total = tgt_rows * lax.axis_size("tgt")
    cand_total = cand_rows * lax.axis_size("cand")
    tgt_unit = unit_rows(targets)
    scores = contract_last(unit_rows(candidates), tgt_unit)
    own_member = lax.dynamic_slice_in_dim(member, lax.axis_index("tgt") * tgt_rows, tgt_rows, 0)
    mass = target_mass(own_member, member, mix_weight, float(cand_total))
    kernel_one = jnp.exp(scores / EPS_FIRST) / tgt_total
    kernel_two = jnp.exp(scores / EPS_SECOND) / tgt_total
    scale_tgt = jnp.ones((mix_weight.shape[0], tgt_rows), jnp.float32)
    scale_cand = jnp.ones((mix_weight.shape[0], cand_rows), jnp.float32)
    for section_index, kernel in enumerate((kernel_one, kernel_two)):
        if section_index == 1:
            scale_tgt = scale_tgt * scale_tgt
        for repeat in range(ITERS):
            partial_value = lax.dot_general(
                scale_tgt, kernel, (((1,), (1,)), ((), ())), precision=lax.Precision.HIGHEST
            )
            scale_cand = 1.0 / lax.psum(partial_value, "tgt")
            column_part = jnp.dot(scale_cand, kernel, precision=lax.Precision.HIGHEST)
            share_cols = tgt_rows // lax.axis_size("cand")
            summed = lax.psum_scatter(column_part, "cand", scatter_dimension=1, tiled=True)
            own_mass = lax.dynamic_slice_in_dim(
                mass, lax.axis_index("cand") * share_cols, share_cols, 1
            )
            scale_tgt = lax.all_gather(own_mass / summed, "cand", axis=1, tiled=True)
    return (jnp.log(scale_cand), jnp.log(scale_tgt))


def solution(mesh):
    in_specs = (
        P(("groups", "cand"), None),
        P(("groups", "tgt"), None),
        P("groups"),
        P("mix", "groups"),
    )
    out_specs = (P("mix", ("groups", "cand")), P("mix", ("groups", "tgt")))
    n_tgt, n_cand, n_mix = mesh.shape["tgt"], mesh.shape["cand"], mesh.shape["mix"]

    def local(candidates, targets, member, mix_weight):
        lanes = targets.shape[0] % (128 * n_cand) == 0 and candidates.shape[0] % 512 == 0
        paired = n_cand % 2 == 0 and n_tgt > 1 and n_mix == 2
        step = fused if lanes and paired else by_collectives
        return step(candidates, targets, member, mix_weight)

    return jax.shard_map(local, mesh=mesh, in_specs=in_specs, out_specs=out_specs, check_vma=False)
```
